32 devices in a mesh: tile: 8 (over z, x), col: 4 (over y, core).
Axes of the slice: x: 2, y: 2, z: 4, core: 2. Of those that a mesh axis runs over, the one named last changes fastest.
Arguments:
- readings: bfloat16 [64, 4, 512], P(('tile', 'col')), may hold values from -6 to 6
- sensitivity: bfloat16 [32768, 64, 64], P(('tile', 'col')), may hold values from -0.75 to 0.75
- kept_tile: int32 [32768], P(('tile', 'col')), may hold values from 0 to 7
- kept_row: int32 [32768], P(('tile', 'col')), may hold values from 0 to 7
- kept_slab: int32 [32768, 1], P(('tile', 'col')), may hold values from 0 to 31; in each aligned block of 1024 rows (0 to 1023, 1024 to 2047, ...) at most 80 rows name the same one
- kept_block: int32 [32768], P(('tile', 'col')), may hold values from 0 to 8191
Outputs:
- model_update: float32 [4, 256, 65536], P(None, None, ('tile', 'col'))
The draws below stay inside these ranges and needn't reach their ends.
Inputs may be any that keep to these rules, and one draw needn't show every extreme that they name: `kept_slab`: among the 1024 kept blocks held by one device, at most 80 name one slab, and in every draw some device has exactly 80 blocks naming one slab.
All inputs are finite; a program needn't handle non-finite values.
Results may differ from the reference program's by a relative error of at most 0.0029.
Values may be sent and summed in bfloat16 or wider, within the bound.
A program may use at most 128 MiB of HBM per device.

```python
import math
import jax
import jax.numpy as jnp
import numpy as np
from jax import lax

NX = 256
NY = 256
NZ = 256
VECS = 4
READINGS = 512
BLK = 64
LEVELS = 3
KEPT_DEV = 1024
TILES = 64
GROUP_TILES = 8
KEPT = 32768
CAP = 80
SLAB_BLOCKS = 8192
N_COL = 4
DEVICES = 32


def set_ends(entries, key, low, top_value):
    longest = entries.shape.index(max(entries.shape))
    spots = []
    for shift in (0, 1):
        where = [jax.random.randint(jax.random.fold_in(key, axis), (), 0, length) for axis, length in enumerate(entries.shape)]
        where[longest] = (where[longest] + shift) % entries.shape[longest]
        spots.append(tuple(where))
    return entries.at[spots[0]].set(low).at[spots[1]].set(top_value)


def shard_levels(stream_key, dims, shards, low, high):
    factor_of = 1.0
    for position, parts in shards:
        draws = jax.random.uniform(jax.random.fold_in(jax.random.fold_in(stream_key, 6), position), (parts,), jnp.float32, low / len(shards), high / len(shards))
        factor_of = factor_of * jnp.repeat(jnp.exp(draws), dims[position] // parts).reshape((-1,) + (1,) * (len(dims) - 1 - position))
    return factor_of


def routed_block(stream_key, own, number, rows, number_of, top, limit, skew):
    sequence = jax.random.permutation(stream_key, number_of)
    crowded, common = load_shares(number_of, rows * top, limit, skew, True), load_shares(number_of, rows * top, limit, skew, False)
    places = jnp.arange(number_of)

    def named(tallies, rotation):
        used = int((tallies > 0).sum())
        fixed = max(1, used // 4)
        passed = fixed + (places - fixed + rotation * (used - fixed)) % max(1, number_of - fixed)
        return jnp.zeros((number_of,), jnp.int32).at[sequence[jnp.where(places < fixed, places, passed)]].set(jnp.asarray(tallies, jnp.int32))

    tallies = jnp.where(number % 4 == 0, named(crowded, number // 4), named(common, number - number // 4 - 1))
    mixed = jax.random.permutation(jax.random.fold_in(own, 3), number_of)
    giver, receiver = mixed[0:number_of // 2 * 2:2], mixed[1:number_of // 2 * 2:2]
    margin = jnp.minimum(tallies[giver] - 1, limit - tallies[receiver]) // 2
    margin = jnp.where((giver == sequence[0]) | (receiver == sequence[0]) | (tallies[receiver] == 0), 0, jnp.maximum(margin, 0))
    passed = jax.random.randint(jax.random.fold_in(own, 4), (number_of // 2,), 0, 1 << 20) % (margin + 1)
    tallies = tallies.at[giver].add(-passed).at[receiver].add(passed)
    labels = jnp.searchsorted(jnp.cumsum(tallies), jnp.arange(rows * top), side="right").astype(jnp.int32)
    grid = labels.reshape(top, rows).T
    grid = grid[jax.random.permutation(jax.random.fold_in(own, 1), rows)]
    rotation = jax.random.randint(jax.random.fold_in(own, 2), (rows, 1), 0, top)
    return jnp.take_along_axis(grid, (jnp.arange(top)[None, :] + rotation) % top, axis=1)


def load_shares(number_of, total, reach, skew, full):
    loads = [(1 << 20) // math.isqrt(standing ** skew) + 1 for standing in range(1, number_of + 1)]
    largest = reach if full else min(reach, max(-(-total // number_of), total * loads[0] // sum(loads)))
    least = 1 if total - largest >= number_of - 1 else 0
    holding, spare = [largest] + [least] * (number_of - 1), total - largest - least * (number_of - 1)
    while spare > 0:
        free = [i for i in range(1, number_of) if holding[i] < largest] or [i for i in range(1, number_of) if holding[i] < reach]
        mass, budget = sum([loads[i] for i in free]), spare
        for i in free:
            extra = min(reach - holding[i], max(1, budget * loads[i] // mass), spare)
            holding[i] = holding[i] + extra
            spare = spare - extra
    return np.array(holding)


def bell_draw(stream_key, shape, scale, limit, split=(), kind=jnp.bfloat16):
    values = scale * jax.random.normal(stream_key, shape, jnp.float32)
    if split:
        values = values * shard_levels(stream_key, shape, split, -0.22, 0.18)
    return jnp.clip(values, -limit, limit).astype(kind)


def setup_inputs(seed: int = 0) -> dict:
    splits = jax.random.split(jax.random.key(seed), 7)
    readings = bell_draw(splits[0], (TILES, VECS, READINGS), 1.0, 6.0, ((0, 32),))
    sensitivity = bell_draw(splits[1], (KEPT, BLK, BLK), BLK ** -0.5, 0.75, ((0, 32),))
    kept_tile = set_ends(jax.random.randint(splits[2], (KEPT,), 0, GROUP_TILES), jax.random.fold_in(splits[2], 1), 0, GROUP_TILES - 1).astype(jnp.int32)
    kept_row = set_ends(jax.random.randint(splits[3], (KEPT,), 0, READINGS // BLK), jax.random.fold_in(splits[3], 1), 0, (READINGS // BLK) - 1).astype(jnp.int32)
    kept_slab_keys = jax.random.split(jax.random.fold_in(splits[4], 1), KEPT // KEPT_DEV)
    kept_slab_turns = jax.random.permutation(jax.random.fold_in(splits[4], 3), KEPT // KEPT_DEV)
    kept_slab = jax.vmap(lambda own, number: routed_block(jax.random.fold_in(splits[4], 2), own, number, KEPT_DEV, DEVICES, 1, CAP, 2))(kept_slab_keys, kept_slab_turns).reshape((KEPT, 1))
    kept_block = set_ends(jax.random.randint(splits[5], (KEPT,), 0, SLAB_BLOCKS), jax.random.fold_in(splits[5], 1), 0, SLAB_BLOCKS - 1).astype(jnp.int32)
    return {"readings": readings, "sensitivity": sensitivity, "kept_tile": kept_tile, "kept_row": kept_row, "kept_slab": kept_slab, "kept_block": kept_block}


def inverse_haar(values, dimension):
    length = values.shape[dimension]
    span_now = length // (2 ** LEVELS)
    coarse_part = lax.slice_in_dim(values, 0, span_now, axis=dimension)
    for level in range(LEVELS):
        detail = lax.slice_in_dim(values, span_now, 2 * span_now, axis=dimension)
        even_part = (coarse_part + detail) * 0.7071067811865476
        odd_part = (coarse_part - detail) * 0.7071067811865476
        paired = jnp.stack([even_part, odd_part], axis=dimension + 1)
        new_shape = list(coarse_part.shape)
        new_shape[dimension] = 2 * span_now
        coarse_part = paired.reshape(new_shape)
        span_now = 2 * span_now
    return coarse_part


def reference(readings, sensitivity, kept_tile, kept_row, kept_slab, kept_block):
    total = sensitivity.shape[0]
    group_rows = KEPT_DEV * N_COL
    tile_ids = (jnp.arange(total, dtype=jnp.int32) // group_rows) * GROUP_TILES + kept_tile
    split_readings = readings.reshape(TILES, VECS, READINGS // BLK, BLK)
    row_step = 8192

    def contribute(pieces):
        sens_part, tiles_part, rows_part = pieces
        picked = split_readings[tiles_part, :, rows_part]
        product = jnp.einsum("krj,kvr->kvj", sens_part.astype(jnp.float32), picked.astype(jnp.float32))
        return product.astype(jnp.bfloat16)

    contrib = lax.map(contribute, (sensitivity.reshape(-1, row_step, BLK, BLK), tile_ids.reshape(-1, row_step), kept_row.reshape(-1, row_step)))
    contrib = contrib.reshape(total, VECS * BLK)
    block_ids = kept_slab[:, 0] * SLAB_BLOCKS + kept_block
    coef = jnp.zeros((NZ * NX * (NY // BLK), VECS * BLK), jnp.float32).at[block_ids].add(contrib.astype(jnp.float32))
    coef = coef.reshape(NZ, NX, NY // BLK, VECS, BLK).transpose(3, 0, 2, 4, 1).reshape(VECS, NZ, NY, NX)
    plane = inverse_haar(inverse_haar(coef, 2), 3)
    return inverse_haar(plane, 1).reshape(VECS, NZ, NY * NX)
```

```python
import functools

import jax
import jax.numpy as jnp
from jax import lax
from jax.experimental import pallas as pl
from jax.experimental.pallas import tpu as pltpu
from jax.sharding import PartitionSpec as P

NX = 256
NY = 256
NZ = 256
LEVELS = 3
ROOT = 0.7071067811865476
LANES = 128
BUCKET = 8
MOVES = 8
GROUP = 4
CAP = 80
WINDOW = 24
STEPS = (239 / 256, 169 / 256, 239 / 512, 169 / 512)
REST = 256 / 239
AXES = ("tile", "col")


def segments(length):
    coarse = length // 2**LEVELS
    found = [(0, coarse, 2**LEVELS)]
    for level in range(LEVELS):
        found.append((coarse * 2**level, coarse * 2**level, 2 ** (LEVELS - level)))
    return found


def haar_sign(out_index, in_index, length):
    value = jnp.zeros(jnp.broadcast_shapes(out_index.shape, in_index.shape), jnp.float32)
    for number, (start, count, reach) in enumerate(segments(length)):
        inside = (in_index >= start) & (in_index < start + count)
        meets = inside & (out_index // reach == in_index - start)
        sign = jnp.where(out_index % reach < reach // 2, 1.0, -1.0) if number else 1.0
        value = jnp.where(meets, sign, value)
    return value


def haar_steps(in_index, length):
    scale = jnp.zeros(in_index.shape, jnp.float32)
    for start, count, reach in segments(length):
        inside = (in_index >= start) & (in_index < start + count)
        scale = jnp.where(inside, STEPS[reach.bit_length() - 1], scale)
    return scale


def y_plan(y_share, width):
    rows = []
    used = {}
    for start, count, reach in segments(NY):
        group = min(start // width, 2)
        for i in range(max(1, y_share // reach)):
            slot = used.get(group, 0)
            used[group] = slot + 1
            rows.append((start, reach, i, slot, group))
    return rows, max(used.values())


def contrib_kernel(ids_ref, table_ref, sens_ref, out_ref):
    width, columns, lanes = sens_ref.shape
    vectors = table_ref.shape[0] // width
    spots = lax.broadcasted_iota(jnp.int32, (table_ref.shape[1], lanes), 0)
    chosen = jnp.where(ids_ref[...] == spots, 1.0, 0.0).astype(jnp.bfloat16)
    picked = jnp.dot(table_ref[...], chosen, preferred_element_type=jnp.float32)
    sums = [jnp.zeros((columns, lanes), jnp.float32) for _ in range(vectors)]
    for r in range(width):
        sens = sens_ref[r].astype(jnp.float32)
        for v in range(vectors):
            sums[v] = sums[v] + sens * picked[v * width + r : v * width + r + 1, :]
    for v in range(vectors):
        out_ref[v * columns : (v + 1) * columns, :] = sums[v].astype(jnp.bfloat16)


def model_kernel(
    plan, vectors, from_ref, to_ref, rows_ref, sign_ref, vals_ref, ids_ref, hx_ref, hz_ref, out_ref,
    rows_src, merged, turned, left, right, plane
):
    sources, height, kept = vals_ref.shape
    slots = height // vectors
    buckets = NZ // BUCKET
    rows = kept // GROUP
    y_share = out_ref.shape[2] // NX
    lead = len(plan) * vectors * BUCKET

    @pl.when(pl.program_id(0) == 0)
    def scatter():
        tail = rows_src.shape[0] - sources * rows
        rows_src[pl.ds(sources * rows, tail), :] = jnp.full((tail, LANES), -1.0, jnp.float32)

        def unpack(src, carry):
            for half in range(rows // LANES):
                parts = []
                for k in range(GROUP):
                    parts.append(vals_ref[src, :, k * rows + half * LANES : k * rows + (half + 1) * LANES].astype(jnp.float32))
                parts.append(ids_ref[src, :, half * LANES : (half + 1) * LANES])
                used = GROUP * height + 2 * GROUP
                parts.append(jnp.zeros((LANES - used, LANES), jnp.float32))
                place = pl.ds(pl.multiple_of(src * rows + half * LANES, LANES), LANES)
                rows_src[place, :] = jnp.concatenate(parts, axis=0).T
            return carry

        lax.fori_loop(0, sources, unpack, 0, unroll=2)
        layer = lax.broadcasted_iota(jnp.int32, (BUCKET, LANES), 0).astype(jnp.float32)
        spot = lax.broadcasted_iota(jnp.int32, (NX, LANES), 0).astype(jnp.float32)

        def bucket_step(s, carry):
            def merge(i, carry):
                for u in range(MOVES):
                    at = (i * MOVES + u) * buckets + s
                    merged[pl.ds(to_ref[at], WINDOW), :] = rows_src[pl.ds(from_ref[at], WINDOW), :]
                return carry

            lax.fori_loop(0, sources // MOVES, merge, 0)
            count = rows_ref[s]
            merged[pl.ds(count, LANES), :] = jnp.full((LANES, LANES), -1.0, jnp.float32)
            here = layer + (s * BUCKET).astype(jnp.float32)

            def add(t, total):
                turned[...] = merged[pl.ds(pl.multiple_of(t * LANES, LANES), LANES), :].T
                for k in range(GROUP):
                    x = turned[GROUP * height + k : GROUP * height + k + 1, :]
                    code = turned[GROUP * height + GROUP + k : GROUP * height + GROUP + k + 1, :]
                    marks = [jnp.where(code == here + g * NZ, 1.0, 0.0) for g in range(3)]
                    pieces = []
                    for _, _, _, slot, group in plan:
                        for v in range(vectors):
                            at = k * height + v * slots + slot
                            pieces.append(turned[at : at + 1, :] * marks[group])
                    left[:, k * LANES : (k + 1) * LANES] = jnp.concatenate(pieces, axis=0).astype(jnp.bfloat16)
                    right[:, k * LANES : (k + 1) * LANES] = jnp.where(x == spot, 1.0, 0.0).astype(jnp.bfloat16)
                return total + lax.dot_general(
                    left[...], right[...], (((1,), (1,)), ((), ())), preferred_element_type=jnp.float32
                )

            coef = lax.fori_loop(0, (count + LANES - 1) // LANES, add, jnp.zeros((lead, NX), jnp.float32))
            along_x = jnp.dot(coef.astype(jnp.bfloat16), hx_ref[...], preferred_element_type=jnp.float32)
            inner = vectors * BUCKET
            parts = [along_x[p * inner : (p + 1) * inner, :] for p in range(len(plan))]
            fixed = REST * REST
            current = [parts[0] * (fixed * ROOT**LEVELS)]
            taken = 1
            for level in range(LEVELS):
                reach = 2 ** (LEVELS - level)
                held = max(1, y_share // reach)
                scale = fixed * ROOT ** (LEVELS - level)
                details = parts[taken : taken + held]
                taken += held
                if y_share >= reach:
                    scaled = [d * scale for d in details]
                    current = [e for c, d in zip(current, scaled) for e in (c + d, c - d)]
                else:
                    current = [current[0] + details[0] * (sign_ref[level] * scale)]
            place = pl.ds(pl.multiple_of(s * BUCKET, BUCKET), BUCKET)
            for y in range(y_share):
                for v in range(vectors):
                    plane[v, place, y * NX : (y + 1) * NX] = current[y][v * BUCKET : (v + 1) * BUCKET, :]
            return carry

        lax.fori_loop(0, buckets, bucket_step, 0)

    v = pl.program_id(0)
    for y in range(y_share):
        part = plane[v, :, y * NX : (y + 1) * NX].astype(jnp.bfloat16)
        out_ref[0, :, y * NX : (y + 1) * NX] = jnp.dot(hz_ref[...], part, preferred_element_type=jnp.float32)


def receive(me, plan, vectors, y_share, arrived, all_spots):
    sources, height, kept = arrived.shape
    rows = kept // GROUP
    buckets = NZ // BUCKET
    per_y = NY // 64
    edges = jnp.arange(buckets + 1, dtype=jnp.int32) * (BUCKET * NX * per_y)
    offsets = jnp.sum((all_spots[:, None, :] < edges[None, :, None]).astype(jnp.int32), axis=2)
    low, high = offsets[:, :-1], offsets[:, 1:]
    first = low // GROUP
    counts = jnp.where(high > low, (high + GROUP - 1) // GROUP - first, 0)
    source = jnp.arange(sources, dtype=jnp.int32)
    to = jnp.sum(jnp.where(source[:, None, None] > source[None, :, None], counts[None], 0), axis=1)
    total = jnp.sum(counts, axis=0)
    begin = first + source[:, None] * rows
    grid_spots = all_spots.reshape(sources, GROUP, rows)
    x = (grid_spots // per_y) % NX
    code = grid_spots // (NX * per_y) + NZ * jnp.minimum(grid_spots % per_y, 2)
    ids = jnp.concatenate([x, code], axis=1).astype(jnp.float32)
    full = jnp.arange(NX, dtype=jnp.int32)
    deep = jnp.arange(NZ, dtype=jnp.int32)
    hx = (haar_sign(full[None, :], full[:, None], NX) * haar_steps(full, NX)[:, None]).astype(jnp.bfloat16)
    hz = (haar_sign(deep[:, None], deep[None, :], NZ) * haar_steps(deep, NZ)[None, :]).astype(jnp.bfloat16)
    reaches = 2 ** (LEVELS - jnp.arange(LEVELS, dtype=jnp.int32))
    signs = jnp.where((me * y_share) % reaches < reaches // 2, 1.0, -1.0).astype(jnp.float32)
    lead = len(plan) * vectors * BUCKET
    most = sources * (-(-CAP // GROUP) + 1)
    most = -(-most // LANES) * LANES + LANES
    smem = pl.BlockSpec(memory_space=pltpu.SMEM)

    def whole(array):
        return pl.BlockSpec(array.shape, lambda v: (0,) * array.ndim)

    return pl.pallas_call(
        functools.partial(model_kernel, plan, vectors),
        out_shape=jax.ShapeDtypeStruct((vectors, NZ, y_share * NX), jnp.float32),
        grid=(vectors,),
        in_specs=[smem] * 4 + [whole(arrived), whole(ids), whole(hx), whole(hz)],
        out_specs=pl.BlockSpec((1, NZ, y_share * NX), lambda v: (v, 0, 0)),
        scratch_shapes=[
            pltpu.VMEM((sources * rows + WINDOW, LANES), jnp.float32),
            pltpu.VMEM((most, LANES), jnp.float32),
            pltpu.VMEM((LANES, LANES), jnp.float32),
            pltpu.VMEM((lead, GROUP * LANES), jnp.bfloat16),
            pltpu.VMEM((NX, GROUP * LANES), jnp.bfloat16),
            pltpu.VMEM((vectors, NZ, y_share * NX), jnp.float32),
        ],
        compiler_params=pltpu.CompilerParams(vmem_limit_bytes=60 * 2**20),
    )(begin.reshape(-1), to.reshape(-1), total, signs, arrived, ids, hx, hz)


def on_device(readings, sensitivity, kept_tile, kept_row, kept_slab, kept_block):
    devices = lax.axis_size(AXES)
    columns = lax.axis_size("col")
    me = lax.axis_index(AXES)
    kept, width, _ = sensitivity.shape
    vectors = readings.shape[1]
    per_y = NY // width
    layers = NZ // devices
    y_share = NY // devices
    buckets = NZ // BUCKET
    plan, slots = y_plan(y_share, width)

    depth = kept_slab[:, 0] * layers + kept_block // (NX * per_y)
    spot = depth * (NX * per_y) + kept_block % (NX * per_y)
    number = jnp.arange(kept, dtype=jnp.int32)
    key = (depth // BUCKET) * kept + number
    position = jnp.sum((key[None, :] < key[:, None]).astype(jnp.int32), axis=1)
    position = (position % GROUP) * (kept // GROUP) + position // GROUP
    moved = position[:, None] == number[None, :]
    spots = jnp.sum(jnp.where(moved, spot[:, None], 0), axis=0)
    all_spots = lax.all_to_all(
        jnp.broadcast_to(spots[None], (devices, kept)), AXES, split_axis=0, concat_axis=0, tiled=True
    )
    group = lax.all_to_all(
        jnp.broadcast_to(readings[None], (columns, *readings.shape)), "col", split_axis=0, concat_axis=0, tiled=True
    )
    row_blocks = readings.shape[2] // width
    table = group.reshape(-1, vectors, row_blocks, width).transpose(1, 3, 0, 2).reshape(vectors * width, -1)
    ids = (kept_tile * row_blocks + kept_row)[None, :]
    contrib = pl.pallas_call(
        contrib_kernel,
        out_shape=jax.ShapeDtypeStruct((vectors * width, kept), jnp.bfloat16),
        grid=(kept // LANES,),
        in_specs=[
            pl.BlockSpec((1, LANES), lambda i: (0, i)),
            pl.BlockSpec(table.shape, lambda i: (0, 0)),
            pl.BlockSpec((width, width, LANES), lambda i: (0, 0, i)),
        ],
        out_specs=pl.BlockSpec((vectors * width, LANES), lambda i: (0, i)),
    )(ids, table, sensitivity.transpose(1, 2, 0))

    contrib = jnp.dot(contrib, moved.astype(jnp.bfloat16), preferred_element_type=jnp.float32).astype(jnp.bfloat16)
    in_y = spots % per_y
    masked = jnp.concatenate([jnp.where((in_y == b)[None, :], contrib, 0) for b in range(per_y)], axis=0)
    row = jnp.arange(per_y * vectors * width, dtype=jnp.int32)[None, :]
    lane = jnp.arange(devices * vectors * slots, dtype=jnp.int32)[:, None]
    y_of_row = row // (vectors * width) * width + row % width
    owner = lane // (vectors * slots)
    spread = jnp.zeros((lane.shape[0], row.shape[1]), jnp.bool_)
    for start, reach, i, slot, _ in plan:
        spread = spread | ((lane % slots == slot) & (y_of_row == start + (owner * y_share) // reach + i))
    spread = spread & (row // width % vectors == lane // slots % vectors)
    outgoing = jnp.dot(spread.astype(jnp.bfloat16), masked, preferred_element_type=jnp.float32).astype(jnp.bfloat16)
    arrived = lax.all_to_all(
        outgoing.reshape(devices, vectors * slots, kept), AXES, split_axis=0, concat_axis=0, tiled=True
    )

    return receive(me, plan, vectors, y_share, arrived, all_spots)


def solution(mesh):
    return jax.shard_map(
        on_device,
        mesh=mesh,
        in_specs=(
            P(AXES, None, None),
            P(AXES, None, None),
            P(AXES),
            P(AXES),
            P(AXES, None),
            P(AXES),
        ),
        out_specs=P(None, None, AXES),
        check_vma=False,
    )
```

```python
import functools

import jax
import jax.numpy as jnp
from jax import lax
from jax.experimental import pallas as pl
from jax.experimental.pallas import tpu as pltpu
from jax.sharding import PartitionSpec as P

NX = 256
NY = 256
NZ = 256
LEVELS = 3
ROOT = 0.7071067811865476
LANES = 128
BUCKET = 8
MOVES = 32
WIDE = 1
STRIP = 32
GROUP = 4
CAP = 80
WINDOW = 24
STEPS = (239 / 256, 169 / 256, 239 / 512, 169 / 512)
REST = 256 / 239
AXES = ("tile", "col")


def segments(length):
    coarse = length // 2**LEVELS
    found = [(0, coarse, 2**LEVELS)]
    for level in range(LEVELS):
        found.append((coarse * 2**level, coarse * 2**level, 2 ** (LEVELS - level)))
    return found


def haar_sign(out_index, in_index, length):
    value = jnp.zeros(jnp.broadcast_shapes(out_index.shape, in_index.shape), jnp.float32)
    for number, (start, count, reach) in enumerate(segments(length)):
        inside = (in_index >= start) & (in_index < start + count)
        meets = inside & (out_index // reach == in_index - start)
        sign = jnp.where(out_index % reach < reach // 2, 1.0, -1.0) if number else 1.0
        value = jnp.where(meets, sign, value)
    return value


def haar_steps(in_index, length):
    scale = jnp.zeros(in_index.shape, jnp.float32)
    for start, count, reach in segments(length):
        inside = (in_index >= start) & (in_index < start + count)
        scale = jnp.where(inside, STEPS[reach.bit_length() - 1], scale)
    return scale


def y_plan(y_share, width):
    rows = []
    used = {}
    for start, count, reach in segments(NY):
        group = min(start // width, 2)
        for i in range(max(1, y_share // reach)):
            slot = used.get(group, 0)
            used[group] = slot + 1
            rows.append((start, reach, i, slot, group))
    return rows, max(used.values())


def contrib_kernel(ids_ref, table_ref, sens_ref, out_ref):
    width, columns, lanes = sens_ref.shape
    vectors = table_ref.shape[0] // width
    spots = lax.broadcasted_iota(jnp.int32, (table_ref.shape[1], lanes), 0)
    chosen = jnp.where(ids_ref[...] == spots, 1.0, 0.0).astype(jnp.bfloat16)
    picked = jnp.dot(table_ref[...], chosen, preferred_element_type=jnp.float32)
    sums = [jnp.zeros((columns, lanes), jnp.float32) for _ in range(vectors)]
    for r in range(width):
        sens = sens_ref[r].astype(jnp.float32)
        for v in range(vectors):
            sums[v] = sums[v] + sens * picked[v * width + r : v * width + r + 1, :]
    for v in range(vectors):
        out_ref[v * columns : (v + 1) * columns, :] = sums[v].astype(jnp.bfloat16)


def model_kernel(
    plan, vectors, from_ref, to_ref, rows_ref, sign_ref, vals_ref, ids_ref, hx_ref, hz_ref, out_ref,
    rows_src, merged, turned, left, right, total, plane, along_y
):
    sources, height, kept = vals_ref.shape
    slots = height // vectors
    buckets = NZ // BUCKET
    rows = kept // GROUP
    y_share = out_ref.shape[2] // NX
    lead = len(plan) * vectors

    @pl.when(pl.program_id(0) == 0)
    def scatter():
        tail = rows_src.shape[0] - sources * rows
        rows_src[pl.ds(sources * rows, tail), :] = jnp.full((tail, LANES), -1.0, jnp.float32)

        def unpack(src, carry):
            for half in range(rows // LANES):
                parts = []
                for k in range(GROUP):
                    parts.append(vals_ref[src, :, k * rows + half * LANES : k * rows + (half + 1) * LANES].astype(jnp.float32))
                parts.append(ids_ref[src, :, half * LANES : (half + 1) * LANES])
                used = GROUP * height + 2 * GROUP
                parts.append(jnp.zeros((LANES - used, LANES), jnp.float32))
                place = pl.ds(pl.multiple_of(src * rows + half * LANES, LANES), LANES)
                rows_src[place, :] = jnp.concatenate(parts, axis=0).T
            return carry

        lax.fori_loop(0, sources, unpack, 0, unroll=4)
        layer = lax.broadcasted_iota(jnp.int32, (BUCKET, LANES), 0).astype(jnp.float32)
        spot = lax.broadcasted_iota(jnp.int32, (NX, LANES), 0).astype(jnp.float32).astype(jnp.bfloat16)
        one, zero = jnp.bfloat16(1.0), jnp.bfloat16(0.0)

        def multiply():
            return lax.dot_general(left[...], right[...], (((1,), (1,)), ((), ())), preferred_element_type=jnp.float32)

        def build(s, t):
            here = layer + (s * BUCKET).astype(jnp.float32)
            for w in range(WIDE):
                turned[w] = merged[pl.ds(pl.multiple_of((t * WIDE + w) * LANES, LANES), LANES), :].T
            for w in range(WIDE):
                for k in range(GROUP):
                    columns = slice((w * GROUP + k) * LANES, (w * GROUP + k + 1) * LANES)
                    x = turned[w, GROUP * height + k : GROUP * height + k + 1, :]
                    code = turned[w, GROUP * height + GROUP + k : GROUP * height + GROUP + k + 1, :]
                    marks = [jnp.where(code == here + g * NZ, 1.0, 0.0) for g in range(3)]
                    marks = [jnp.concatenate([m, m], axis=0).astype(jnp.bfloat16) for m in marks]
                    lines = {}
                    for v in range(0, vectors, 2):
                        for slot in range(slots):
                            at = k * height + v * slots + slot
                            pair = [turned[w, i : i + 1, :] for i in (at, at + slots)]
                            pair = [jnp.broadcast_to(line, (BUCKET, LANES)) for line in pair]
                            lines[v, slot] = jnp.concatenate(pair, axis=0).astype(jnp.bfloat16)
                    pieces = []
                    for _, _, _, slot, group in plan:
                        pieces += [lines[v, slot] * marks[group] for v in range(0, vectors, 2)]
                    left[:, columns] = jnp.concatenate(pieces, axis=0)
                    right[:, columns] = jnp.where(x.astype(jnp.bfloat16) == spot, one, zero)

        def store(s, coef):
            place = pl.ds(pl.multiple_of(s * BUCKET, BUCKET), BUCKET)
            plane[:, place, :] = coef.reshape(lead, BUCKET, NX)

        def bucket_step(s, carry):
            def merge(i, carry):
                for u in range(MOVES):
                    at = (i * MOVES + u) * buckets + s
                    merged[pl.ds(to_ref[at], WINDOW), :] = rows_src[pl.ds(from_ref[at], WINDOW), :]
                return carry

            lax.fori_loop(0, sources // MOVES, merge, 0)
            count = rows_ref[s]
            merged[pl.ds(count, WIDE * LANES), :] = jnp.full((WIDE * LANES, LANES), -1.0, jnp.float32)
            last = multiply()
            build(s, 0)
            store(jnp.maximum(s - 1, 0), total[...] + last)
            total[...] = jnp.zeros_like(total)

            def add(t, carry):
                product = multiply()
                build(s, t)
                total[...] += product
                return carry

            lax.fori_loop(1, (count + WIDE * LANES - 1) // (WIDE * LANES), add, 0)
            return carry

        lax.fori_loop(0, buckets, bucket_step, 0)
        store(buckets - 1, total[...] + multiply())

    v = pl.program_id(0)
    fixed = REST * REST
    for begin in range(0, NZ, STRIP):
        strip = [plane[p * vectors + v, begin : begin + STRIP, :] for p in range(len(plan))]
        strip = jnp.concatenate(strip, axis=0).astype(jnp.bfloat16)
        along_x = jnp.dot(strip, hx_ref[...], preferred_element_type=jnp.float32)
        parts = [along_x[p * STRIP : (p + 1) * STRIP, :] for p in range(len(plan))]
        current = [parts[0] * (fixed * ROOT**LEVELS)]
        taken = 1
        for level in range(LEVELS):
            reach = 2 ** (LEVELS - level)
            held = max(1, y_share // reach)
            scale = fixed * ROOT ** (LEVELS - level)
            details = parts[taken : taken + held]
            taken += held
            if y_share >= reach:
                scaled = [d * scale for d in details]
                current = [e for c, d in zip(current, scaled) for e in (c + d, c - d)]
            else:
                current = [current[0] + details[0] * (sign_ref[level] * scale)]
        for y in range(y_share):
            along_y[y, begin : begin + STRIP, :] = current[y].astype(jnp.bfloat16)
    for y in range(y_share):
        out_ref[0, :, y * NX : (y + 1) * NX] = jnp.dot(hz_ref[...], along_y[y], preferred_element_type=jnp.float32)


def receive(me, plan, vectors, y_share, arrived, all_spots):
    sources, height, kept = arrived.shape
    rows = kept // GROUP
    buckets = NZ // BUCKET
    per_y = NY // 64
    edges = jnp.arange(buckets + 1, dtype=jnp.int32) * (BUCKET * NX * per_y)
    offsets = jnp.sum((all_spots[:, None, :] < edges[None, :, None]).astype(jnp.int32), axis=2)
    low, high = offsets[:, :-1], offsets[:, 1:]
    first = low // GROUP
    counts = jnp.where(high > low, (high + GROUP - 1) // GROUP - first, 0)
    source = jnp.arange(sources, dtype=jnp.int32)
    to = jnp.sum(jnp.where(source[:, None, None] > source[None, :, None], counts[None], 0), axis=1)
    total = jnp.sum(counts, axis=0)
    begin = first + source[:, None] * rows
    grid_spots = all_spots.reshape(sources, GROUP, rows)
    x = (grid_spots // per_y) % NX
    code = grid_spots // (NX * per_y) + NZ * jnp.minimum(grid_spots % per_y, 2)
    ids = jnp.concatenate([x, code], axis=1).astype(jnp.float32)
    full = jnp.arange(NX, dtype=jnp.int32)
    deep = jnp.arange(NZ, dtype=jnp.int32)
    hx = (haar_sign(full[None, :], full[:, None], NX) * haar_steps(full, NX)[:, None]).astype(jnp.bfloat16)
    hz = (haar_sign(deep[:, None], deep[None, :], NZ) * haar_steps(deep, NZ)[None, :]).astype(jnp.bfloat16)
    reaches = 2 ** (LEVELS - jnp.arange(LEVELS, dtype=jnp.int32))
    signs = jnp.where((me * y_share) % reaches < reaches // 2, 1.0, -1.0).astype(jnp.float32)
    lead = len(plan) * vectors
    most = sources * (-(-CAP // GROUP) + 1)
    most = (-(-most // (WIDE * LANES)) + 1) * WIDE * LANES
    smem = pl.BlockSpec(memory_space=pltpu.SMEM)

    def whole(array):
        return pl.BlockSpec(array.shape, lambda v: (0,) * array.ndim)

    return pl.pallas_call(
        functools.partial(model_kernel, plan, vectors),
        out_shape=jax.ShapeDtypeStruct((vectors, NZ, y_share * NX), jnp.float32),
        grid=(vectors,),
        in_specs=[smem] * 4 + [whole(arrived), whole(ids), whole(hx), whole(hz)],
        out_specs=pl.BlockSpec((1, NZ, y_share * NX), lambda v: (v, 0, 0)),
        scratch_shapes=[
            pltpu.VMEM((sources * rows + WINDOW, LANES), jnp.float32),
            pltpu.VMEM((most, LANES), jnp.float32),
            pltpu.VMEM((WIDE, LANES, LANES), jnp.float32),
            pltpu.VMEM((lead * BUCKET, WIDE * GROUP * LANES), jnp.bfloat16),
            pltpu.VMEM((NX, WIDE * GROUP * LANES), jnp.bfloat16),
            pltpu.VMEM((lead * BUCKET, NX), jnp.float32),
            pltpu.VMEM((lead, NZ, NX), jnp.float32),
            pltpu.VMEM((y_share, NZ, NX), jnp.bfloat16),
        ],
        compiler_params=pltpu.CompilerParams(vmem_limit_bytes=60 * 2**20),
    )(begin.reshape(-1), to.reshape(-1), total, signs, arrived, ids, hx, hz)


def on_device(readings, sensitivity, kept_tile, kept_row, kept_slab, kept_block):
    devices = lax.axis_size(AXES)
    columns = lax.axis_size("col")
    me = lax.axis_index(AXES)
    kept, width, _ = sensitivity.shape
    vectors = readings.shape[1]
    per_y = NY // width
    layers = NZ // devices
    y_share = NY // devices
    buckets = NZ // BUCKET
    plan, slots = y_plan(y_share, width)

    depth = kept_slab[:, 0] * layers + kept_block // (NX * per_y)
    spot = depth * (NX * per_y) + kept_block % (NX * per_y)
    number = jnp.arange(kept, dtype=jnp.int32)
    key = (depth // BUCKET) * kept + number
    position = jnp.sum((key[None, :] < key[:, None]).astype(jnp.int32), axis=1)
    position = (position % GROUP) * (kept // GROUP) + position // GROUP
    moved = position[:, None] == number[None, :]
    spots = jnp.sum(jnp.where(moved, spot[:, None], 0), axis=0)
    all_spots = lax.all_to_all(
        jnp.broadcast_to(spots[None], (devices, kept)), AXES, split_axis=0, concat_axis=0, tiled=True
    )
    group = lax.all_to_all(
        jnp.broadcast_to(readings[None], (columns, *readings.shape)), "col", split_axis=0, concat_axis=0, tiled=True
    )
    row_blocks = readings.shape[2] // width
    table = group.reshape(-1, vectors, row_blocks, width).transpose(1, 3, 0, 2).reshape(vectors * width, -1)
    ids = (kept_tile * row_blocks + kept_row)[None, :]
    contrib = pl.pallas_call(
        contrib_kernel,
        out_shape=jax.ShapeDtypeStruct((vectors * width, kept), jnp.bfloat16),
        grid=(kept // LANES,),
        in_specs=[
            pl.BlockSpec((1, LANES), lambda i: (0, i)),
            pl.BlockSpec(table.shape, lambda i: (0, 0)),
            pl.BlockSpec((width, width, LANES), lambda i: (0, 0, i)),
        ],
        out_specs=pl.BlockSpec((vectors * width, LANES), lambda i: (0, i)),
    )(ids, table, sensitivity.transpose(1, 2, 0))

    contrib = jnp.dot(contrib, moved.astype(jnp.bfloat16), preferred_element_type=jnp.float32).astype(jnp.bfloat16)
    in_y = spots % per_y
    masked = jnp.concatenate([jnp.where((in_y == b)[None, :], contrib, 0) for b in range(per_y)], axis=0)
    row = jnp.arange(per_y * vectors * width, dtype=jnp.int32)[None, :]
    lane = jnp.arange(devices * vectors * slots, dtype=jnp.int32)[:, None]
    y_of_row = row // (vectors * width) * width + row % width
    owner = lane // (vectors * slots)
    spread = jnp.zeros((lane.shape[0], row.shape[1]), jnp.bool_)
    for start, reach, i, slot, _ in plan:
        spread = spread | ((lane % slots == slot) & (y_of_row == start + (owner * y_share) // reach + i))
    spread = spread & (row // width % vectors == lane // slots % vectors)
    outgoing = jnp.dot(spread.astype(jnp.bfloat16), masked, preferred_element_type=jnp.float32).astype(jnp.bfloat16)
    arrived = lax.all_to_all(
        outgoing.reshape(devices, vectors * slots, kept), AXES, split_axis=0, concat_axis=0, tiled=True
    )

    return receive(me, plan, vectors, y_share, arrived, all_spots)


def solution(mesh):
    return jax.shard_map(
        on_device,
        mesh=mesh,
        in_specs=(
            P(AXES, None, None),
            P(AXES, None, None),
            P(AXES),
            P(AXES),
            P(AXES, None),
            P(AXES),
        ),
        out_specs=P(None, None, AXES),
        check_vma=False,
    )
```

```python
import functools

import jax
import jax.numpy as jnp
import numpy as np
from jax import lax
from jax.experimental import pallas as pl
from jax.experimental.pallas import tpu as pltpu
from jax.sharding import PartitionSpec as P

NX = 256
NY = 256
NZ = 256
LEVELS = 3
ROOT = 0.7071067811865476
LANES = 128
BUCKET = 8
MOVES = 32
WIDE = 1
STRIP = 32
PACK = 2
GROUP = 4
CAP = 80
WINDOW = 24
STEPS = (239 / 256, 169 / 256, 239 / 512, 169 / 512)
REST = 256 / 239
AXES = ("tile", "col")


def segments(length):
    coarse = length // 2**LEVELS
    found = [(0, coarse, 2**LEVELS)]
    for level in range(LEVELS):
        found.append((coarse * 2**level, coarse * 2**level, 2 ** (LEVELS - level)))
    return found


def haar(length):
    matrix = np.zeros((length, length), np.float32)
    for number, (start, count, reach) in enumerate(segments(length)):
        for i in range(count):
            half = reach // 2 if number else reach
            matrix[start + i, i * reach : i * reach + half] = STEPS[reach.bit_length() - 1]
            matrix[start + i, i * reach + half : (i + 1) * reach] = -STEPS[reach.bit_length() - 1]
    return matrix


def y_plan(y_share, width):
    rows = []
    used = {}
    for start, count, reach in segments(NY):
        group = min(start // width, 2)
        for i in range(max(1, y_share // reach)):
            slot = used.get(group, 0)
            used[group] = slot + 1
            rows.append((start, reach, i, slot, group))
    return rows, max(used.values())


def spread_matrix(plan, slots, devices, vectors, width, y_share):
    per_y = NY // width
    matrix = np.zeros((devices, vectors, slots, per_y, vectors, width), np.float32)
    for start, reach, i, slot, _ in plan:
        for owner in range(devices):
            y = start + owner * y_share // reach + i
            for v in range(vectors):
                matrix[owner, v, slot, y // width, v, y % width] = 1.0
    return matrix.reshape(devices * vectors * slots, per_y * vectors * width)


def gather_kernel(lift, mine_ref, slab_ref, block_ref, group_ref, place_ref, sorted_ref, send_sem, recv_sem):
    columns = group_ref.shape[0]
    tile, col = lax.axis_index("tile"), lax.axis_index("col")
    barrier = pltpu.get_barrier_semaphore()

    def greet(i, carry):
        other = lax.rem(col + i, columns)
        pl.semaphore_signal(barrier, inc=1, device_id=(tile, other), device_id_type=pl.DeviceIdType.MESH)
        return carry

    lax.fori_loop(1, columns, greet, 0)
    spot = slab_ref[...] * lift + block_ref[...]
    chunks, lanes = spot.shape
    kept = chunks * lanes
    number = lax.broadcasted_iota(jnp.int32, (chunks, lanes), 0) * lanes + lax.broadcasted_iota(jnp.int32, (chunks, lanes), 1)
    key = ((spot // (BUCKET * NX * (NY // 64))) * kept + number).astype(jnp.float32)
    spot = spot.astype(jnp.float32)
    pl.semaphore_wait(barrier, columns - 1)

    def send(i, carry):
        other = lax.rem(col + i, columns)
        pltpu.make_async_remote_copy(
            src_ref=mine_ref, dst_ref=group_ref.at[col], send_sem=send_sem, recv_sem=recv_sem,
            device_id=(tile, other), device_id_type=pl.DeviceIdType.MESH,
        ).start()
        return carry

    lax.fori_loop(1, columns, send, 0)

    def upright(rows):
        return [jnp.broadcast_to(rows[c : c + 1, :], (lanes, lanes)).T for c in range(chunks)]

    key_up, spot_up = upright(key), upright(spot)
    ranks = []
    for c in range(chunks):
        line = key[c : c + 1, :]
        total = jnp.zeros((lanes, lanes), jnp.float32)
        for d in range(chunks):
            total = total + jnp.where(key_up[d] < line, 1.0, 0.0)
        ranks.append(jnp.sum(total, axis=0, keepdims=True))
    rank = jnp.concatenate(ranks, axis=0).astype(jnp.int32)
    wide = GROUP * lanes
    place = (rank // wide) * wide + (rank % GROUP) * lanes + (rank // GROUP) % lanes
    place_ref[...] = place
    place_up = upright(place.astype(jnp.float32))
    goal = number.astype(jnp.float32)
    spots = []
    for c in range(chunks):
        line = goal[c : c + 1, :]
        total = jnp.zeros((lanes, lanes), jnp.float32)
        for d in range(chunks):
            total = total + jnp.where(place_up[d] == line, spot_up[d], 0.0)
        spots.append(jnp.sum(total, axis=0, keepdims=True))
    sorted_ref[...] = jnp.concatenate(spots, axis=0).astype(jnp.int32)
    group_ref[col] = mine_ref[...]
    others = group_ref.at[pl.ds(0, columns - 1)]
    wait = pltpu.make_async_remote_copy(
        src_ref=others, dst_ref=others, send_sem=send_sem, recv_sem=recv_sem,
        device_id=(tile, col), device_id_type=pl.DeviceIdType.MESH,
    )
    wait.wait_send()
    wait.wait_recv()


def products_kernel(ids_ref, table_ref, place_ref, sorted_ref, spread_ref, sens_ref, out_ref, picked, made):
    width, columns, lanes = sens_ref.shape
    vectors = table_ref.shape[0] // width
    step = pl.program_id(0)
    spots = lax.broadcasted_iota(jnp.int32, (table_ref.shape[1], lanes), 0)
    chosen = jnp.where(ids_ref[...] == spots, 1.0, 0.0).astype(jnp.bfloat16)
    picked[...] = jnp.dot(table_ref[...], chosen, preferred_element_type=jnp.float32)
    sums = [jnp.zeros((columns, lanes), jnp.float32) for _ in range(vectors)]
    for r in range(width):
        sens = sens_ref[r].astype(jnp.float32)
        for v in range(vectors):
            sums[v] = sums[v] + sens * picked[v * width + r : v * width + r + 1, :]
    here = pl.ds(pl.multiple_of(step * lanes, lanes), lanes)
    for v in range(vectors):
        made[v * columns : (v + 1) * columns, here] = sums[v].astype(jnp.bfloat16)

    @pl.when(step == pl.num_programs(0) - 1)
    def send_order():
        chunks = place_ref.shape[0]
        per_y = NY // width
        goal = lax.broadcasted_iota(jnp.int32, (PACK * lanes, lanes), 0)
        for c in range(0, chunks, PACK):
            moved = [jnp.where(place_ref[d : d + 1, :] - c * lanes == goal, 1.0, 0.0) for d in range(chunks)]
            moved = jnp.concatenate(moved, axis=1).astype(jnp.bfloat16)
            ordered = lax.dot_general(made[...], moved, (((1,), (1,)), ((), ())), preferred_element_type=jnp.float32)
            in_y = jnp.concatenate([sorted_ref[d : d + 1, :] for d in range(c, c + PACK)], axis=1) % per_y
            masked = [jnp.where(in_y == b, ordered, 0.0).astype(jnp.bfloat16) for b in range(per_y)]
            masked = jnp.concatenate(masked, axis=0)
            sent = jnp.dot(spread_ref[...], masked, preferred_element_type=jnp.float32)
            out_ref[:, c * lanes : (c + PACK) * lanes] = sent.astype(jnp.bfloat16)


def exchange_kernel(columns, out_ref, in_ref, send_sem, recv_sem, own_sem):
    devices = out_ref.shape[0]
    me = lax.axis_index("tile") * columns + lax.axis_index("col")
    own = pltpu.make_async_copy(out_ref.at[me], in_ref.at[me], own_sem)
    own.start()
    barrier = pltpu.get_barrier_semaphore()

    def greet(i, carry):
        other = lax.rem(me + i, devices)
        where = (other // columns, lax.rem(other, columns))
        pl.semaphore_signal(barrier, inc=1, device_id=where, device_id_type=pl.DeviceIdType.MESH)
        return carry

    lax.fori_loop(1, devices, greet, 0)
    pl.semaphore_wait(barrier, devices - 1)

    def send(i, carry):
        other = lax.rem(me + i, devices)
        where = (other // columns, lax.rem(other, columns))
        pltpu.make_async_remote_copy(
            src_ref=out_ref.at[other], dst_ref=in_ref.at[me], send_sem=send_sem, recv_sem=recv_sem,
            device_id=where, device_id_type=pl.DeviceIdType.MESH,
        ).start()
        return carry

    lax.fori_loop(1, devices, send, 0)
    own.wait()
    others = pl.ds(0, devices - 1)
    wait = pltpu.make_async_remote_copy(
        src_ref=out_ref.at[others], dst_ref=in_ref.at[others], send_sem=send_sem, recv_sem=recv_sem,
        device_id=(lax.axis_index("tile"), lax.axis_index("col")), device_id_type=pl.DeviceIdType.MESH,
    )
    wait.wait_send()
    wait.wait_recv()


def index_kernel(spots_ref, begin_ref, to_ref, total_ref):
    sources, kept = spots_ref.shape
    lane = lax.broadcasted_iota(jnp.int32, (sources, LANES), 1)
    low = jnp.zeros((sources, LANES), jnp.float32)
    buckets = NZ // BUCKET
    spots = spots_ref[...]
    for s in range(1, buckets + 1):
        below = jnp.where(spots < s * (BUCKET * NX * (NY // 64)), 1.0, 0.0)
        sums = below[:, :LANES]
        for c in range(LANES, kept, LANES):
            sums = sums + below[:, c : c + LANES]
        low = jnp.where(lane == s, jnp.sum(sums, axis=1, keepdims=True), low)
    low = low.astype(jnp.int32)
    high = pltpu.roll(low, LANES - 1, 1)
    first = low // GROUP
    counts = jnp.where(high > low, (high + GROUP - 1) // GROUP - first, 0)
    counts = jnp.where(lane < buckets, counts, 0).astype(jnp.float32)
    row = lax.broadcasted_iota(jnp.int32, (sources, sources), 0)
    before = jnp.where(row > lax.broadcasted_iota(jnp.int32, (sources, sources), 1), 1.0, 0.0)
    ahead = jnp.dot(before.astype(jnp.bfloat16), counts.astype(jnp.bfloat16), preferred_element_type=jnp.float32)
    source = lax.broadcasted_iota(jnp.int32, (sources, LANES), 0)
    begin_ref[...] = first + source * (kept // GROUP)
    to_ref[...] = ahead.astype(jnp.int32)
    total_ref[...] = jnp.broadcast_to(jnp.sum(counts, axis=0, keepdims=True), (8, LANES)).astype(jnp.int32)


def model_kernel(
    plan, vectors, from_ref, to_ref, rows_ref, sign_ref, vals_ref, spots_ref, hx_ref, hz_ref, out_ref,
    rows_src, merged, turned, left, right, total, plane, along_y
):
    sources, height, kept = vals_ref.shape
    slots = height // vectors
    buckets = NZ // BUCKET
    rows = kept // GROUP
    y_share = out_ref.shape[2] // NX
    lead = len(plan) * vectors

    @pl.when(pl.program_id(0) == 0)
    def scatter():
        tail = rows_src.shape[0] - sources * rows
        rows_src[pl.ds(sources * rows, tail), :] = jnp.full((tail, LANES), -1.0, jnp.float32)

        def unpack(src, carry):
            per_y = NY // 64
            spots = spots_ref[src]
            x = ((spots // per_y) % NX).astype(jnp.float32)
            code = (spots // (NX * per_y) + NZ * jnp.minimum(spots % per_y, 2)).astype(jnp.float32)
            for half in range(rows // LANES):
                parts = []
                for k in range(GROUP):
                    first = (half * GROUP + k) * LANES
                    parts.append(vals_ref[src, :, first : first + LANES].astype(jnp.float32))
                parts.append(x[half * GROUP : (half + 1) * GROUP, :])
                parts.append(code[half * GROUP : (half + 1) * GROUP, :])
                used = GROUP * height + 2 * GROUP
                parts.append(jnp.zeros((LANES - used, LANES), jnp.float32))
                place = pl.ds(pl.multiple_of(src * rows + half * LANES, LANES), LANES)
                rows_src[place, :] = jnp.concatenate(parts, axis=0).T
            return carry

        lax.fori_loop(0, sources, unpack, 0, unroll=4)
        layer = lax.broadcasted_iota(jnp.int32, (BUCKET, LANES), 0).astype(jnp.float32)
        spot = lax.broadcasted_iota(jnp.int32, (NX, LANES), 0).astype(jnp.float32).astype(jnp.bfloat16)
        one, zero = jnp.bfloat16(1.0), jnp.bfloat16(0.0)

        def multiply():
            return lax.dot_general(left[...], right[...], (((1,), (1,)), ((), ())), preferred_element_type=jnp.float32)

        def build(s, t):
            here = layer + (s * BUCKET).astype(jnp.float32)
            for w in range(WIDE):
                turned[w] = merged[pl.ds(pl.multiple_of((t * WIDE + w) * LANES, LANES), LANES), :].T
            for w in range(WIDE):
                for k in range(GROUP):
                    columns = slice((w * GROUP + k) * LANES, (w * GROUP + k + 1) * LANES)
                    x = turned[w, GROUP * height + k : GROUP * height + k + 1, :]
                    code = turned[w, GROUP * height + GROUP + k : GROUP * height + GROUP + k + 1, :]
                    marks = [jnp.where(code == here + g * NZ, 1.0, 0.0) for g in range(3)]
                    marks = [jnp.concatenate([m, m], axis=0).astype(jnp.bfloat16) for m in marks]
                    lines = {}
                    for v in range(0, vectors, 2):
                        for slot in range(slots):
                            at = k * height + v * slots + slot
                            pair = [turned[w, i : i + 1, :] for i in (at, at + slots)]
                            pair = [jnp.broadcast_to(line, (BUCKET, LANES)) for line in pair]
                            lines[v, slot] = jnp.concatenate(pair, axis=0).astype(jnp.bfloat16)
                    pieces = []
                    for _, _, _, slot, group in plan:
                        pieces += [lines[v, slot] * marks[group] for v in range(0, vectors, 2)]
                    left[:, columns] = jnp.concatenate(pieces, axis=0)
                    right[:, columns] = jnp.where(x.astype(jnp.bfloat16) == spot, one, zero)

        def store(s, coef):
            place = pl.ds(pl.multiple_of(s * BUCKET, BUCKET), BUCKET)
            plane[:, place, :] = coef.reshape(lead, BUCKET, NX)

        def bucket_step(s, carry):
            def merge(i, carry):
                for u in range(MOVES):
                    src = i * MOVES + u
                    merged[pl.ds(to_ref[src, s], WINDOW), :] = rows_src[pl.ds(from_ref[src, s], WINDOW), :]
                return carry

            lax.fori_loop(0, sources // MOVES, merge, 0)
            count = rows_ref[0, s]
            merged[pl.ds(count, WIDE * LANES), :] = jnp.full((WIDE * LANES, LANES), -1.0, jnp.float32)
            last = multiply()
            build(s, 0)
            store(jnp.maximum(s - 1, 0), total[...] + last)
            total[...] = jnp.zeros_like(total)

            def add(t, carry):
                product = multiply()
                build(s, t)
                total[...] += product
                return carry

            lax.fori_loop(1, (count + WIDE * LANES - 1) // (WIDE * LANES), add, 0)
            return carry

        lax.fori_loop(0, buckets, bucket_step, 0)
        store(buckets - 1, total[...] + multiply())

    v = pl.program_id(0)
    fixed = REST * REST
    for begin in range(0, NZ, STRIP):
        strip = [plane[p * vectors + v, begin : begin + STRIP, :] for p in range(len(plan))]
        strip = jnp.concatenate(strip, axis=0).astype(jnp.bfloat16)
        along_x = jnp.dot(strip, hx_ref[...], preferred_element_type=jnp.float32)
        parts = [along_x[p * STRIP : (p + 1) * STRIP, :] for p in range(len(plan))]
        current = [parts[0] * (fixed * ROOT**LEVELS)]
        taken = 1
        for level in range(LEVELS):
            reach = 2 ** (LEVELS - level)
            held = max(1, y_share // reach)
            scale = fixed * ROOT ** (LEVELS - level)
            details = parts[taken : taken + held]
            taken += held
            if y_share >= reach:
                scaled = [d * scale for d in details]
                current = [e for c, d in zip(current, scaled) for e in (c + d, c - d)]
            else:
                current = [current[0] + details[0] * (sign_ref[level] * scale)]
        for y in range(y_share):
            along_y[y, begin : begin + STRIP, :] = current[y].astype(jnp.bfloat16)
    for y in range(y_share):
        out_ref[0, :, y * NX : (y + 1) * NX] = jnp.dot(hz_ref[...], along_y[y], preferred_element_type=jnp.float32)


def receive(me, plan, vectors, y_share, arrived, all_spots):
    sources, height, kept = arrived.shape
    rows = kept // GROUP
    table = jax.ShapeDtypeStruct((sources, LANES), jnp.int32)
    begin, to, total = pl.pallas_call(
        index_kernel, out_shape=(table, table, jax.ShapeDtypeStruct((8, LANES), jnp.int32))
    )(all_spots)
    hx = jnp.asarray(haar(NX), jnp.bfloat16)
    hz = jnp.asarray(haar(NZ).T, jnp.bfloat16)
    signs = jnp.ones((LEVELS,), jnp.float32)
    if y_share < 2**LEVELS:
        reaches = 2 ** (LEVELS - jnp.arange(LEVELS, dtype=jnp.int32))
        signs = jnp.where((me * y_share) % reaches < reaches // 2, 1.0, -1.0).astype(jnp.float32)
    all_spots = all_spots.reshape(sources, kept // LANES, LANES)
    lead = len(plan) * vectors
    most = sources * (-(-CAP // GROUP) + 1)
    most = (-(-most // (WIDE * LANES)) + 1) * WIDE * LANES
    smem = pl.BlockSpec(memory_space=pltpu.SMEM)

    def whole(array):
        return pl.BlockSpec(array.shape, lambda v: (0,) * array.ndim)

    return pl.pallas_call(
        functools.partial(model_kernel, plan, vectors),
        out_shape=jax.ShapeDtypeStruct((vectors, NZ, y_share * NX), jnp.float32),
        grid=(vectors,),
        in_specs=[smem] * 4 + [whole(arrived), whole(all_spots), whole(hx), whole(hz)],
        out_specs=pl.BlockSpec((1, NZ, y_share * NX), lambda v: (v, 0, 0)),
        scratch_shapes=[
            pltpu.VMEM((sources * rows + WINDOW, LANES), jnp.float32),
            pltpu.VMEM((most, LANES), jnp.float32),
            pltpu.VMEM((WIDE, LANES, LANES), jnp.float32),
            pltpu.VMEM((lead * BUCKET, WIDE * GROUP * LANES), jnp.bfloat16),
            pltpu.VMEM((NX, WIDE * GROUP * LANES), jnp.bfloat16),
            pltpu.VMEM((lead * BUCKET, NX), jnp.float32),
            pltpu.VMEM((lead, NZ, NX), jnp.float32),
            pltpu.VMEM((y_share, NZ, NX), jnp.bfloat16),
        ],
        compiler_params=pltpu.CompilerParams(vmem_limit_bytes=60 * 2**20),
    )(begin, to, total, signs, arrived, all_spots, hx, hz)


def on_device(readings, sensitivity, kept_tile, kept_row, kept_slab, kept_block):
    devices = lax.axis_size(AXES)
    columns = lax.axis_size("col")
    me = lax.axis_index(AXES)
    kept, width, _ = sensitivity.shape
    vectors = readings.shape[1]
    per_y = NY // width
    layers = NZ // devices
    y_share = NY // devices
    plan, slots = y_plan(y_share, width)
    chunks = kept // LANES
    square = jax.ShapeDtypeStruct((chunks, LANES), jnp.int32)
    mine = readings.reshape(16, -1)
    vmem = pl.BlockSpec(memory_space=pltpu.VMEM)
    group, place, spots = pl.pallas_call(
        functools.partial(gather_kernel, layers * NX * per_y),
        out_shape=(jax.ShapeDtypeStruct((columns, *mine.shape), mine.dtype), square, square),
        in_specs=[vmem] * 3,
        out_specs=(vmem, vmem, vmem),
        scratch_shapes=[pltpu.SemaphoreType.DMA, pltpu.SemaphoreType.DMA],
        compiler_params=pltpu.CompilerParams(collective_id=0, has_side_effects=True),
    )(mine, kept_slab.reshape(chunks, LANES), kept_block.reshape(chunks, LANES))
    all_spots = lax.all_gather(spots.reshape(kept), AXES)

    row_blocks = readings.shape[2] // width
    table = group.reshape(-1, vectors, row_blocks, width).transpose(1, 3, 0, 2).reshape(vectors * width, -1)
    ids = (kept_tile * row_blocks + kept_row)[None, :]
    spread = jnp.asarray(spread_matrix(plan, slots, devices, vectors, width, y_share), jnp.bfloat16)
    outgoing = pl.pallas_call(
        products_kernel,
        out_shape=jax.ShapeDtypeStruct((devices * vectors * slots, kept), jnp.bfloat16),
        grid=(chunks,),
        in_specs=[
            pl.BlockSpec((1, LANES), lambda i: (0, i)),
            pl.BlockSpec(table.shape, lambda i: (0, 0)),
            pl.BlockSpec((chunks, LANES), lambda i: (0, 0)),
            pl.BlockSpec((chunks, LANES), lambda i: (0, 0)),
            pl.BlockSpec(spread.shape, lambda i: (0, 0)),
            pl.BlockSpec((width, width, LANES), lambda i: (0, 0, i)),
        ],
        out_specs=pl.BlockSpec((devices * vectors * slots, kept), lambda i: (0, 0)),
        scratch_shapes=[
            pltpu.VMEM((vectors * width, LANES), jnp.float32),
            pltpu.VMEM((vectors * width, kept), jnp.bfloat16),
        ],
        compiler_params=pltpu.CompilerParams(vmem_limit_bytes=48 * 2**20),
    )(ids, table, place, spots, spread, sensitivity.transpose(1, 2, 0))
    outgoing = outgoing.reshape(devices, vectors * slots, kept)
    arrived = pl.pallas_call(
        functools.partial(exchange_kernel, columns),
        out_shape=jax.ShapeDtypeStruct(outgoing.shape, outgoing.dtype),
        in_specs=[vmem],
        out_specs=vmem,
        scratch_shapes=[pltpu.SemaphoreType.DMA] * 3,
        compiler_params=pltpu.CompilerParams(
            collective_id=1, has_side_effects=True, vmem_limit_bytes=48 * 2**20
        ),
    )(outgoing)
    return receive(me, plan, vectors, y_share, arrived, all_spots)


def solution(mesh):
    return jax.shard_map(
        on_device,
        mesh=mesh,
        in_specs=(
            P(AXES, None, None),
            P(AXES, None, None),
            P(AXES),
            P(AXES),
            P(AXES, None),
            P(AXES),
        ),
        out_specs=P(None, None, AXES),
        check_vma=False,
    )
```

```python
import functools

import jax
import jax.numpy as jnp
import numpy as np
from jax import lax
from jax.experimental import pallas as pl
from jax.experimental.pallas import tpu as pltpu
from jax.sharding import PartitionSpec as P

NX = 256
NY = 256
NZ = 256
LEVELS = 3
ROOT = 0.7071067811865476
LANES = 128
BUCKET = 8
MOVES = 32
WIDE = 1
STRIP = 32
PACK = 2
GROUP = 4
CAP = 80
WINDOW = 24
STEPS = (239 / 256, 169 / 256, 239 / 512, 169 / 512)
REST = 256 / 239
AXES = ("tile", "col")


def segments(length):
    coarse = length // 2**LEVELS
    found = [(0, coarse, 2**LEVELS)]
    for level in range(LEVELS):
        found.append((coarse * 2**level, coarse * 2**level, 2 ** (LEVELS - level)))
    return found


def haar(length):
    matrix = np.zeros((length, length), np.float32)
    for number, (start, count, reach) in enumerate(segments(length)):
        for i in range(count):
            half = reach // 2 if number else reach
            matrix[start + i, i * reach : i * reach + half] = STEPS[reach.bit_length() - 1]
            matrix[start + i, i * reach + half : (i + 1) * reach] = -STEPS[reach.bit_length() - 1]
    return matrix


def y_plan(y_share, width):
    rows = []
    used = {}
    for start, count, reach in segments(NY):
        group = min(start // width, 2)
        for i in range(max(1, y_share // reach)):
            slot = used.get(group, 0)
            used[group] = slot + 1
            rows.append((start, reach, i, slot, group))
    return rows, max(used.values())


def spread_matrix(plan, slots, devices, vectors, width, y_share):
    per_y = NY // width
    matrix = np.zeros((devices, vectors, slots, per_y, vectors, width), np.float32)
    for start, reach, i, slot, _ in plan:
        for owner in range(devices):
            y = start + owner * y_share // reach + i
            for v in range(vectors):
                matrix[owner, v, slot, y // width, v, y % width] = 1.0
    return matrix.reshape(devices * vectors * slots, per_y * vectors * width)


def gather_kernel(lift, mine_ref, slab_ref, block_ref, group_ref, place_ref, sorted_ref, send_sem, recv_sem):
    columns = group_ref.shape[0]
    tile, col = lax.axis_index("tile"), lax.axis_index("col")
    barrier = pltpu.get_barrier_semaphore()

    def greet(i, carry):
        other = lax.rem(col + i, columns)
        pl.semaphore_signal(barrier, inc=1, device_id=(tile, other), device_id_type=pl.DeviceIdType.MESH)
        return carry

    lax.fori_loop(1, columns, greet, 0)
    spot = slab_ref[...] * lift + block_ref[...]
    chunks, lanes = spot.shape
    kept = chunks * lanes
    number = lax.broadcasted_iota(jnp.int32, (chunks, lanes), 0) * lanes + lax.broadcasted_iota(jnp.int32, (chunks, lanes), 1)
    key = ((spot // (BUCKET * NX * (NY // 64))) * kept + number).astype(jnp.float32)
    spot = spot.astype(jnp.float32)
    pl.semaphore_wait(barrier, columns - 1)

    def send(i, carry):
        other = lax.rem(col + i, columns)
        pltpu.make_async_remote_copy(
            src_ref=mine_ref, dst_ref=group_ref.at[col], send_sem=send_sem, recv_sem=recv_sem,
            device_id=(tile, other), device_id_type=pl.DeviceIdType.MESH,
        ).start()
        return carry

    lax.fori_loop(1, columns, send, 0)

    def upright(rows):
        return [jnp.broadcast_to(rows[c : c + 1, :], (lanes, lanes)).T for c in range(chunks)]

    key_up, spot_up = upright(key), upright(spot)
    ranks = []
    for c in range(chunks):
        line = key[c : c + 1, :]
        total = jnp.zeros((lanes, lanes), jnp.float32)
        for d in range(chunks):
            total = total + jnp.where(key_up[d] < line, 1.0, 0.0)
        ranks.append(jnp.sum(total, axis=0, keepdims=True))
    rank = jnp.concatenate(ranks, axis=0).astype(jnp.int32)
    wide = GROUP * lanes
    place = (rank // wide) * wide + (rank % GROUP) * lanes + (rank // GROUP) % lanes
    place_ref[...] = place
    place_up = upright(place.astype(jnp.float32))
    goal = number.astype(jnp.float32)
    spots = []
    for c in range(chunks):
        line = goal[c : c + 1, :]
        total = jnp.zeros((lanes, lanes), jnp.float32)
        for d in range(chunks):
            total = total + jnp.where(place_up[d] == line, spot_up[d], 0.0)
        spots.append(jnp.sum(total, axis=0, keepdims=True))
    sorted_ref[...] = jnp.concatenate(spots, axis=0).astype(jnp.int32)
    group_ref[col] = mine_ref[...]
    others = group_ref.at[pl.ds(0, columns - 1)]
    wait = pltpu.make_async_remote_copy(
        src_ref=others, dst_ref=others, send_sem=send_sem, recv_sem=recv_sem,
        device_id=(tile, col), device_id_type=pl.DeviceIdType.MESH,
    )
    wait.wait_send()
    wait.wait_recv()


def products_kernel(tiles_ref, rows_ref, group_ref, place_ref, sorted_ref, spread_ref, sens_ref, out_ref, table, picked, made):
    width, columns, lanes = sens_ref.shape
    sources, share, vectors, readings = group_ref.shape
    tiles = sources * share
    row_blocks = readings // width
    step = pl.program_id(0)

    @pl.when(step == 0)
    def make_table():
        lines = [group_ref[i, j].astype(jnp.float32) for i in range(sources) for j in range(share)]
        by_vector = [jnp.concatenate([line[v : v + 1, :] for line in lines], axis=0) for v in range(vectors)]
        rows = []
        for b in range(row_blocks):
            rows.append(jnp.concatenate([a[:, b * width : (b + 1) * width] for a in by_vector], axis=1))
        if row_blocks * tiles < table.shape[1]:
            rows.append(jnp.zeros((table.shape[1] - row_blocks * tiles, vectors * width), jnp.float32))
        table[...] = jnp.concatenate(rows, axis=0).T.astype(jnp.bfloat16)

    spots = lax.broadcasted_iota(jnp.int32, (table.shape[1], lanes), 0)
    chosen = jnp.where(rows_ref[...] * tiles + tiles_ref[...] == spots, 1.0, 0.0).astype(jnp.bfloat16)
    picked[...] = jnp.dot(table[...], chosen, preferred_element_type=jnp.float32)
    sums = [jnp.zeros((columns, lanes), jnp.float32) for _ in range(vectors)]
    for r in range(width):
        sens = sens_ref[r].astype(jnp.float32)
        for v in range(vectors):
            sums[v] = sums[v] + sens * picked[v * width + r : v * width + r + 1, :]
    here = pl.ds(pl.multiple_of(step * lanes, lanes), lanes)
    for v in range(vectors):
        made[v * columns : (v + 1) * columns, here] = sums[v].astype(jnp.bfloat16)

    @pl.when(step == pl.num_programs(0) - 1)
    def send_order():
        chunks = place_ref.shape[0]
        per_y = NY // width
        goal = lax.broadcasted_iota(jnp.int32, (PACK * lanes, lanes), 0)
        for c in range(0, chunks, PACK):
            moved = [jnp.where(place_ref[d : d + 1, :] - c * lanes == goal, 1.0, 0.0) for d in range(chunks)]
            moved = jnp.concatenate(moved, axis=1).astype(jnp.bfloat16)
            ordered = lax.dot_general(made[...], moved, (((1,), (1,)), ((), ())), preferred_element_type=jnp.float32)
            in_y = jnp.concatenate([sorted_ref[d : d + 1, :] for d in range(c, c + PACK)], axis=1) % per_y
            masked = [jnp.where(in_y == b, ordered, 0.0).astype(jnp.bfloat16) for b in range(per_y)]
            masked = jnp.concatenate(masked, axis=0)
            sent = jnp.dot(spread_ref[...], masked, preferred_element_type=jnp.float32)
            out_ref[:, c * lanes : (c + PACK) * lanes] = sent.astype(jnp.bfloat16)


def exchange_kernel(columns, out_ref, spots_ref, in_ref, all_ref, table_ref, send_sem, recv_sem, own_sem, spots_send, spots_recv):
    devices = out_ref.shape[0]
    me = lax.axis_index("tile") * columns + lax.axis_index("col")
    own = pltpu.make_async_copy(out_ref.at[me], in_ref.at[me], own_sem)
    own.start()
    barrier = pltpu.get_barrier_semaphore()

    def place(i):
        other = lax.rem(me + i, devices)
        return other, (other // columns, lax.rem(other, columns))

    def greet(i, carry):
        pl.semaphore_signal(barrier, inc=1, device_id=place(i)[1], device_id_type=pl.DeviceIdType.MESH)
        return carry

    lax.fori_loop(1, devices, greet, 0)
    all_ref[me] = spots_ref[...]
    pl.semaphore_wait(barrier, devices - 1)

    def send_spots(i, carry):
        pltpu.make_async_remote_copy(
            src_ref=spots_ref, dst_ref=all_ref.at[me], send_sem=spots_send, recv_sem=spots_recv,
            device_id=place(i)[1], device_id_type=pl.DeviceIdType.MESH,
        ).start()
        return carry

    lax.fori_loop(1, devices, send_spots, 0)

    def send(i, carry):
        other, where = place(i)
        pltpu.make_async_remote_copy(
            src_ref=out_ref.at[other], dst_ref=in_ref.at[me], send_sem=send_sem, recv_sem=recv_sem,
            device_id=where, device_id_type=pl.DeviceIdType.MESH,
        ).start()
        return carry

    lax.fori_loop(1, devices, send, 0)
    others = pl.ds(0, devices - 1)
    here = (lax.axis_index("tile"), lax.axis_index("col"))
    wait = pltpu.make_async_remote_copy(
        src_ref=all_ref.at[others], dst_ref=all_ref.at[others], send_sem=spots_send, recv_sem=spots_recv,
        device_id=here, device_id_type=pl.DeviceIdType.MESH,
    )
    wait.wait_send()
    wait.wait_recv()
    index_tables(all_ref, table_ref)
    own.wait()
    wait = pltpu.make_async_remote_copy(
        src_ref=out_ref.at[others], dst_ref=in_ref.at[others], send_sem=send_sem, recv_sem=recv_sem,
        device_id=here, device_id_type=pl.DeviceIdType.MESH,
    )
    wait.wait_send()
    wait.wait_recv()


def index_tables(all_ref, table_ref):
    sources, chunks, lanes = all_ref.shape
    lane = lax.broadcasted_iota(jnp.int32, (sources, LANES), 1)
    buckets = NZ // BUCKET

    def below(s, low):
        less = jnp.where(all_ref[...] < s * (BUCKET * NX * (NY // 64)), 1.0, 0.0)
        return jnp.where(lane == s, jnp.sum(jnp.sum(less, axis=1), axis=1, keepdims=True), low)

    low = lax.fori_loop(1, buckets + 1, below, jnp.zeros((sources, LANES), jnp.float32)).astype(jnp.int32)
    high = pltpu.roll(low, LANES - 1, 1)
    first = low // GROUP
    counts = jnp.where(high > low, (high + GROUP - 1) // GROUP - first, 0)
    counts = jnp.where(lane < buckets, counts, 0).astype(jnp.float32)
    row = lax.broadcasted_iota(jnp.int32, (sources, sources), 0)
    before = jnp.where(row > lax.broadcasted_iota(jnp.int32, (sources, sources), 1), 1.0, 0.0)
    ahead = jnp.dot(before.astype(jnp.bfloat16), counts.astype(jnp.bfloat16), preferred_element_type=jnp.float32)
    source = lax.broadcasted_iota(jnp.int32, (sources, LANES), 0)
    total = jnp.broadcast_to(jnp.sum(counts, axis=0, keepdims=True), (8, LANES))
    table_ref[:sources, :] = first + source * (chunks * lanes // GROUP)
    table_ref[sources : 2 * sources, :] = ahead.astype(jnp.int32)
    table_ref[2 * sources :, :] = total.astype(jnp.int32)


def model_kernel(
    plan, vectors, table_ref, vals_ref, spots_ref, hx_ref, hz_ref, out_ref,
    index, index_sem, rows_src, merged, turned, left, right, total, plane, along_y
):
    sources, height, kept = vals_ref.shape
    slots = height // vectors
    buckets = NZ // BUCKET
    rows = kept // GROUP
    y_share = out_ref.shape[2] // NX
    lead = len(plan) * vectors

    @pl.when(pl.program_id(0) == 0)
    def scatter():
        fetch = pltpu.make_async_copy(table_ref, index, index_sem)
        fetch.start()
        tail = rows_src.shape[0] - sources * rows
        rows_src[pl.ds(sources * rows, tail), :] = jnp.full((tail, LANES), -1.0, jnp.float32)

        def unpack(src, carry):
            per_y = NY // 64
            spots = spots_ref[src]
            x = ((spots // per_y) % NX).astype(jnp.float32)
            code = (spots // (NX * per_y) + NZ * jnp.minimum(spots % per_y, 2)).astype(jnp.float32)
            for half in range(rows // LANES):
                parts = []
                for k in range(GROUP):
                    first = (half * GROUP + k) * LANES
                    parts.append(vals_ref[src, :, first : first + LANES].astype(jnp.float32))
                parts.append(x[half * GROUP : (half + 1) * GROUP, :])
                parts.append(code[half * GROUP : (half + 1) * GROUP, :])
                used = GROUP * height + 2 * GROUP
                parts.append(jnp.zeros((LANES - used, LANES), jnp.float32))
                place = pl.ds(pl.multiple_of(src * rows + half * LANES, LANES), LANES)
                rows_src[place, :] = jnp.concatenate(parts, axis=0).T
            return carry

        lax.fori_loop(0, sources, unpack, 0, unroll=4)
        fetch.wait()
        layer = lax.broadcasted_iota(jnp.int32, (BUCKET, LANES), 0).astype(jnp.float32)
        spot = lax.broadcasted_iota(jnp.int32, (NX, LANES), 0).astype(jnp.float32).astype(jnp.bfloat16)
        one, zero = jnp.bfloat16(1.0), jnp.bfloat16(0.0)

        def multiply():
            return lax.dot_general(left[...], right[...], (((1,), (1,)), ((), ())), preferred_element_type=jnp.float32)

        def build(s, t):
            here = layer + (s * BUCKET).astype(jnp.float32)
            for w in range(WIDE):
                turned[w] = merged[pl.ds(pl.multiple_of((t * WIDE + w) * LANES, LANES), LANES), :].T
            for w in range(WIDE):
                for k in range(GROUP):
                    columns = slice((w * GROUP + k) * LANES, (w * GROUP + k + 1) * LANES)
                    x = turned[w, GROUP * height + k : GROUP * height + k + 1, :]
                    code = turned[w, GROUP * height + GROUP + k : GROUP * height + GROUP + k + 1, :]
                    marks = [jnp.where(code == here + g * NZ, 1.0, 0.0) for g in range(3)]
                    marks = [jnp.concatenate([m, m], axis=0).astype(jnp.bfloat16) for m in marks]
                    lines = {}
                    for v in range(0, vectors, 2):
                        for slot in range(slots):
                            at = k * height + v * slots + slot
                            pair = [turned[w, i : i + 1, :] for i in (at, at + slots)]
                            pair = [jnp.broadcast_to(line, (BUCKET, LANES)) for line in pair]
                            lines[v, slot] = jnp.concatenate(pair, axis=0).astype(jnp.bfloat16)
                    pieces = []
                    for _, _, _, slot, group in plan:
                        pieces += [lines[v, slot] * marks[group] for v in range(0, vectors, 2)]
                    left[:, columns] = jnp.concatenate(pieces, axis=0)
                    right[:, columns] = jnp.where(x.astype(jnp.bfloat16) == spot, one, zero)

        def store(s, coef):
            place = pl.ds(pl.multiple_of(s * BUCKET, BUCKET), BUCKET)
            plane[:, place, :] = coef.reshape(lead, BUCKET, NX)

        def bucket_step(s, carry):
            def merge(i, carry):
                for u in range(MOVES):
                    src = i * MOVES + u
                    merged[pl.ds(index[sources + src, s], WINDOW), :] = rows_src[pl.ds(index[src, s], WINDOW), :]
                return carry

            lax.fori_loop(0, sources // MOVES, merge, 0)
            count = index[2 * sources, s]
            merged[pl.ds(count, WIDE * LANES), :] = jnp.full((WIDE * LANES, LANES), -1.0, jnp.float32)
            last = multiply()
            build(s, 0)
            store(jnp.maximum(s - 1, 0), total[...] + last)
            total[...] = jnp.zeros_like(total)

            def add(t, carry):
                product = multiply()
                build(s, t)
                total[...] += product
                return carry

            lax.fori_loop(1, (count + WIDE * LANES - 1) // (WIDE * LANES), add, 0)
            return carry

        lax.fori_loop(0, buckets, bucket_step, 0)
        store(buckets - 1, total[...] + multiply())

    me = lax.axis_index("tile") * lax.axis_size("col") + lax.axis_index("col")
    v = pl.program_id(0)
    fixed = REST * REST
    for begin in range(0, NZ, STRIP):
        strip = [plane[p * vectors + v, begin : begin + STRIP, :] for p in range(len(plan))]
        strip = jnp.concatenate(strip, axis=0).astype(jnp.bfloat16)
        along_x = jnp.dot(strip, hx_ref[...], preferred_element_type=jnp.float32)
        parts = [along_x[p * STRIP : (p + 1) * STRIP, :] for p in range(len(plan))]
        current = [parts[0] * (fixed * ROOT**LEVELS)]
        taken = 1
        for level in range(LEVELS):
            reach = 2 ** (LEVELS - level)
            held = max(1, y_share // reach)
            scale = fixed * ROOT ** (LEVELS - level)
            details = parts[taken : taken + held]
            taken += held
            if y_share >= reach:
                scaled = [d * scale for d in details]
                current = [e for c, d in zip(current, scaled) for e in (c + d, c - d)]
            else:
                current = [current[0] + details[0] * jnp.where(lax.rem(me * y_share, reach) < reach // 2, scale, -scale)]
        for y in range(y_share):
            along_y[y, begin : begin + STRIP, :] = current[y].astype(jnp.bfloat16)
    for y in range(y_share):
        out_ref[0, :, y * NX : (y + 1) * NX] = jnp.dot(hz_ref[...], along_y[y], preferred_element_type=jnp.float32)


def receive(plan, vectors, y_share, table, arrived, all_spots):
    sources, height, kept = arrived.shape
    rows = kept // GROUP
    hx = jnp.asarray(haar(NX), jnp.bfloat16)
    hz = jnp.asarray(haar(NZ).T, jnp.bfloat16)
    lead = len(plan) * vectors
    most = sources * (-(-CAP // GROUP) + 1)
    most = (-(-most // (WIDE * LANES)) + 1) * WIDE * LANES

    def whole(array):
        return pl.BlockSpec(array.shape, lambda v: (0,) * array.ndim)

    return pl.pallas_call(
        functools.partial(model_kernel, plan, vectors),
        out_shape=jax.ShapeDtypeStruct((vectors, NZ, y_share * NX), jnp.float32),
        grid=(vectors,),
        in_specs=[pl.BlockSpec(memory_space=pl.ANY), whole(arrived), whole(all_spots), whole(hx), whole(hz)],
        out_specs=pl.BlockSpec((1, NZ, y_share * NX), lambda v: (v, 0, 0)),
        scratch_shapes=[
            pltpu.SMEM(table.shape, jnp.int32),
            pltpu.SemaphoreType.DMA,
            pltpu.VMEM((sources * rows + WINDOW, LANES), jnp.float32),
            pltpu.VMEM((most, LANES), jnp.float32),
            pltpu.VMEM((WIDE, LANES, LANES), jnp.float32),
            pltpu.VMEM((lead * BUCKET, WIDE * GROUP * LANES), jnp.bfloat16),
            pltpu.VMEM((NX, WIDE * GROUP * LANES), jnp.bfloat16),
            pltpu.VMEM((lead * BUCKET, NX), jnp.float32),
            pltpu.VMEM((lead, NZ, NX), jnp.float32),
            pltpu.VMEM((y_share, NZ, NX), jnp.bfloat16),
        ],
        compiler_params=pltpu.CompilerParams(vmem_limit_bytes=60 * 2**20),
    )(table, arrived, all_spots, hx, hz)


def on_device(readings, sensitivity, kept_tile, kept_row, kept_slab, kept_block):
    devices = lax.axis_size(AXES)
    columns = lax.axis_size("col")
    kept, width, _ = sensitivity.shape
    vectors = readings.shape[1]
    per_y = NY // width
    layers = NZ // devices
    y_share = NY // devices
    plan, slots = y_plan(y_share, width)
    chunks = kept // LANES
    square = jax.ShapeDtypeStruct((chunks, LANES), jnp.int32)
    vmem = pl.BlockSpec(memory_space=pltpu.VMEM)
    group, place, spots = pl.pallas_call(
        functools.partial(gather_kernel, layers * NX * per_y),
        out_shape=(jax.ShapeDtypeStruct((columns, *readings.shape), readings.dtype), square, square),
        in_specs=[vmem] * 3,
        out_specs=(vmem, vmem, vmem),
        scratch_shapes=[pltpu.SemaphoreType.DMA, pltpu.SemaphoreType.DMA],
        compiler_params=pltpu.CompilerParams(collective_id=0, has_side_effects=True),
    )(readings, kept_slab.reshape(chunks, LANES), kept_block.reshape(chunks, LANES))
    spread = jnp.asarray(spread_matrix(plan, slots, devices, vectors, width, y_share), jnp.bfloat16)
    table_spots = columns * readings.shape[0] * (readings.shape[2] // width)
    spots_pad = -(-table_spots // LANES) * LANES
    outgoing = pl.pallas_call(
        products_kernel,
        out_shape=jax.ShapeDtypeStruct((devices * vectors * slots, kept), jnp.bfloat16),
        grid=(chunks,),
        in_specs=[
            pl.BlockSpec((1, LANES), lambda i: (0, i)),
            pl.BlockSpec((1, LANES), lambda i: (0, i)),
            pl.BlockSpec(group.shape, lambda i: (0, 0, 0, 0)),
            pl.BlockSpec((chunks, LANES), lambda i: (0, 0)),
            pl.BlockSpec((chunks, LANES), lambda i: (0, 0)),
            pl.BlockSpec(spread.shape, lambda i: (0, 0)),
            pl.BlockSpec((width, width, LANES), lambda i: (0, 0, i)),
        ],
        out_specs=pl.BlockSpec((devices * vectors * slots, kept), lambda i: (0, 0)),
        scratch_shapes=[
            pltpu.VMEM((vectors * width, spots_pad), jnp.bfloat16),
            pltpu.VMEM((vectors * width, LANES), jnp.float32),
            pltpu.VMEM((vectors * width, kept), jnp.bfloat16),
        ],
        compiler_params=pltpu.CompilerParams(vmem_limit_bytes=48 * 2**20),
    )(kept_tile[None, :], kept_row[None, :], group, place, spots, spread, sensitivity.transpose(1, 2, 0))
    outgoing = outgoing.reshape(devices, vectors * slots, kept)
    arrived, all_spots, table = pl.pallas_call(
        functools.partial(exchange_kernel, columns),
        out_shape=(
            jax.ShapeDtypeStruct(outgoing.shape, outgoing.dtype),
            jax.ShapeDtypeStruct((devices, chunks, LANES), jnp.int32),
            jax.ShapeDtypeStruct((2 * devices + 8, LANES), jnp.int32),
        ),
        in_specs=[vmem] * 2,
        out_specs=(vmem, vmem, vmem),
        scratch_shapes=[pltpu.SemaphoreType.DMA] * 5,
        compiler_params=pltpu.CompilerParams(
            collective_id=1, has_side_effects=True, vmem_limit_bytes=48 * 2**20
        ),
    )(outgoing, spots)
    return receive(plan, vectors, y_share, table, arrived, all_spots)


def solution(mesh):
    return jax.shard_map(
        on_device,
        mesh=mesh,
        in_specs=(
            P(AXES, None, None),
            P(AXES, None, None),
            P(AXES),
            P(AXES),
            P(AXES, None),
            P(AXES),
        ),
        out_specs=P(None, None, AXES),
        check_vma=False,
    )
```

```python
import functools

import jax
import jax.numpy as jnp
import numpy as np
from jax import lax
from jax.experimental import pallas as pl
from jax.experimental.pallas import tpu as pltpu
from jax.sharding import PartitionSpec as P

NX = 256
NY = 256
NZ = 256
LEVELS = 3
ROOT = 0.7071067811865476
LANES = 128
BUCKET = 8
MOVES = 32
PAIR = 4
STRIP = 32
PACK = 2
GROUP = 4
CAP = 80
WINDOW = 24
STEPS = (239 / 256, 169 / 256, 239 / 512, 169 / 512)
REST = 256 / 239
AXES = ("tile", "col")


def segments(length):
    coarse = length // 2**LEVELS
    found = [(0, coarse, 2**LEVELS)]
    for level in range(LEVELS):
        found.append((coarse * 2**level, coarse * 2**level, 2 ** (LEVELS - level)))
    return found


def haar(length):
    matrix = np.zeros((length, length), np.float32)
    for number, (start, count, reach) in enumerate(segments(length)):
        for i in range(count):
            half = reach // 2 if number else reach
            matrix[start + i, i * reach : i * reach + half] = STEPS[reach.bit_length() - 1]
            matrix[start + i, i * reach + half : (i + 1) * reach] = -STEPS[reach.bit_length() - 1]
    return matrix


def y_plan(y_share, width):
    rows = []
    used = {}
    for start, count, reach in segments(NY):
        group = min(start // width, 2)
        for i in range(max(1, y_share // reach)):
            slot = used.get(group, 0)
            used[group] = slot + 1
            rows.append((start, reach, i, slot, group))
    return rows, max(used.values())


def spread_matrix(plan, slots, devices, vectors, width, y_share):
    per_y = NY // width
    matrix = np.zeros((devices, vectors, slots, per_y, vectors, width), np.float32)
    for start, reach, i, slot, _ in plan:
        for owner in range(devices):
            y = start + owner * y_share // reach + i
            for v in range(vectors):
                matrix[owner, v, slot, y // width, v, y % width] = 1.0
    return matrix.reshape(devices * vectors * slots, per_y * vectors * width)


def gather_kernel(lift, mine_ref, slab_ref, block_ref, group_ref, place_ref, sorted_ref, send_sem, recv_sem):
    columns = group_ref.shape[0]
    tile, col = lax.axis_index("tile"), lax.axis_index("col")
    barrier = pltpu.get_barrier_semaphore()

    def greet(i, carry):
        other = lax.rem(col + i, columns)
        pl.semaphore_signal(barrier, inc=1, device_id=(tile, other), device_id_type=pl.DeviceIdType.MESH)
        return carry

    lax.fori_loop(1, columns, greet, 0)
    spot = slab_ref[...] * lift + block_ref[...]
    chunks, lanes = spot.shape
    kept = chunks * lanes
    number = lax.broadcasted_iota(jnp.int32, (chunks, lanes), 0) * lanes + lax.broadcasted_iota(jnp.int32, (chunks, lanes), 1)
    key = ((spot // (BUCKET * NX * (NY // 64))) * kept + number).astype(jnp.float32)
    spot = spot.astype(jnp.float32)
    pl.semaphore_wait(barrier, columns - 1)

    def send(i, carry):
        other = lax.rem(col + i, columns)
        pltpu.make_async_remote_copy(
            src_ref=mine_ref, dst_ref=group_ref.at[col], send_sem=send_sem, recv_sem=recv_sem,
            device_id=(tile, other), device_id_type=pl.DeviceIdType.MESH,
        ).start()
        return carry

    lax.fori_loop(1, columns, send, 0)

    def upright(rows):
        return [jnp.broadcast_to(rows[c : c + 1, :], (lanes, lanes)).T for c in range(chunks)]

    key_up, spot_up = upright(key), upright(spot)
    ranks = []
    for c in range(chunks):
        line = key[c : c + 1, :]
        total = jnp.zeros((lanes, lanes), jnp.float32)
        for d in range(chunks):
            total = total + jnp.where(key_up[d] < line, 1.0, 0.0)
        ranks.append(jnp.sum(total, axis=0, keepdims=True))
    rank = jnp.concatenate(ranks, axis=0).astype(jnp.int32)
    wide = GROUP * lanes
    place = (rank // wide) * wide + (rank % GROUP) * lanes + (rank // GROUP) % lanes
    place_ref[...] = place
    place_up = upright(place.astype(jnp.float32))
    goal = number.astype(jnp.float32)
    spots = []
    for c in range(chunks):
        line = goal[c : c + 1, :]
        total = jnp.zeros((lanes, lanes), jnp.float32)
        for d in range(chunks):
            total = total + jnp.where(place_up[d] == line, spot_up[d], 0.0)
        spots.append(jnp.sum(total, axis=0, keepdims=True))
    sorted_ref[...] = jnp.concatenate(spots, axis=0).astype(jnp.int32)
    group_ref[col] = mine_ref[...]
    others = group_ref.at[pl.ds(0, columns - 1)]
    wait = pltpu.make_async_remote_copy(
        src_ref=others, dst_ref=others, send_sem=send_sem, recv_sem=recv_sem,
        device_id=(tile, col), device_id_type=pl.DeviceIdType.MESH,
    )
    wait.wait_send()
    wait.wait_recv()


def products_kernel(tiles_ref, rows_ref, group_ref, place_ref, sorted_ref, spread_ref, sens_ref, out_ref, table, picked, made):
    width, columns, lanes = sens_ref.shape
    sources, share, vectors, readings = group_ref.shape
    tiles = sources * share
    row_blocks = readings // width
    step = pl.program_id(0)

    @pl.when(step == 0)
    def make_table():
        lines = [group_ref[i, j].astype(jnp.float32) for i in range(sources) for j in range(share)]
        by_vector = [jnp.concatenate([line[v : v + 1, :] for line in lines], axis=0) for v in range(vectors)]
        rows = []
        for b in range(row_blocks):
            rows.append(jnp.concatenate([a[:, b * width : (b + 1) * width] for a in by_vector], axis=1))
        if row_blocks * tiles < table.shape[1]:
            rows.append(jnp.zeros((table.shape[1] - row_blocks * tiles, vectors * width), jnp.float32))
        table[...] = jnp.concatenate(rows, axis=0).T.astype(jnp.bfloat16)

    spots = lax.broadcasted_iota(jnp.int32, (table.shape[1], lanes), 0)
    chosen = jnp.where(rows_ref[...] * tiles + tiles_ref[...] == spots, 1.0, 0.0).astype(jnp.bfloat16)
    picked[...] = jnp.dot(table[...], chosen, preferred_element_type=jnp.float32)
    sums = [jnp.zeros((columns, lanes), jnp.float32) for _ in range(vectors)]
    for r in range(width):
        sens = sens_ref[r].astype(jnp.float32)
        for v in range(vectors):
            sums[v] = sums[v] + sens * picked[v * width + r : v * width + r + 1, :]
    here = pl.ds(pl.multiple_of(step * lanes, lanes), lanes)
    for v in range(vectors):
        made[v * columns : (v + 1) * columns, here] = sums[v].astype(jnp.bfloat16)

    @pl.when(step == pl.num_programs(0) - 1)
    def send_order():
        chunks = place_ref.shape[0]
        per_y = NY // width
        goal = lax.broadcasted_iota(jnp.int32, (PACK * lanes, lanes), 0)
        for c in range(0, chunks, PACK):
            moved = [jnp.where(place_ref[d : d + 1, :] - c * lanes == goal, 1.0, 0.0) for d in range(chunks)]
            moved = jnp.concatenate(moved, axis=1).astype(jnp.bfloat16)
            ordered = lax.dot_general(made[...], moved, (((1,), (1,)), ((), ())), preferred_element_type=jnp.float32)
            in_y = jnp.concatenate([sorted_ref[d : d + 1, :] for d in range(c, c + PACK)], axis=1) % per_y
            masked = [jnp.where(in_y == b, ordered, 0.0).astype(jnp.bfloat16) for b in range(per_y)]
            masked = jnp.concatenate(masked, axis=0)
            sent = jnp.dot(spread_ref[...], masked, preferred_element_type=jnp.float32)
            out_ref[:, c * lanes : (c + PACK) * lanes] = sent.astype(jnp.bfloat16)


def exchange_kernel(columns, out_ref, spots_ref, in_ref, all_ref, table_ref, send_sem, recv_sem, own_sem, spots_send, spots_recv):
    devices = out_ref.shape[0]
    me = lax.axis_index("tile") * columns + lax.axis_index("col")
    own = pltpu.make_async_copy(out_ref.at[me], in_ref.at[me], own_sem)
    own.start()
    barrier = pltpu.get_barrier_semaphore()

    def place(i):
        other = lax.rem(me + i, devices)
        return other, (other // columns, lax.rem(other, columns))

    def greet(i, carry):
        pl.semaphore_signal(barrier, inc=1, device_id=place(i)[1], device_id_type=pl.DeviceIdType.MESH)
        return carry

    lax.fori_loop(1, devices, greet, 0)
    all_ref[me] = spots_ref[...]
    pl.semaphore_wait(barrier, devices - 1)

    def send_spots(i, carry):
        pltpu.make_async_remote_copy(
            src_ref=spots_ref, dst_ref=all_ref.at[me], send_sem=spots_send, recv_sem=spots_recv,
            device_id=place(i)[1], device_id_type=pl.DeviceIdType.MESH,
        ).start()
        return carry

    lax.fori_loop(1, devices, send_spots, 0)

    def send(i, carry):
        other, where = place(i)
        pltpu.make_async_remote_copy(
            src_ref=out_ref.at[other], dst_ref=in_ref.at[me], send_sem=send_sem, recv_sem=recv_sem,
            device_id=where, device_id_type=pl.DeviceIdType.MESH,
        ).start()
        return carry

    lax.fori_loop(1, devices, send, 0)
    others = pl.ds(0, devices - 1)
    here = (lax.axis_index("tile"), lax.axis_index("col"))
    wait = pltpu.make_async_remote_copy(
        src_ref=all_ref.at[others], dst_ref=all_ref.at[others], send_sem=spots_send, recv_sem=spots_recv,
        device_id=here, device_id_type=pl.DeviceIdType.MESH,
    )
    wait.wait_send()
    wait.wait_recv()
    index_tables(all_ref, table_ref)
    own.wait()
    wait = pltpu.make_async_remote_copy(
        src_ref=out_ref.at[others], dst_ref=in_ref.at[others], send_sem=send_sem, recv_sem=recv_sem,
        device_id=here, device_id_type=pl.DeviceIdType.MESH,
    )
    wait.wait_send()
    wait.wait_recv()


def index_tables(all_ref, table_ref):
    sources, chunks, lanes = all_ref.shape
    lane = lax.broadcasted_iota(jnp.int32, (sources, LANES), 1)
    buckets = NZ // BUCKET

    def below(s, low):
        less = jnp.where(all_ref[...] < s * (BUCKET * NX * (NY // 64)), 1.0, 0.0)
        return jnp.where(lane == s, jnp.sum(jnp.sum(less, axis=1), axis=1, keepdims=True), low)

    low = lax.fori_loop(1, buckets + 1, below, jnp.zeros((sources, LANES), jnp.float32)).astype(jnp.int32)
    high = pltpu.roll(low, LANES - 1, 1)
    first = low // GROUP
    counts = jnp.where(high > low, (high + GROUP - 1) // GROUP - first, 0)
    counts = jnp.where(lane < buckets, counts, 0).astype(jnp.float32)
    row = lax.broadcasted_iota(jnp.int32, (sources, sources), 0)
    before = jnp.where(row > lax.broadcasted_iota(jnp.int32, (sources, sources), 1), 1.0, 0.0)
    ahead = jnp.dot(before.astype(jnp.bfloat16), counts.astype(jnp.bfloat16), preferred_element_type=jnp.float32)
    source = lax.broadcasted_iota(jnp.int32, (sources, LANES), 0)
    total = jnp.broadcast_to(jnp.sum(counts, axis=0, keepdims=True), (8, LANES))
    table_ref[:sources, :] = first + source * (chunks * lanes // GROUP)
    table_ref[sources : 2 * sources, :] = ahead.astype(jnp.int32)
    table_ref[2 * sources :, :] = total.astype(jnp.int32)


def model_kernel(
    plan, vectors, table_ref, vals_ref, spots_ref, hx_ref, hz_ref, out_ref,
    index, index_sem, owner, rows_src, merged, left, right, plane, along_y
):
    sources, height, kept = vals_ref.shape
    slots = height // vectors
    buckets = NZ // BUCKET
    rows = kept // GROUP
    y_share = out_ref.shape[2] // NX
    lead = len(plan) * vectors

    row = lax.broadcasted_iota(jnp.int32, (LANES, LANES), 0)
    eye = jnp.where(row == lax.broadcasted_iota(jnp.int32, (LANES, LANES), 1), 1.0, 0.0).astype(jnp.bfloat16)

    def turned(block):
        return lax.dot_general(eye, block, (((1,), (1,)), ((), ())), preferred_element_type=jnp.float32)

    @pl.when(pl.program_id(0) == 0)
    def scatter():
        fetch = pltpu.make_async_copy(table_ref, index, index_sem)
        fetch.start()
        tail = rows_src.shape[0] - sources * rows
        rows_src[pl.ds(sources * rows, tail), :] = jnp.full((tail, LANES), -1.0, jnp.float32)

        def unpack(src, carry):
            per_y = NY // 64
            spots = spots_ref[src]
            marks = [(spots // per_y) % NX, spots // (NX * per_y), jnp.minimum(spots % per_y, 2)]
            marks = [m.astype(jnp.float32) for m in marks]
            for half in range(rows // LANES):
                first = half * GROUP * LANES
                parts = [vals_ref[src, :, first + k * LANES : first + (k + 1) * LANES] for k in range(GROUP)]
                used = GROUP * height + len(marks) * GROUP
                lines = [m[half * GROUP : (half + 1) * GROUP, :] for m in marks]
                lines.append(jnp.zeros((LANES - used, LANES), jnp.float32))
                parts.append(jnp.concatenate(lines, axis=0).astype(jnp.bfloat16))
                place = pl.ds(pl.multiple_of(src * rows + half * LANES, LANES), LANES)
                rows_src[place, :] = turned(jnp.concatenate(parts, axis=0))
            return carry

        lax.fori_loop(0, sources, unpack, 0, unroll=4)
        fetch.wait()
        layer = lax.broadcasted_iota(jnp.int32, (BUCKET, LANES), 0).astype(jnp.float32)
        spot = lax.broadcasted_iota(jnp.int32, (NX, LANES), 0).astype(jnp.float32).astype(jnp.bfloat16)
        one, zero = jnp.bfloat16(1.0), jnp.bfloat16(0.0)

        def bucket_step(s, base):
            def merge(i, carry):
                for u in range(MOVES):
                    src = i * MOVES + u
                    to = pl.ds(base * LANES + index[sources + src, s], WINDOW)
                    merged[to, :] = rows_src[pl.ds(index[src, s], WINDOW), :]
                return carry

            lax.fori_loop(0, sources // MOVES, merge, 0)
            count = index[2 * sources, s]
            merged[pl.ds(base * LANES + count, LANES), :] = jnp.full((LANES, LANES), -1.0, jnp.float32)
            tiles = (count + LANES - 1) // LANES

            def name(t, carry):
                owner[base + t] = s
                return carry

            lax.fori_loop(0, tiles, name, 0)
            return base + tiles

        tiles = lax.fori_loop(0, buckets, bucket_step, 0)
        for extra in range(PAIR):
            owner[tiles + extra] = 0
            place = pl.ds(pl.multiple_of((tiles + extra) * LANES, LANES), LANES)
            merged[place, :] = jnp.full((LANES, LANES), -1.0, jnp.float32)
        steps = (tiles + PAIR - 1) // PAIR

        def turn(first):
            block = [merged[pl.ds(first + u * LANES, LANES), :].T for u in range(PAIR)]
            for u in range(PAIR):
                merged[pl.ds(first + u * LANES, LANES), :] = block[u]

        turn(0)
        plane[...] = jnp.zeros_like(plane)
        left[...] = jnp.zeros_like(left)
        right[...] = jnp.zeros_like(right)

        def build(u, t, first):
            here = layer + (owner[t] * BUCKET).astype(jnp.float32)
            for k in range(GROUP):
                columns = slice(k * LANES, (k + 1) * LANES)

                def line(row):
                    return merged[pl.ds(first + row, 1), :]

                x = line(GROUP * height + k)
                code = line(GROUP * height + GROUP + k) + NZ * line(GROUP * height + 2 * GROUP + k)
                marks = [jnp.where(code == here + g * NZ, 1.0, 0.0) for g in range(3)]
                marks = [jnp.concatenate([m, m], axis=0).astype(jnp.bfloat16) for m in marks]
                lines = {}
                for v in range(0, vectors, 2):
                    for slot in range(slots):
                        at = k * height + v * slots + slot
                        pair = [jnp.broadcast_to(line(i), (BUCKET, LANES)) for i in (at, at + slots)]
                        lines[v, slot] = jnp.concatenate(pair, axis=0).astype(jnp.bfloat16)
                pieces = []
                for _, _, _, slot, group in plan:
                    pieces += [lines[v, slot] * marks[group] for v in range(0, vectors, 2)]
                left[u, :, columns] = jnp.concatenate(pieces, axis=0)
                right[u, :, columns] = jnp.where(x.astype(jnp.bfloat16) == spot, one, zero)

        def tile_step(i, carry):
            first = pl.multiple_of(i * PAIR * LANES, LANES)
            turn(first + PAIR * LANES)
            products = []
            for u in range(PAIR):
                product = lax.dot_general(left[u], right[u], (((1,), (1,)), ((), ())), preferred_element_type=jnp.float32)
                products.append(product.reshape(lead, BUCKET, NX))
            for u in range(PAIR):
                build(u, i * PAIR + u, first + u * LANES)
            for u in range(PAIR):
                s = owner[jnp.maximum((i - 1) * PAIR + u, 0)]
                place = pl.ds(pl.multiple_of(s * BUCKET, BUCKET), BUCKET)
                plane[:, place, :] += products[u]
            return carry

        lax.fori_loop(0, steps + 1, tile_step, 0)

    me = lax.axis_index("tile") * lax.axis_size("col") + lax.axis_index("col")
    v = pl.program_id(0)
    fixed = REST * REST
    for begin in range(0, NZ, STRIP):
        strip = [plane[p * vectors + v, begin : begin + STRIP, :] for p in range(len(plan))]
        strip = jnp.concatenate(strip, axis=0).astype(jnp.bfloat16)
        along_x = jnp.dot(strip, hx_ref[...], preferred_element_type=jnp.float32)
        parts = [along_x[p * STRIP : (p + 1) * STRIP, :] for p in range(len(plan))]
        current = [parts[0] * (fixed * ROOT**LEVELS)]
        taken = 1
        for level in range(LEVELS):
            reach = 2 ** (LEVELS - level)
            held = max(1, y_share // reach)
            scale = fixed * ROOT ** (LEVELS - level)
            details = parts[taken : taken + held]
            taken += held
            if y_share >= reach:
                scaled = [d * scale for d in details]
                current = [e for c, d in zip(current, scaled) for e in (c + d, c - d)]
            else:
                current = [current[0] + details[0] * jnp.where(lax.rem(me * y_share, reach) < reach // 2, scale, -scale)]
        for y in range(y_share):
            along_y[y, begin : begin + STRIP, :] = current[y].astype(jnp.bfloat16)
    for y in range(y_share):
        out_ref[0, :, y * NX : (y + 1) * NX] = jnp.dot(hz_ref[...], along_y[y], preferred_element_type=jnp.float32)


def receive(plan, vectors, y_share, table, arrived, all_spots):
    sources, height, kept = arrived.shape
    rows = kept // GROUP
    hx = jnp.asarray(haar(NX), jnp.bfloat16)
    hz = jnp.asarray(haar(NZ).T, jnp.bfloat16)
    lead = len(plan) * vectors
    most = sources * (rows + NZ // BUCKET)
    most_tiles = most // LANES + NZ // BUCKET + 3 * PAIR

    def whole(array):
        return pl.BlockSpec(array.shape, lambda v: (0,) * array.ndim)

    return pl.pallas_call(
        functools.partial(model_kernel, plan, vectors),
        out_shape=jax.ShapeDtypeStruct((vectors, NZ, y_share * NX), jnp.float32),
        grid=(vectors,),
        in_specs=[pl.BlockSpec(memory_space=pl.ANY), whole(arrived), whole(all_spots), whole(hx), whole(hz)],
        out_specs=pl.BlockSpec((1, NZ, y_share * NX), lambda v: (v, 0, 0)),
        scratch_shapes=[
            pltpu.SMEM(table.shape, jnp.int32),
            pltpu.SemaphoreType.DMA,
            pltpu.SMEM((most_tiles,), jnp.int32),
            pltpu.VMEM((sources * rows + WINDOW, LANES), jnp.float32),
            pltpu.VMEM((most_tiles * LANES, LANES), jnp.float32),
            pltpu.VMEM((PAIR, lead * BUCKET, GROUP * LANES), jnp.bfloat16),
            pltpu.VMEM((PAIR, NX, GROUP * LANES), jnp.bfloat16),
            pltpu.VMEM((lead, NZ, NX), jnp.float32),
            pltpu.VMEM((y_share, NZ, NX), jnp.bfloat16),
        ],
        compiler_params=pltpu.CompilerParams(vmem_limit_bytes=60 * 2**20),
    )(table, arrived, all_spots, hx, hz)


def on_device(readings, sensitivity, kept_tile, kept_row, kept_slab, kept_block):
    devices = lax.axis_size(AXES)
    columns = lax.axis_size("col")
    kept, width, _ = sensitivity.shape
    vectors = readings.shape[1]
    per_y = NY // width
    layers = NZ // devices
    y_share = NY // devices
    plan, slots = y_plan(y_share, width)
    chunks = kept // LANES
    square = jax.ShapeDtypeStruct((chunks, LANES), jnp.int32)
    vmem = pl.BlockSpec(memory_space=pltpu.VMEM)
    group, place, spots = pl.pallas_call(
        functools.partial(gather_kernel, layers * NX * per_y),
        out_shape=(jax.ShapeDtypeStruct((columns, *readings.shape), readings.dtype), square, square),
        in_specs=[vmem] * 3,
        out_specs=(vmem, vmem, vmem),
        scratch_shapes=[pltpu.SemaphoreType.DMA, pltpu.SemaphoreType.DMA],
        compiler_params=pltpu.CompilerParams(
            collective_id=0, has_side_effects=True, vmem_limit_bytes=60 * 2**20
        ),
    )(readings, kept_slab.reshape(chunks, LANES), kept_block.reshape(chunks, LANES))
    spread = jnp.asarray(spread_matrix(plan, slots, devices, vectors, width, y_share), jnp.bfloat16)
    table_spots = columns * readings.shape[0] * (readings.shape[2] // width)
    spots_pad = -(-table_spots // LANES) * LANES
    outgoing = pl.pallas_call(
        products_kernel,
        out_shape=jax.ShapeDtypeStruct((devices * vectors * slots, kept), jnp.bfloat16),
        grid=(chunks,),
        in_specs=[
            pl.BlockSpec((1, LANES), lambda i: (0, i)),
            pl.BlockSpec((1, LANES), lambda i: (0, i)),
            pl.BlockSpec(group.shape, lambda i: (0, 0, 0, 0)),
            pl.BlockSpec((chunks, LANES), lambda i: (0, 0)),
            pl.BlockSpec((chunks, LANES), lambda i: (0, 0)),
            pl.BlockSpec(spread.shape, lambda i: (0, 0)),
            pl.BlockSpec((width, width, LANES), lambda i: (0, 0, i)),
        ],
        out_specs=pl.BlockSpec((devices * vectors * slots, kept), lambda i: (0, 0)),
        scratch_shapes=[
            pltpu.VMEM((vectors * width, spots_pad), jnp.bfloat16),
            pltpu.VMEM((vectors * width, LANES), jnp.float32),
            pltpu.VMEM((vectors * width, kept), jnp.bfloat16),
        ],
        compiler_params=pltpu.CompilerParams(vmem_limit_bytes=60 * 2**20),
    )(kept_tile[None, :], kept_row[None, :], group, place, spots, spread, sensitivity.transpose(1, 2, 0))
    outgoing = outgoing.reshape(devices, vectors * slots, kept)
    arrived, all_spots, table = pl.pallas_call(
        functools.partial(exchange_kernel, columns),
        out_shape=(
            jax.ShapeDtypeStruct(outgoing.shape, outgoing.dtype),
            jax.ShapeDtypeStruct((devices, chunks, LANES), jnp.int32),
            jax.ShapeDtypeStruct((2 * devices + 8, LANES), jnp.int32),
        ),
        in_specs=[pl.BlockSpec(memory_space=pl.ANY), vmem],
        out_specs=(pl.BlockSpec(memory_space=pl.ANY), vmem, vmem),
        scratch_shapes=[pltpu.SemaphoreType.DMA] * 5,
        compiler_params=pltpu.CompilerParams(
            collective_id=1, has_side_effects=True, vmem_limit_bytes=60 * 2**20
        ),
    )(outgoing, spots)
    return receive(plan, vectors, y_share, table, arrived, all_spots)


def solution(mesh):
    return jax.shard_map(
        on_device,
        mesh=mesh,
        in_specs=(
            P(AXES, None, None),
            P(AXES, None, None),
            P(AXES),
            P(AXES),
            P(AXES, None),
            P(AXES),
        ),
        out_specs=P(None, None, AXES),
        check_vma=False,
    )
```

```python
import functools

import jax
import jax.numpy as jnp
import numpy as np
from jax import lax
from jax.experimental import pallas as pl
from jax.experimental.pallas import tpu as pltpu
from jax.sharding import PartitionSpec as P

NX = 256
NY = 256
NZ = 256
LEVELS = 3
ROOT = 0.7071067811865476
LANES = 128
BUCKET = 8
MOVES = 32
PAIR = 4
STRIP = 32
HALVES = 2
GROUP = 4
CAP = 80
WINDOW = 24
STEPS = (239 / 256, 169 / 256, 239 / 512, 169 / 512)
REST = 256 / 239
AXES = ("tile", "col")


def segments(length):
    coarse = length // 2**LEVELS
    found = [(0, coarse, 2**LEVELS)]
    for level in range(LEVELS):
        found.append((coarse * 2**level, coarse * 2**level, 2 ** (LEVELS - level)))
    return found


def haar(length):
    matrix = np.zeros((length, length), np.float32)
    for number, (start, count, reach) in enumerate(segments(length)):
        for i in range(count):
            half = reach // 2 if number else reach
            matrix[start + i, i * reach : i * reach + half] = STEPS[reach.bit_length() - 1]
            matrix[start + i, i * reach + half : (i + 1) * reach] = -STEPS[reach.bit_length() - 1]
    return matrix


def y_plan(y_share, width):
    rows = []
    used = {}
    for start, count, reach in segments(NY):
        group = min(start // width, 2)
        for i in range(max(1, y_share // reach)):
            slot = used.get(group, 0)
            used[group] = slot + 1
            rows.append((start, reach, i, slot, group))
    return rows, max(used.values())


def fold(vectors, slots):
    height = vectors // HALVES * slots
    stack = 16 // height
    return height, stack, GROUP // stack


def row_of(k, v, slot, vectors, slots):
    height, stack, beside = fold(vectors, slots)
    share = vectors // HALVES
    return ((v // share) * beside + k % beside) * 16 + k // beside * height + v % share * slots + slot


def spread_matrix(plan, slots, devices, vectors, width, y_share):
    per_y = NY // width
    height, stack, _ = fold(vectors, slots)
    share = vectors // HALVES
    matrix = np.zeros((devices, stack, share, slots, stack, per_y, share, width), np.float32)
    for start, reach, i, slot, _ in plan:
        for owner in range(devices):
            y = start + owner * y_share // reach + i
            for v in range(share):
                for k in range(stack):
                    matrix[owner, k, v, slot, k, y // width, v, y % width] = 1.0
    return matrix.reshape(devices * 16, stack * per_y * share * width)


def front_kernel(
    lift, slots, readings_ref, slab_ref, block_ref, tiles_ref, rows_ref, spread_ref, sens_ref,
    first_ref, second_ref, spots_ref, index_ref,
    group, place, everyone, table, picked, made, moved, outgoing, group_sems, spots_sems, value_sems, own_sems,
):
    width, _, lanes = sens_ref.shape
    columns, _, vectors, readings = group.shape
    devices, chunks, _ = everyone.shape
    share = vectors // HALVES
    _, stack, beside = fold(vectors, slots)
    per_y = NY // width
    half, step = pl.program_id(0), pl.program_id(1)
    tile, col = lax.axis_index("tile"), lax.axis_index("col")
    me = tile * columns + col
    MESH = pl.DeviceIdType.MESH

    def other(i):
        number = lax.rem(me + i, devices)
        return number, (number // columns, lax.rem(number, columns))

    def wait_all(ref, count, sems):
        part = ref.at[pl.ds(0, count)]
        copy = pltpu.make_async_remote_copy(
            src_ref=part, dst_ref=part, send_sem=sems.at[0], recv_sem=sems.at[1], device_id=(tile, col), device_id_type=MESH
        )
        copy.wait_send()
        copy.wait_recv()

    @pl.when((half == 0) & (step == 0))
    def begin():
        barrier = pltpu.get_barrier_semaphore()

        def greet(i, carry):
            pl.semaphore_signal(barrier, inc=1, device_id=other(i)[1], device_id_type=MESH)
            return carry

        lax.fori_loop(1, devices, greet, 0)
        group[col] = readings_ref[...]
        pl.semaphore_wait(barrier, devices - 1)

        def send_readings(i, carry):
            pltpu.make_async_remote_copy(
                src_ref=group.at[col], dst_ref=group.at[col], send_sem=group_sems.at[0], recv_sem=group_sems.at[1],
                device_id=(tile, lax.rem(col + i, columns)), device_id_type=MESH,
            ).start()
            return carry

        lax.fori_loop(1, columns, send_readings, 0)
        sort_blocks(lift, me, slab_ref, block_ref, place, everyone)

        def send_spots(i, carry):
            pltpu.make_async_remote_copy(
                src_ref=everyone.at[me], dst_ref=everyone.at[me], send_sem=spots_sems.at[0], recv_sem=spots_sems.at[1],
                device_id=other(i)[1], device_id_type=MESH,
            ).start()
            return carry

        lax.fori_loop(1, devices, send_spots, 0)
        wait_all(group, columns - 1, group_sems)
        make_table(group, width, table)

    tiles = group.shape[0] * group.shape[1]
    spots = lax.broadcasted_iota(jnp.int32, (table.shape[1], lanes), 0)
    chosen = jnp.where(rows_ref[...] * tiles + tiles_ref[...] == spots, 1.0, 0.0).astype(jnp.bfloat16)
    mine = table[pl.ds(pl.multiple_of(half * (share * width), share * width), share * width), :]
    picked[...] = jnp.dot(mine, chosen, preferred_element_type=jnp.float32)
    sums = [jnp.zeros((width, lanes), jnp.float32) for _ in range(share)]
    for r in range(width):
        sens = sens_ref[r].astype(jnp.float32)
        for v in range(share):
            sums[v] = sums[v] + sens * picked[v * width + r : v * width + r + 1, :]
    here = pl.ds(pl.multiple_of(step * lanes, lanes), lanes)
    for v in range(share):
        made[v * width : (v + 1) * width, here] = sums[v].astype(jnp.bfloat16)

    @pl.when(half == 0)
    def order():
        goal = lax.broadcasted_iota(jnp.int32, (lanes, lanes), 0) + step * lanes
        hits = [jnp.where(place[d : d + 1, :] == goal, 1.0, 0.0) for d in range(chunks)]
        moved[here, :] = jnp.concatenate(hits, axis=1).astype(jnp.bfloat16)

    @pl.when(step == chunks - 1)
    def send_half():
        in_y = everyone[me] % per_y
        for part in range(chunks // GROUP):
            for k in range(beside):
                picks = [part * GROUP + up * beside + k for up in range(stack)]
                rows = jnp.concatenate([moved[p * lanes : (p + 1) * lanes, :] for p in picks], axis=0)
                ordered = lax.dot_general(made[...], rows, (((1,), (1,)), ((), ())), preferred_element_type=jnp.float32)
                masked = []
                for up, p in enumerate(picks):
                    values = ordered[:, up * lanes : (up + 1) * lanes]
                    masked += [jnp.where(in_y[p : p + 1, :] == b, values, 0.0) for b in range(per_y)]
                masked = jnp.concatenate(masked, axis=0).astype(jnp.bfloat16)
                sent = jnp.dot(spread_ref[...], masked, preferred_element_type=jnp.float32)
                at = (part * beside + k) * lanes
                outgoing[half, :, :, at : at + lanes] = sent.reshape(devices, 16, lanes).astype(jnp.bfloat16)
        for h, target in enumerate((first_ref, second_ref)):

            @pl.when(half == h)
            def send_values():
                pltpu.make_async_copy(outgoing.at[h, me], target.at[me], own_sems.at[h]).start()

                def send(i, carry):
                    number, where = other(i)
                    pltpu.make_async_remote_copy(
                        src_ref=outgoing.at[h, number], dst_ref=target.at[me],
                        send_sem=value_sems.at[h, 0], recv_sem=value_sems.at[h, 1], device_id=where, device_id_type=MESH,
                    ).start()
                    return carry

                lax.fori_loop(1, devices, send, 0)

    @pl.when((half == HALVES - 1) & (step == chunks - 1))
    def end():
        wait_all(everyone, devices - 1, spots_sems)
        index_tables(everyone, index_ref)
        spots_ref[...] = everyone[...]
        for h, target in enumerate((first_ref, second_ref)):
            pltpu.make_async_copy(outgoing.at[h, me], target.at[me], own_sems.at[h]).wait()
            wait_all(target, devices - 1, value_sems.at[h])


def sort_blocks(lift, me, slab_ref, block_ref, place, everyone):
    spot = slab_ref[...] * lift + block_ref[...]
    chunks, lanes = spot.shape
    kept = chunks * lanes
    number = lax.broadcasted_iota(jnp.int32, (chunks, lanes), 0) * lanes + lax.broadcasted_iota(jnp.int32, (chunks, lanes), 1)
    key = ((spot // (BUCKET * NX * (NY // 64))) * kept + number).astype(jnp.float32)
    spot = spot.astype(jnp.float32)

    def upright(rows):
        return [jnp.broadcast_to(rows[c : c + 1, :], (lanes, lanes)).T for c in range(chunks)]

    key_up, spot_up = upright(key), upright(spot)
    ranks = []
    for c in range(chunks):
        line = key[c : c + 1, :]
        total = jnp.zeros((lanes, lanes), jnp.float32)
        for d in range(chunks):
            total = total + jnp.where(key_up[d] < line, 1.0, 0.0)
        ranks.append(jnp.sum(total, axis=0, keepdims=True))
    rank = jnp.concatenate(ranks, axis=0).astype(jnp.int32)
    wide = GROUP * lanes
    found = (rank // wide) * wide + (rank % GROUP) * lanes + (rank // GROUP) % lanes
    place[...] = found
    place_up = upright(found.astype(jnp.float32))
    goal = number.astype(jnp.float32)
    spots = []
    for c in range(chunks):
        line = goal[c : c + 1, :]
        total = jnp.zeros((lanes, lanes), jnp.float32)
        for d in range(chunks):
            total = total + jnp.where(place_up[d] == line, spot_up[d], 0.0)
        spots.append(jnp.sum(total, axis=0, keepdims=True))
    everyone[me] = jnp.concatenate(spots, axis=0).astype(jnp.int32)


def make_table(group, width, table):
    sources, share, vectors, readings = group.shape
    lines = [group[i, j].astype(jnp.float32) for i in range(sources) for j in range(share)]
    by_vector = [jnp.concatenate([line[v : v + 1, :] for line in lines], axis=0) for v in range(vectors)]
    rows = []
    for b in range(readings // width):
        rows.append(jnp.concatenate([a[:, b * width : (b + 1) * width] for a in by_vector], axis=1))
    used = sources * share * (readings // width)
    if used < table.shape[1]:
        rows.append(jnp.zeros((table.shape[1] - used, vectors * width), jnp.float32))
    table[...] = jnp.concatenate(rows, axis=0).T.astype(jnp.bfloat16)


def index_tables(all_ref, table_ref):
    sources, chunks, lanes = all_ref.shape
    lane = lax.broadcasted_iota(jnp.int32, (sources, LANES), 1)
    buckets = NZ // BUCKET

    def below(s, low):
        less = jnp.where(all_ref[...] < s * (BUCKET * NX * (NY // 64)), 1.0, 0.0)
        return jnp.where(lane == s, jnp.sum(jnp.sum(less, axis=1), axis=1, keepdims=True), low)

    low = lax.fori_loop(1, buckets + 1, below, jnp.zeros((sources, LANES), jnp.float32)).astype(jnp.int32)
    high = pltpu.roll(low, LANES - 1, 1)
    first = low // GROUP
    counts = jnp.where(high > low, (high + GROUP - 1) // GROUP - first, 0)
    counts = jnp.where(lane < buckets, counts, 0).astype(jnp.float32)
    row = lax.broadcasted_iota(jnp.int32, (sources, sources), 0)
    before = jnp.where(row > lax.broadcasted_iota(jnp.int32, (sources, sources), 1), 1.0, 0.0)
    ahead = jnp.dot(before.astype(jnp.bfloat16), counts.astype(jnp.bfloat16), preferred_element_type=jnp.float32)
    source = lax.broadcasted_iota(jnp.int32, (sources, LANES), 0)
    total = jnp.broadcast_to(jnp.sum(counts, axis=0, keepdims=True), (8, LANES))
    table_ref[:sources, :] = first + source * (chunks * lanes // GROUP)
    table_ref[sources : 2 * sources, :] = ahead.astype(jnp.int32)
    table_ref[2 * sources :, :] = total.astype(jnp.int32)


def model_kernel(
    plan, vectors, slots, table_ref, first_ref, second_ref, spots_ref, hx_ref, hz_ref, out_ref,
    index, index_sem, owner, rows_src, merged, left, right, plane, along_y
):
    sources, chunks, _ = spots_ref.shape
    kept = chunks * LANES
    height = vectors * slots
    beside = fold(vectors, slots)[2]
    buckets = NZ // BUCKET
    rows = kept // GROUP
    y_share = out_ref.shape[2] // NX
    lead = len(plan) * vectors

    row = lax.broadcasted_iota(jnp.int32, (LANES, LANES), 0)
    eye = jnp.where(row == lax.broadcasted_iota(jnp.int32, (LANES, LANES), 1), 1.0, 0.0).astype(jnp.bfloat16)

    def turned(block):
        return lax.dot_general(eye, block, (((1,), (1,)), ((), ())), preferred_element_type=jnp.float32)

    @pl.when(pl.program_id(0) == 0)
    def scatter():
        fetch = pltpu.make_async_copy(table_ref, index, index_sem)
        fetch.start()
        tail = rows_src.shape[0] - sources * rows
        rows_src[pl.ds(sources * rows, tail), :] = jnp.full((tail, LANES), -1.0, jnp.float32)

        def unpack(src, carry):
            per_y = NY // 64
            spots = spots_ref[src]
            marks = [(spots // per_y) % NX, spots // (NX * per_y), jnp.minimum(spots % per_y, 2)]
            marks = [m.astype(jnp.float32) for m in marks]
            for half in range(rows // LANES):
                tiles = [slice((half * beside + k) * LANES, (half * beside + k + 1) * LANES) for k in range(beside)]
                parts = [ref[src, :, lanes] for ref in (first_ref, second_ref) for lanes in tiles]
                used = GROUP * height + len(marks) * GROUP
                lines = [m[half * GROUP : (half + 1) * GROUP, :] for m in marks]
                lines.append(jnp.zeros((LANES - used, LANES), jnp.float32))
                parts.append(jnp.concatenate(lines, axis=0).astype(jnp.bfloat16))
                place = pl.ds(pl.multiple_of(src * rows + half * LANES, LANES), LANES)
                rows_src[place, :] = turned(jnp.concatenate(parts, axis=0))
            return carry

        lax.fori_loop(0, sources, unpack, 0, unroll=4)
        fetch.wait()
        layer = lax.broadcasted_iota(jnp.int32, (BUCKET, LANES), 0).astype(jnp.float32)
        spot = lax.broadcasted_iota(jnp.int32, (NX, LANES), 0).astype(jnp.float32).astype(jnp.bfloat16)
        one, zero = jnp.bfloat16(1.0), jnp.bfloat16(0.0)

        def bucket_step(s, base):
            def merge(i, carry):
                for u in range(MOVES):
                    src = i * MOVES + u
                    to = pl.ds(base * LANES + index[sources + src, s], WINDOW)
                    merged[to, :] = rows_src[pl.ds(index[src, s], WINDOW), :]
                return carry

            lax.fori_loop(0, sources // MOVES, merge, 0)
            count = index[2 * sources, s]
            merged[pl.ds(base * LANES + count, LANES), :] = jnp.full((LANES, LANES), -1.0, jnp.float32)
            tiles = (count + LANES - 1) // LANES

            def name(t, carry):
                owner[base + t] = s
                return carry

            lax.fori_loop(0, tiles, name, 0)
            return base + tiles

        tiles = lax.fori_loop(0, buckets, bucket_step, 0)
        for extra in range(PAIR):
            owner[tiles + extra] = 0
            place = pl.ds(pl.multiple_of((tiles + extra) * LANES, LANES), LANES)
            merged[place, :] = jnp.full((LANES, LANES), -1.0, jnp.float32)
        steps = (tiles + PAIR - 1) // PAIR

        def turn(first):
            block = [merged[pl.ds(first + u * LANES, LANES), :].T for u in range(PAIR)]
            for u in range(PAIR):
                merged[pl.ds(first + u * LANES, LANES), :] = block[u]

        turn(0)
        plane[...] = jnp.zeros_like(plane)
        left[...] = jnp.zeros_like(left)
        right[...] = jnp.zeros_like(right)

        def build(u, t, first):
            here = layer + (owner[t] * BUCKET).astype(jnp.float32)
            for k in range(GROUP):
                columns = slice(k * LANES, (k + 1) * LANES)

                def line(row):
                    return merged[pl.ds(first + row, 1), :]

                x = line(GROUP * height + k)
                code = line(GROUP * height + GROUP + k) + NZ * line(GROUP * height + 2 * GROUP + k)
                marks = [jnp.where(code == here + g * NZ, 1.0, 0.0) for g in range(3)]
                marks = [jnp.concatenate([m, m], axis=0).astype(jnp.bfloat16) for m in marks]
                lines = {}
                for v in range(0, vectors, 2):
                    for slot in range(slots):
                        pair = [line(row_of(k, i, slot, vectors, slots)) for i in (v, v + 1)]
                        pair = [jnp.broadcast_to(row, (BUCKET, LANES)) for row in pair]
                        lines[v, slot] = jnp.concatenate(pair, axis=0).astype(jnp.bfloat16)
                pieces = []
                for _, _, _, slot, group in plan:
                    pieces += [lines[v, slot] * marks[group] for v in range(0, vectors, 2)]
                left[u, :, columns] = jnp.concatenate(pieces, axis=0)
                right[u, :, columns] = jnp.where(x.astype(jnp.bfloat16) == spot, one, zero)

        def tile_step(i, carry):
            first = pl.multiple_of(i * PAIR * LANES, LANES)
            turn(first + PAIR * LANES)
            products = []
            for u in range(PAIR):
                product = lax.dot_general(left[u], right[u], (((1,), (1,)), ((), ())), preferred_element_type=jnp.float32)
                products.append(product.reshape(lead, BUCKET, NX))
            for u in range(PAIR):
                build(u, i * PAIR + u, first + u * LANES)
            for u in range(PAIR):
                s = owner[jnp.maximum((i - 1) * PAIR + u, 0)]
                place = pl.ds(pl.multiple_of(s * BUCKET, BUCKET), BUCKET)
                plane[:, place, :] += products[u]
            return carry

        lax.fori_loop(0, steps + 1, tile_step, 0)

    me = lax.axis_index("tile") * lax.axis_size("col") + lax.axis_index("col")
    v = pl.program_id(0)
    fixed = REST * REST
    for begin in range(0, NZ, STRIP):
        strip = [plane[p * vectors + v, begin : begin + STRIP, :] for p in range(len(plan))]
        strip = jnp.concatenate(strip, axis=0).astype(jnp.bfloat16)
        along_x = jnp.dot(strip, hx_ref[...], preferred_element_type=jnp.float32)
        parts = [along_x[p * STRIP : (p + 1) * STRIP, :] for p in range(len(plan))]
        current = [parts[0] * (fixed * ROOT**LEVELS)]
        taken = 1
        for level in range(LEVELS):
            reach = 2 ** (LEVELS - level)
            held = max(1, y_share // reach)
            scale = fixed * ROOT ** (LEVELS - level)
            details = parts[taken : taken + held]
            taken += held
            if y_share >= reach:
                scaled = [d * scale for d in details]
                current = [e for c, d in zip(current, scaled) for e in (c + d, c - d)]
            else:
                current = [current[0] + details[0] * jnp.where(lax.rem(me * y_share, reach) < reach // 2, scale, -scale)]
        for y in range(y_share):
            along_y[y, begin : begin + STRIP, :] = current[y].astype(jnp.bfloat16)
    for y in range(y_share):
        out_ref[0, :, y * NX : (y + 1) * NX] = jnp.dot(hz_ref[...], along_y[y], preferred_element_type=jnp.float32)


def receive(plan, vectors, slots, y_share, table, first, second, all_spots):
    sources, chunks, _ = all_spots.shape
    rows = chunks * LANES // GROUP
    hx = jnp.asarray(haar(NX), jnp.bfloat16)
    hz = jnp.asarray(haar(NZ).T, jnp.bfloat16)
    lead = len(plan) * vectors
    most = sources * (rows + NZ // BUCKET)
    most_tiles = most // LANES + NZ // BUCKET + 3 * PAIR

    def whole(array):
        return pl.BlockSpec(array.shape, lambda v: (0,) * array.ndim)

    return pl.pallas_call(
        functools.partial(model_kernel, plan, vectors, slots),
        out_shape=jax.ShapeDtypeStruct((vectors, NZ, y_share * NX), jnp.float32),
        grid=(vectors,),
        in_specs=[pl.BlockSpec(memory_space=pl.ANY), whole(first), whole(second), whole(all_spots), whole(hx), whole(hz)],
        out_specs=pl.BlockSpec((1, NZ, y_share * NX), lambda v: (v, 0, 0)),
        scratch_shapes=[
            pltpu.SMEM(table.shape, jnp.int32),
            pltpu.SemaphoreType.DMA,
            pltpu.SMEM((most_tiles,), jnp.int32),
            pltpu.VMEM((sources * rows + WINDOW, LANES), jnp.float32),
            pltpu.VMEM((most_tiles * LANES, LANES), jnp.float32),
            pltpu.VMEM((PAIR, lead * BUCKET, GROUP * LANES), jnp.bfloat16),
            pltpu.VMEM((PAIR, NX, GROUP * LANES), jnp.bfloat16),
            pltpu.VMEM((lead, NZ, NX), jnp.float32),
            pltpu.VMEM((y_share, NZ, NX), jnp.bfloat16),
        ],
        compiler_params=pltpu.CompilerParams(vmem_limit_bytes=60 * 2**20),
    )(table, first, second, all_spots, hx, hz)


def on_device(readings, sensitivity, kept_tile, kept_row, kept_slab, kept_block):
    devices = lax.axis_size(AXES)
    columns = lax.axis_size("col")
    kept, width, _ = sensitivity.shape
    vectors = readings.shape[1]
    per_y = NY // width
    layers = NZ // devices
    y_share = NY // devices
    plan, slots = y_plan(y_share, width)
    chunks = kept // LANES
    spread = jnp.asarray(spread_matrix(plan, slots, devices, vectors, width, y_share), jnp.bfloat16)
    used = columns * readings.shape[0] * (readings.shape[2] // width)
    part = fold(vectors, slots)[2] * (chunks // GROUP) * LANES
    values = jax.ShapeDtypeStruct((devices, 16, part), jnp.bfloat16)
    spots = jax.ShapeDtypeStruct((devices, chunks, LANES), jnp.int32)
    index = jax.ShapeDtypeStruct((2 * devices + 8, LANES), jnp.int32)
    hbm = pl.BlockSpec(memory_space=pl.ANY)

    def whole(array):
        return pl.BlockSpec(array.shape, lambda h, i: (0,) * len(array.shape))

    square = jax.ShapeDtypeStruct((chunks, LANES), jnp.int32)
    first, second, all_spots, table = pl.pallas_call(
        functools.partial(front_kernel, layers * NX * per_y, slots),
        out_shape=(values, values, spots, index),
        grid=(HALVES, chunks),
        in_specs=[
            whole(readings),
            whole(square),
            whole(square),
            pl.BlockSpec((1, LANES), lambda h, i: (0, i)),
            pl.BlockSpec((1, LANES), lambda h, i: (0, i)),
            whole(spread),
            pl.BlockSpec((width, width, LANES), lambda h, i: (0, 0, i)),
        ],
        out_specs=(hbm, hbm, whole(spots), whole(index)),
        scratch_shapes=[
            pltpu.VMEM((columns, *readings.shape), readings.dtype),
            pltpu.VMEM((chunks, LANES), jnp.int32),
            pltpu.VMEM(spots.shape, jnp.int32),
            pltpu.VMEM((vectors * width, -(-used // LANES) * LANES), jnp.bfloat16),
            pltpu.VMEM((vectors // HALVES * width, LANES), jnp.float32),
            pltpu.VMEM((vectors // HALVES * width, kept), jnp.bfloat16),
            pltpu.VMEM((kept, kept), jnp.bfloat16),
            pltpu.VMEM((HALVES, *values.shape), jnp.bfloat16),
            pltpu.SemaphoreType.DMA((2,)),
            pltpu.SemaphoreType.DMA((2,)),
            pltpu.SemaphoreType.DMA((HALVES, 2)),
            pltpu.SemaphoreType.DMA((HALVES,)),
        ],
        compiler_params=pltpu.CompilerParams(collective_id=0, has_side_effects=True, vmem_limit_bytes=60 * 2**20),
    )(
        readings, kept_slab.reshape(chunks, LANES), kept_block.reshape(chunks, LANES), kept_tile[None, :],
        kept_row[None, :], spread, sensitivity.transpose(1, 2, 0),
    )
    return receive(plan, vectors, slots, y_share, table, first, second, all_spots)


def solution(mesh):
    return jax.shard_map(
        on_device,
        mesh=mesh,
        in_specs=(
            P(AXES, None, None),
            P(AXES, None, None),
            P(AXES),
            P(AXES),
            P(AXES, None),
            P(AXES),
        ),
        out_specs=P(None, None, AXES),
        check_vma=False,
    )
```

```python
import functools

import jax
import jax.numpy as jnp
import numpy as np
from jax import lax
from jax.experimental import pallas as pl
from jax.experimental.pallas import tpu as pltpu
from jax.sharding import PartitionSpec as P

NX = 256
NY = 256
NZ = 256
LEVELS = 3
ROOT = 0.7071067811865476
LANES = 128
BUCKET = 8
MOVES = 32
PAIR = 4
STRIP = 32
GROUP = 4
CAP = 80
WINDOW = 24
STEPS = (239 / 256, 169 / 256, 239 / 512, 169 / 512)
REST = 256 / 239
AXES = ("tile", "col")


def segments(length):
    coarse = length // 2**LEVELS
    found = [(0, coarse, 2**LEVELS)]
    for level in range(LEVELS):
        found.append((coarse * 2**level, coarse * 2**level, 2 ** (LEVELS - level)))
    return found


def haar(length):
    matrix = np.zeros((length, length), np.float32)
    for number, (start, count, reach) in enumerate(segments(length)):
        for i in range(count):
            half = reach // 2 if number else reach
            matrix[start + i, i * reach : i * reach + half] = STEPS[reach.bit_length() - 1]
            matrix[start + i, i * reach + half : (i + 1) * reach] = -STEPS[reach.bit_length() - 1]
    return matrix


def y_plan(y_share, width):
    rows = []
    used = {}
    for start, count, reach in segments(NY):
        group = min(start // width, 2)
        for i in range(max(1, y_share // reach)):
            slot = used.get(group, 0)
            used[group] = slot + 1
            rows.append((start, reach, i, slot, group))
    return rows, max(used.values())


def fold(vectors, slots):
    parts = 2
    height = vectors // parts * slots
    stack = 16 // height
    return parts, height, stack, GROUP // stack


def row_of(k, v, slot, vectors, slots):
    parts, height, stack, beside = fold(vectors, slots)
    share = vectors // parts
    return ((v // share) * beside + k % beside) * 16 + k // beside * height + v % share * slots + slot


def spread_matrix(plan, slots, devices, vectors, width, y_share):
    per_y = NY // width
    parts, height, stack, _ = fold(vectors, slots)
    share = vectors // parts
    matrix = np.zeros((devices, stack, share, slots, stack, per_y, share, width), np.float32)
    for start, reach, i, slot, _ in plan:
        for owner in range(devices):
            y = start + owner * y_share // reach + i
            for v in range(share):
                for k in range(stack):
                    matrix[owner, k, v, slot, k, y // width, v, y % width] = 1.0
    return matrix.reshape(devices * 16, stack * per_y * share * width)


def front_kernel(
    lift, slots, readings_ref, slab_ref, block_ref, tiles_ref, rows_ref, spread_ref, sens_ref,
    *refs,
):
    parts, _, stack, beside = fold(readings_ref.shape[1], slots)
    value_refs, (spots_ref, index_ref, sens, group, place, everyone, table, picked, made, moved, outgoing), sems = (
        refs[:parts], refs[parts : parts + 11], refs[parts + 11 :]
    )
    group_sems, spots_sems, value_sems, own_sems, sens_sems = sems
    width = sens_ref.shape[0]
    columns, _, vectors, readings = group.shape
    devices, chunks, lanes = everyone.shape
    share = vectors // parts
    per_y = NY // width
    half, step = pl.program_id(0), pl.program_id(1)
    tile, col = lax.axis_index("tile"), lax.axis_index("col")
    me = tile * columns + col
    MESH = pl.DeviceIdType.MESH

    def other(i):
        number = lax.rem(me + i, devices)
        return number, (number // columns, lax.rem(number, columns))

    def wait_all(ref, count, sems):
        part = ref.at[pl.ds(0, count)]
        copy = pltpu.make_async_remote_copy(
            src_ref=part, dst_ref=part, send_sem=sems.at[0], recv_sem=sems.at[1], device_id=(tile, col), device_id_type=MESH
        )
        copy.wait_send()
        copy.wait_recv()

    def fetch(c):
        column = pl.ds(c * lanes, lanes)
        return pltpu.make_async_copy(sens_ref.at[:, :, column], sens.at[:, :, column], sens_sems.at[c])

    @pl.when((half == 0) & (step == 0))
    def begin():
        barrier = pltpu.get_barrier_semaphore()

        def greet(i, carry):
            pl.semaphore_signal(barrier, inc=1, device_id=other(i)[1], device_id_type=MESH)
            return carry

        lax.fori_loop(1, devices, greet, 0)
        for c in range(chunks):
            fetch(c).start()
        group[col] = readings_ref[...]
        sort_blocks(lift, me, slab_ref, block_ref, place, everyone)
        pl.semaphore_wait(barrier, devices - 1)

        def send_readings(i, carry):
            pltpu.make_async_remote_copy(
                src_ref=group.at[col], dst_ref=group.at[col], send_sem=group_sems.at[0], recv_sem=group_sems.at[1],
                device_id=(tile, lax.rem(col + i, columns)), device_id_type=MESH,
            ).start()
            return carry

        lax.fori_loop(1, columns, send_readings, 0)

        def send_spots(i, carry):
            pltpu.make_async_remote_copy(
                src_ref=everyone.at[me], dst_ref=everyone.at[me], send_sem=spots_sems.at[0], recv_sem=spots_sems.at[1],
                device_id=other(i)[1], device_id_type=MESH,
            ).start()
            return carry

        lax.fori_loop(1, devices, send_spots, 0)
        wait_all(group, columns - 1, group_sems)
        make_table(group, width, table)

    tiles = group.shape[0] * group.shape[1]
    spots = lax.broadcasted_iota(jnp.int32, (table.shape[1], lanes), 0)
    here = pl.ds(pl.multiple_of(step * lanes, lanes), lanes)
    chosen = jnp.where(rows_ref[:, here] * tiles + tiles_ref[:, here] == spots, 1.0, 0.0).astype(jnp.bfloat16)

    @pl.when(half == 0)
    def arrive():
        pltpu.make_async_copy(sens_ref.at[:, :, here], sens.at[:, :, here], sens_sems.at[step]).wait()

    mine = table[pl.ds(pl.multiple_of(half * (share * width), share * width), share * width), :]
    picked[...] = jnp.dot(mine, chosen, preferred_element_type=jnp.float32)
    sums = [jnp.zeros((width, lanes), jnp.float32) for _ in range(share)]
    for r in range(width):
        block = sens[r, :, here].astype(jnp.float32)
        for v in range(share):
            sums[v] = sums[v] + block * picked[v * width + r : v * width + r + 1, :]
    for v in range(share):
        made[v * width : (v + 1) * width, here] = sums[v].astype(jnp.bfloat16)

    @pl.when(half == 0)
    def order():
        goal = lax.broadcasted_iota(jnp.int32, (lanes, lanes), 0) + step * lanes
        hits = [jnp.where(place[d : d + 1, :] == goal, 1.0, 0.0) for d in range(chunks)]
        moved[here, :] = jnp.concatenate(hits, axis=1).astype(jnp.bfloat16)

    @pl.when(step == chunks - 1)
    def send_half():
        in_y = everyone[me] % per_y
        ordered = lax.dot_general(made[...], moved[...], (((1,), (1,)), ((), ())), preferred_element_type=jnp.float32)
        masked = []
        for up in range(stack):
            picks = [part * GROUP + up * beside + k for part in range(chunks // GROUP) for k in range(beside)]
            values = jnp.concatenate([ordered[:, p * lanes : (p + 1) * lanes] for p in picks], axis=1)
            block = jnp.concatenate([in_y[p : p + 1, :] for p in picks], axis=1)
            masked += [jnp.where(block == b, values, 0.0).astype(jnp.bfloat16) for b in range(per_y)]
        sent = jnp.dot(spread_ref[...], jnp.concatenate(masked, axis=0), preferred_element_type=jnp.float32)
        outgoing[half] = sent.reshape(outgoing.shape[1:]).astype(jnp.bfloat16)
        for h, target in enumerate(value_refs):

            @pl.when(half == h)
            def send_values():
                pltpu.make_async_copy(outgoing.at[h, me], target.at[me], own_sems.at[h]).start()

                def send(i, carry):
                    number, where = other(i)
                    pltpu.make_async_remote_copy(
                        src_ref=outgoing.at[h, number], dst_ref=target.at[me],
                        send_sem=value_sems.at[h, 0], recv_sem=value_sems.at[h, 1], device_id=where, device_id_type=MESH,
                    ).start()
                    return carry

                lax.fori_loop(1, devices, send, 0)

    @pl.when((half == parts - 1) & (step == chunks - 1))
    def end():
        wait_all(everyone, devices - 1, spots_sems)
        index_tables(everyone, index_ref)
        spots_ref[...] = everyone[...]
        for h, target in enumerate(value_refs):
            pltpu.make_async_copy(outgoing.at[h, me], target.at[me], own_sems.at[h]).wait()
            wait_all(target, devices - 1, value_sems.at[h])


def sort_blocks(lift, me, slab_ref, block_ref, place, everyone):
    spot = slab_ref[...] * lift + block_ref[...]
    chunks, lanes = spot.shape
    kept = chunks * lanes
    number = lax.broadcasted_iota(jnp.int32, (chunks, lanes), 0) * lanes + lax.broadcasted_iota(jnp.int32, (chunks, lanes), 1)
    key = ((spot // (BUCKET * NX * (NY // 64))) * kept + number).astype(jnp.float32)
    spot = spot.astype(jnp.float32)

    def upright(rows):
        return [jnp.broadcast_to(rows[c : c + 1, :], (lanes, lanes)).T for c in range(chunks)]

    key_up, spot_up = upright(key), upright(spot)
    ranks = []
    for c in range(chunks):
        line = key[c : c + 1, :]
        total = jnp.zeros((lanes, lanes), jnp.float32)
        for d in range(chunks):
            total = total + jnp.where(key_up[d] < line, 1.0, 0.0)
        ranks.append(jnp.sum(total, axis=0, keepdims=True))
    rank = jnp.concatenate(ranks, axis=0).astype(jnp.int32)
    wide = GROUP * lanes
    found = (rank // wide) * wide + (rank % GROUP) * lanes + (rank // GROUP) % lanes
    place[...] = found
    place_up = upright(found.astype(jnp.float32))
    goal = number.astype(jnp.float32)
    spots = []
    for c in range(chunks):
        line = goal[c : c + 1, :]
        total = jnp.zeros((lanes, lanes), jnp.float32)
        for d in range(chunks):
            total = total + jnp.where(place_up[d] == line, spot_up[d], 0.0)
        spots.append(jnp.sum(total, axis=0, keepdims=True))
    everyone[me] = jnp.concatenate(spots, axis=0).astype(jnp.int32)


def make_table(group, width, table):
    sources, share, vectors, readings = group.shape
    lines = [group[i, j].astype(jnp.float32) for i in range(sources) for j in range(share)]
    by_vector = [jnp.concatenate([line[v : v + 1, :] for line in lines], axis=0) for v in range(vectors)]
    rows = []
    for b in range(readings // width):
        rows.append(jnp.concatenate([a[:, b * width : (b + 1) * width] for a in by_vector], axis=1))
    used = sources * share * (readings // width)
    if used < table.shape[1]:
        rows.append(jnp.zeros((table.shape[1] - used, vectors * width), jnp.float32))
    table[...] = jnp.concatenate(rows, axis=0).T.astype(jnp.bfloat16)


def index_tables(all_ref, table_ref):
    sources, chunks, lanes = all_ref.shape
    lane = lax.broadcasted_iota(jnp.int32, (sources, LANES), 1)
    buckets = NZ // BUCKET

    def below(s, low):
        less = jnp.where(all_ref[...] < s * (BUCKET * NX * (NY // 64)), 1.0, 0.0)
        return jnp.where(lane == s, jnp.sum(jnp.sum(less, axis=1), axis=1, keepdims=True), low)

    low = lax.fori_loop(1, buckets + 1, below, jnp.zeros((sources, LANES), jnp.float32)).astype(jnp.int32)
    high = pltpu.roll(low, LANES - 1, 1)
    first = low // GROUP
    counts = jnp.where(high > low, (high + GROUP - 1) // GROUP - first, 0)
    counts = jnp.where(lane < buckets, counts, 0).astype(jnp.float32)
    row = lax.broadcasted_iota(jnp.int32, (sources, sources), 0)
    before = jnp.where(row > lax.broadcasted_iota(jnp.int32, (sources, sources), 1), 1.0, 0.0)
    ahead = jnp.dot(before.astype(jnp.bfloat16), counts.astype(jnp.bfloat16), preferred_element_type=jnp.float32)
    source = lax.broadcasted_iota(jnp.int32, (sources, LANES), 0)
    total = jnp.broadcast_to(jnp.sum(counts, axis=0, keepdims=True), (8, LANES))
    table_ref[:sources, :] = first + source * (chunks * lanes // GROUP)
    table_ref[sources : 2 * sources, :] = ahead.astype(jnp.int32)
    table_ref[2 * sources :, :] = total.astype(jnp.int32)


def model_kernel(
    plan, vectors, slots, table_ref, spots_ref, hx_ref, hz_ref, *refs
):
    sources, chunks, _ = spots_ref.shape
    kept = chunks * LANES
    height = vectors * slots
    parts, _, _, beside = fold(vectors, slots)
    value_refs, (out_ref, index, index_sem, owner, rows_src, merged, left, right, plane, along_y) = refs[:parts], refs[parts:]
    buckets = NZ // BUCKET
    rows = kept // GROUP
    y_share = out_ref.shape[2] // NX
    lead = len(plan) * vectors

    row = lax.broadcasted_iota(jnp.int32, (LANES, LANES), 0)
    eye = jnp.where(row == lax.broadcasted_iota(jnp.int32, (LANES, LANES), 1), 1.0, 0.0).astype(jnp.bfloat16)

    def turned(block):
        return lax.dot_general(eye, block, (((1,), (1,)), ((), ())), preferred_element_type=jnp.float32)

    @pl.when(pl.program_id(0) == 0)
    def scatter():
        fetch = pltpu.make_async_copy(table_ref, index, index_sem)
        fetch.start()
        tail = rows_src.shape[0] - sources * rows
        rows_src[pl.ds(sources * rows, tail), :] = jnp.full((tail, LANES), -1.0, jnp.float32)

        def unpack(src, carry):
            per_y = NY // 64
            spots = spots_ref[src]
            marks = [(spots // per_y) % NX, spots // (NX * per_y), jnp.minimum(spots % per_y, 2)]
            marks = [m.astype(jnp.float32) for m in marks]
            for half in range(rows // LANES):
                tiles = [slice((half * beside + k) * LANES, (half * beside + k + 1) * LANES) for k in range(beside)]
                block = [ref[src, :, lanes] for ref in value_refs for lanes in tiles]
                used = GROUP * height + len(marks) * GROUP
                lines = [m[half * GROUP : (half + 1) * GROUP, :] for m in marks]
                lines.append(jnp.zeros((LANES - used, LANES), jnp.float32))
                block.append(jnp.concatenate(lines, axis=0).astype(jnp.bfloat16))
                place = pl.ds(pl.multiple_of(src * rows + half * LANES, LANES), LANES)
                rows_src[place, :] = turned(jnp.concatenate(block, axis=0))
            return carry

        lax.fori_loop(0, sources, unpack, 0, unroll=4)
        fetch.wait()
        layer = lax.broadcasted_iota(jnp.int32, (BUCKET, LANES), 0).astype(jnp.float32)
        spot = lax.broadcasted_iota(jnp.int32, (NX, LANES), 0).astype(jnp.float32).astype(jnp.bfloat16)
        one, zero = jnp.bfloat16(1.0), jnp.bfloat16(0.0)

        def bucket_step(s, base):
            def merge(i, carry):
                for u in range(MOVES):
                    src = i * MOVES + u
                    to = pl.ds(base * LANES + index[sources + src, s], WINDOW)
                    merged[to, :] = rows_src[pl.ds(index[src, s], WINDOW), :]
                return carry

            lax.fori_loop(0, sources // MOVES, merge, 0)
            count = index[2 * sources, s]
            merged[pl.ds(base * LANES + count, LANES), :] = jnp.full((LANES, LANES), -1.0, jnp.float32)
            tiles = (count + LANES - 1) // LANES

            def name(t, carry):
                owner[base + t] = s
                return carry

            lax.fori_loop(0, tiles, name, 0)
            return base + tiles

        tiles = lax.fori_loop(0, buckets, bucket_step, 0)
        for extra in range(PAIR):
            owner[tiles + extra] = 0
            place = pl.ds(pl.multiple_of((tiles + extra) * LANES, LANES), LANES)
            merged[place, :] = jnp.full((LANES, LANES), -1.0, jnp.float32)
        steps = (tiles + PAIR - 1) // PAIR

        def turn(first):
            block = [merged[pl.ds(first + u * LANES, LANES), :].T for u in range(PAIR)]
            for u in range(PAIR):
                merged[pl.ds(first + u * LANES, LANES), :] = block[u]

        turn(0)
        plane[...] = jnp.zeros_like(plane)
        left[...] = jnp.zeros_like(left)
        right[...] = jnp.zeros_like(right)

        def build(u, t, first):
            here = layer + (owner[t] * BUCKET).astype(jnp.float32)
            for k in range(GROUP):
                columns = slice(k * LANES, (k + 1) * LANES)

                def line(row):
                    return merged[pl.ds(first + row, 1), :]

                x = line(GROUP * height + k)
                code = line(GROUP * height + GROUP + k) + NZ * line(GROUP * height + 2 * GROUP + k)
                marks = [jnp.where(code == here + g * NZ, 1.0, 0.0) for g in range(3)]
                marks = [jnp.concatenate([m, m], axis=0).astype(jnp.bfloat16) for m in marks]
                lines = {}
                for v in range(0, vectors, 2):
                    for slot in range(slots):
                        pair = [line(row_of(k, i, slot, vectors, slots)) for i in (v, v + 1)]
                        pair = [jnp.broadcast_to(row, (BUCKET, LANES)) for row in pair]
                        lines[v, slot] = jnp.concatenate(pair, axis=0).astype(jnp.bfloat16)
                pieces = []
                for _, _, _, slot, group in plan:
                    pieces += [lines[v, slot] * marks[group] for v in range(0, vectors, 2)]
                left[u, :, columns] = jnp.concatenate(pieces, axis=0)
                right[u, :, columns] = jnp.where(x.astype(jnp.bfloat16) == spot, one, zero)

        def tile_step(i, carry):
            first = pl.multiple_of(i * PAIR * LANES, LANES)
            turn(first + PAIR * LANES)
            products = []
            for u in range(PAIR):
                product = lax.dot_general(left[u], right[u], (((1,), (1,)), ((), ())), preferred_element_type=jnp.float32)
                products.append(product.reshape(lead, BUCKET, NX))
            for u in range(PAIR):
                build(u, i * PAIR + u, first + u * LANES)
            for u in range(PAIR):
                s = owner[jnp.maximum((i - 1) * PAIR + u, 0)]
                place = pl.ds(pl.multiple_of(s * BUCKET, BUCKET), BUCKET)
                plane[:, place, :] += products[u]
            return carry

        lax.fori_loop(0, steps + 1, tile_step, 0)

    me = lax.axis_index("tile") * lax.axis_size("col") + lax.axis_index("col")
    v = pl.program_id(0)
    fixed = REST * REST
    for begin in range(0, NZ, STRIP):
        strip = [plane[p * vectors + v, begin : begin + STRIP, :] for p in range(len(plan))]
        strip = jnp.concatenate(strip, axis=0).astype(jnp.bfloat16)
        along_x = jnp.dot(strip, hx_ref[...], preferred_element_type=jnp.float32)
        parts = [along_x[p * STRIP : (p + 1) * STRIP, :] for p in range(len(plan))]
        current = [parts[0] * (fixed * ROOT**LEVELS)]
        taken = 1
        for level in range(LEVELS):
            reach = 2 ** (LEVELS - level)
            held = max(1, y_share // reach)
            scale = fixed * ROOT ** (LEVELS - level)
            details = parts[taken : taken + held]
            taken += held
            if y_share >= reach:
                scaled = [d * scale for d in details]
                current = [e for c, d in zip(current, scaled) for e in (c + d, c - d)]
            else:
                current = [current[0] + details[0] * jnp.where(lax.rem(me * y_share, reach) < reach // 2, scale, -scale)]
        for y in range(y_share):
            along_y[y, begin : begin + STRIP, :] = current[y].astype(jnp.bfloat16)
    for y in range(y_share):
        out_ref[0, :, y * NX : (y + 1) * NX] = jnp.dot(hz_ref[...], along_y[y], preferred_element_type=jnp.float32)


def receive(plan, vectors, slots, y_share, table, values, all_spots):
    sources, chunks, _ = all_spots.shape
    rows = chunks * LANES // GROUP
    hx = jnp.asarray(haar(NX), jnp.bfloat16)
    hz = jnp.asarray(haar(NZ).T, jnp.bfloat16)
    lead = len(plan) * vectors
    most = sources * (rows + NZ // BUCKET)
    most_tiles = most // LANES + NZ // BUCKET + 3 * PAIR

    def whole(array):
        return pl.BlockSpec(array.shape, lambda v: (0,) * array.ndim)

    return pl.pallas_call(
        functools.partial(model_kernel, plan, vectors, slots),
        out_shape=jax.ShapeDtypeStruct((vectors, NZ, y_share * NX), jnp.float32),
        grid=(vectors,),
        in_specs=[pl.BlockSpec(memory_space=pl.ANY), whole(all_spots), whole(hx), whole(hz)] + [whole(v) for v in values],
        out_specs=pl.BlockSpec((1, NZ, y_share * NX), lambda v: (v, 0, 0)),
        scratch_shapes=[
            pltpu.SMEM(table.shape, jnp.int32),
            pltpu.SemaphoreType.DMA,
            pltpu.SMEM((most_tiles,), jnp.int32),
            pltpu.VMEM((sources * rows + WINDOW, LANES), jnp.float32),
            pltpu.VMEM((most_tiles * LANES, LANES), jnp.float32),
            pltpu.VMEM((PAIR, lead * BUCKET, GROUP * LANES), jnp.bfloat16),
            pltpu.VMEM((PAIR, NX, GROUP * LANES), jnp.bfloat16),
            pltpu.VMEM((lead, NZ, NX), jnp.float32),
            pltpu.VMEM((y_share, NZ, NX), jnp.bfloat16),
        ],
        compiler_params=pltpu.CompilerParams(vmem_limit_bytes=60 * 2**20),
    )(table, all_spots, hx, hz, *values)


def on_device(readings, sensitivity, kept_tile, kept_row, kept_slab, kept_block):
    devices = lax.axis_size(AXES)
    columns = lax.axis_size("col")
    kept, width, _ = sensitivity.shape
    vectors = readings.shape[1]
    per_y = NY // width
    layers = NZ // devices
    y_share = NY // devices
    plan, slots = y_plan(y_share, width)
    chunks = kept // LANES
    spread = jnp.asarray(spread_matrix(plan, slots, devices, vectors, width, y_share), jnp.bfloat16)
    used = columns * readings.shape[0] * (readings.shape[2] // width)
    parts, _, _, beside = fold(vectors, slots)
    values = jax.ShapeDtypeStruct((devices, 16, beside * (chunks // GROUP) * LANES), jnp.bfloat16)
    spots = jax.ShapeDtypeStruct((devices, chunks, LANES), jnp.int32)
    index = jax.ShapeDtypeStruct((2 * devices + 8, LANES), jnp.int32)
    hbm = pl.BlockSpec(memory_space=pl.ANY)

    def whole(array):
        return pl.BlockSpec(array.shape, lambda h, i: (0,) * len(array.shape))

    square = jax.ShapeDtypeStruct((chunks, LANES), jnp.int32)
    *values, all_spots, table = pl.pallas_call(
        functools.partial(front_kernel, layers * NX * per_y, slots),
        out_shape=(*[values] * parts, spots, index),
        grid=(parts, chunks),
        in_specs=[
            whole(readings),
            whole(square),
            whole(square),
            pl.BlockSpec((1, kept), lambda h, i: (0, 0)),
            pl.BlockSpec((1, kept), lambda h, i: (0, 0)),
            whole(spread),
            hbm,
        ],
        out_specs=(*[hbm] * parts, whole(spots), whole(index)),
        scratch_shapes=[
            pltpu.VMEM((width, width, kept), jnp.bfloat16),
            pltpu.VMEM((columns, *readings.shape), readings.dtype),
            pltpu.VMEM((chunks, LANES), jnp.int32),
            pltpu.VMEM(spots.shape, jnp.int32),
            pltpu.VMEM((vectors * width, -(-used // LANES) * LANES), jnp.bfloat16),
            pltpu.VMEM((vectors // parts * width, LANES), jnp.float32),
            pltpu.VMEM((vectors // parts * width, kept), jnp.bfloat16),
            pltpu.VMEM((kept, kept), jnp.bfloat16),
            pltpu.VMEM((parts, *values.shape), jnp.bfloat16),
            pltpu.SemaphoreType.DMA((2,)),
            pltpu.SemaphoreType.DMA((2,)),
            pltpu.SemaphoreType.DMA((parts, 2)),
            pltpu.SemaphoreType.DMA((parts,)),
            pltpu.SemaphoreType.DMA((chunks,)),
        ],
        compiler_params=pltpu.CompilerParams(collective_id=0, has_side_effects=True, vmem_limit_bytes=60 * 2**20),
    )(
        readings, kept_slab.reshape(chunks, LANES), kept_block.reshape(chunks, LANES), kept_tile[None, :],
        kept_row[None, :], spread, sensitivity.transpose(1, 2, 0),
    )
    return receive(plan, vectors, slots, y_share, table, values, all_spots)


def solution(mesh):
    return jax.shard_map(
        on_device,
        mesh=mesh,
        in_specs=(
            P(AXES, None, None),
            P(AXES, None, None),
            P(AXES),
            P(AXES),
            P(AXES, None),
            P(AXES),
        ),
        out_specs=P(None, None, AXES),
        check_vma=False,
    )
```

```python
import functools

import jax
import jax.numpy as jnp
import numpy as np
from jax import lax
from jax.experimental import pallas as pl
from jax.experimental.pallas import tpu as pltpu
from jax.sharding import PartitionSpec as P

NX = 256
NY = 256
NZ = 256
LEVELS = 3
ROOT = 0.7071067811865476
LANES = 128
BUCKET = 8
MOVES = 32
PAIR = 4
STRIP = 32
GROUP = 4
CAP = 80
WINDOW = 24
STEPS = (239 / 256, 169 / 256, 239 / 512, 169 / 512)
REST = 256 / 239
AXES = ("tile", "col")


def segments(length):
    coarse = length // 2**LEVELS
    found = [(0, coarse, 2**LEVELS)]
    for level in range(LEVELS):
        found.append((coarse * 2**level, coarse * 2**level, 2 ** (LEVELS - level)))
    return found


def haar(length):
    matrix = np.zeros((length, length), np.float32)
    for number, (start, count, reach) in enumerate(segments(length)):
        for i in range(count):
            half = reach // 2 if number else reach
            matrix[start + i, i * reach : i * reach + half] = STEPS[reach.bit_length() - 1]
            matrix[start + i, i * reach + half : (i + 1) * reach] = -STEPS[reach.bit_length() - 1]
    return matrix


def y_plan(y_share, width):
    rows = []
    used = {}
    for start, count, reach in segments(NY):
        group = min(start // width, 2)
        for i in range(max(1, y_share // reach)):
            slot = used.get(group, 0)
            used[group] = slot + 1
            rows.append((start, reach, i, slot, group))
    return rows, max(used.values())


def fold(vectors, slots):
    parts = 2
    height = vectors // parts * slots
    stack = 16 // height
    return parts, height, stack, GROUP // stack


def row_of(k, v, slot, vectors, slots):
    parts, height, stack, beside = fold(vectors, slots)
    share = vectors // parts
    return ((v // share) * beside + k % beside) * 16 + k // beside * height + v % share * slots + slot


def spread_matrix(plan, slots, devices, vectors, width, y_share):
    per_y = NY // width
    parts, height, stack, _ = fold(vectors, slots)
    share = vectors // parts
    matrix = np.zeros((devices, stack, share, slots, stack, per_y, share, width), np.float32)
    for start, reach, i, slot, _ in plan:
        for owner in range(devices):
            y = start + owner * y_share // reach + i
            for v in range(share):
                for k in range(stack):
                    matrix[owner, k, v, slot, k, y // width, v, y % width] = 1.0
    matrix = matrix.reshape(devices, 16, stack, per_y, share * width)
    halves = np.split(matrix, 2)
    return np.stack([h[:, :, :, meets(o, per_y)].reshape(devices * 8, -1) for o, h in enumerate(halves)])


def meets(half, per_y):
    return list(range(per_y // 2)) + [per_y // 2 + half]


def front_kernel(
    lift, slots, readings_ref, slab_ref, block_ref, tiles_ref, rows_ref, spread_ref, sens_ref,
    *refs,
):
    parts, _, stack, beside = fold(readings_ref.shape[1], slots)
    value_refs, (spots_ref, index_ref, sens, group, place, mine, everyone, table, picked, made, moved, outgoing), sems = (
        refs[:parts], refs[parts : parts + 12], refs[parts + 12 :]
    )
    group_sems, spots_sems, value_sems, own_sems, sens_sems = sems
    width = sens_ref.shape[0]
    columns, _, vectors, readings = group.shape
    devices, chunks, lanes = everyone.shape
    share = vectors // parts
    per_y = NY // width
    half, step = pl.program_id(0), pl.program_id(1)
    tile, col = lax.axis_index("tile"), lax.axis_index("col")
    me = tile * columns + col
    MESH = pl.DeviceIdType.MESH

    def other(i):
        number = lax.rem(me + i, devices)
        return number, (number // columns, lax.rem(number, columns))

    def wait_all(ref, count, sems):
        part = ref.at[pl.ds(0, count)]
        copy = pltpu.make_async_remote_copy(
            src_ref=part, dst_ref=part, send_sem=sems.at[0], recv_sem=sems.at[1], device_id=(tile, col), device_id_type=MESH
        )
        copy.wait_send()
        copy.wait_recv()

    def fetch(c):
        column = pl.ds(c * lanes, lanes)
        return pltpu.make_async_copy(sens_ref.at[:, :, column], sens.at[:, :, column], sens_sems.at[c])

    @pl.when((half == 0) & (step == 0))
    def begin():
        barrier = pltpu.get_barrier_semaphore()

        def greet(i, carry):
            pl.semaphore_signal(barrier, inc=1, device_id=other(i)[1], device_id_type=MESH)
            return carry

        lax.fori_loop(1, devices, greet, 0)
        for c in range(chunks):
            fetch(c).start()
        group[col] = readings_ref[...]
        sort_blocks(lift, per_y, slab_ref, block_ref, place, mine)
        everyone[me] = mine[me // (devices // 2)]
        pl.semaphore_wait(barrier, devices - 1)

        def send_readings(i, carry):
            pltpu.make_async_remote_copy(
                src_ref=group.at[col], dst_ref=group.at[col], send_sem=group_sems.at[0], recv_sem=group_sems.at[1],
                device_id=(tile, lax.rem(col + i, columns)), device_id_type=MESH,
            ).start()
            return carry

        lax.fori_loop(1, columns, send_readings, 0)

        def send_spots(i, carry):
            number, where = other(i)
            pltpu.make_async_remote_copy(
                src_ref=mine.at[number // (devices // 2)], dst_ref=everyone.at[me],
                send_sem=spots_sems.at[0], recv_sem=spots_sems.at[1], device_id=where, device_id_type=MESH,
            ).start()
            return carry

        lax.fori_loop(1, devices, send_spots, 0)
        wait_all(group, columns - 1, group_sems)
        make_table(group, width, table)

    tiles = group.shape[0] * group.shape[1]
    spots = lax.broadcasted_iota(jnp.int32, (table.shape[1], lanes), 0)
    here = pl.ds(pl.multiple_of(step * lanes, lanes), lanes)
    chosen = jnp.where(rows_ref[:, here] * tiles + tiles_ref[:, here] == spots, 1.0, 0.0).astype(jnp.bfloat16)

    @pl.when(half == 0)
    def arrive():
        pltpu.make_async_copy(sens_ref.at[:, :, here], sens.at[:, :, here], sens_sems.at[step]).wait()

    readings_here = table[pl.ds(pl.multiple_of(half * (share * width), share * width), share * width), :]
    picked[...] = jnp.dot(readings_here, chosen, preferred_element_type=jnp.float32)
    sums = [jnp.zeros((width, lanes), jnp.float32) for _ in range(share)]
    for r in range(width):
        block = sens[r, :, here].astype(jnp.float32)
        for v in range(share):
            sums[v] = sums[v] + block * picked[v * width + r : v * width + r + 1, :]
    for v in range(share):
        made[v * width : (v + 1) * width, here] = sums[v].astype(jnp.bfloat16)

    @pl.when(half == 0)
    def order():
        goal = lax.broadcasted_iota(jnp.int32, (lanes, lanes), 0) + step * lanes
        for o in range(2):
            hits = [jnp.where(place[o, d : d + 1, :] == goal, 1.0, 0.0) for d in range(chunks)]
            moved[o, here, :] = jnp.concatenate(hits, axis=1).astype(jnp.bfloat16)

    @pl.when(step == chunks - 1)
    def send_half():
        middle = devices // 2
        for o in range(2):
            in_y = mine[o] % per_y
            ordered = lax.dot_general(made[...], moved[o], (((1,), (1,)), ((), ())), preferred_element_type=jnp.float32)
            masked = []
            for up in range(stack):
                picks = [part * GROUP + up * beside + k for part in range(chunks // GROUP) for k in range(beside)]
                values = jnp.concatenate([ordered[:, p * lanes : (p + 1) * lanes] for p in picks], axis=1)
                block = jnp.concatenate([in_y[p : p + 1, :] for p in picks], axis=1)
                masked += [jnp.where(block == b, values, 0.0).astype(jnp.bfloat16) for b in meets(o, per_y)]
            sent = jnp.dot(spread_ref[o], jnp.concatenate(masked, axis=0), preferred_element_type=jnp.float32)
            sent = sent.reshape(middle, *outgoing.shape[2:]).astype(jnp.bfloat16)
            outgoing[half, o * middle : (o + 1) * middle] = sent
        for h, target in enumerate(value_refs):

            @pl.when(half == h)
            def send_values():
                pltpu.make_async_copy(outgoing.at[h, me], target.at[me], own_sems.at[h]).start()

                def send(i, carry):
                    number, where = other(i)
                    pltpu.make_async_remote_copy(
                        src_ref=outgoing.at[h, number], dst_ref=target.at[me],
                        send_sem=value_sems.at[h, 0], recv_sem=value_sems.at[h, 1], device_id=where, device_id_type=MESH,
                    ).start()
                    return carry

                lax.fori_loop(1, devices, send, 0)

    @pl.when((half == parts - 1) & (step == chunks - 1))
    def end():
        wait_all(everyone, devices - 1, spots_sems)
        index_tables(everyone, index_ref)
        spots_ref[...] = everyone[...]
        for h, target in enumerate(value_refs):
            pltpu.make_async_copy(outgoing.at[h, me], target.at[me], own_sems.at[h]).wait()
            wait_all(target, devices - 1, value_sems.at[h])


def sort_blocks(lift, per_y, slab_ref, block_ref, place, mine):
    spot_all = slab_ref[...] * lift + block_ref[...]
    chunks, lanes = spot_all.shape
    kept = chunks * lanes
    number = lax.broadcasted_iota(jnp.int32, (chunks, lanes), 0) * lanes + lax.broadcasted_iota(jnp.int32, (chunks, lanes), 1)
    in_y = spot_all % per_y

    def upright(rows):
        return [jnp.broadcast_to(rows[c : c + 1, :], (lanes, lanes)).T for c in range(chunks)]

    for o in range(2):
        away = in_y == per_y // 2 + 1 - o
        spot = jnp.where(away, 3 * NZ * NX * per_y, spot_all)
        bucket = jnp.minimum(spot // (BUCKET * NX * per_y), NZ // BUCKET)
        key = (bucket * kept + number).astype(jnp.float32)
        spot = spot.astype(jnp.float32)
        key_up, spot_up = upright(key), upright(spot)
        ranks = []
        for c in range(chunks):
            line = key[c : c + 1, :]
            total = jnp.zeros((lanes, lanes), jnp.float32)
            for d in range(chunks):
                total = total + jnp.where(key_up[d] < line, 1.0, 0.0)
            ranks.append(jnp.sum(total, axis=0, keepdims=True))
        rank = jnp.concatenate(ranks, axis=0).astype(jnp.int32)
        wide = GROUP * lanes
        found = (rank // wide) * wide + (rank % GROUP) * lanes + (rank // GROUP) % lanes
        place[o] = found
        place_up = upright(found.astype(jnp.float32))
        goal = number.astype(jnp.float32)
        spots = []
        for c in range(chunks):
            line = goal[c : c + 1, :]
            total = jnp.zeros((lanes, lanes), jnp.float32)
            for d in range(chunks):
                total = total + jnp.where(place_up[d] == line, spot_up[d], 0.0)
            spots.append(jnp.sum(total, axis=0, keepdims=True))
        mine[o] = jnp.concatenate(spots, axis=0).astype(jnp.int32)


def make_table(group, width, table):
    sources, share, vectors, readings = group.shape
    lines = [group[i, j].astype(jnp.float32) for i in range(sources) for j in range(share)]
    by_vector = [jnp.concatenate([line[v : v + 1, :] for line in lines], axis=0) for v in range(vectors)]
    rows = []
    for b in range(readings // width):
        rows.append(jnp.concatenate([a[:, b * width : (b + 1) * width] for a in by_vector], axis=1))
    used = sources * share * (readings // width)
    if used < table.shape[1]:
        rows.append(jnp.zeros((table.shape[1] - used, vectors * width), jnp.float32))
    table[...] = jnp.concatenate(rows, axis=0).T.astype(jnp.bfloat16)


def index_tables(all_ref, table_ref):
    sources, chunks, lanes = all_ref.shape
    lane = lax.broadcasted_iota(jnp.int32, (sources, LANES), 1)
    buckets = NZ // BUCKET

    def below(s, low):
        less = jnp.where(all_ref[...] < s * (BUCKET * NX * (NY // 64)), 1.0, 0.0)
        return jnp.where(lane == s, jnp.sum(jnp.sum(less, axis=1), axis=1, keepdims=True), low)

    low = lax.fori_loop(1, buckets + 1, below, jnp.zeros((sources, LANES), jnp.float32)).astype(jnp.int32)
    high = pltpu.roll(low, LANES - 1, 1)
    first = low // GROUP
    counts = jnp.where(high > low, (high + GROUP - 1) // GROUP - first, 0)
    counts = jnp.where(lane < buckets, counts, 0).astype(jnp.float32)
    row = lax.broadcasted_iota(jnp.int32, (sources, sources), 0)
    before = jnp.where(row > lax.broadcasted_iota(jnp.int32, (sources, sources), 1), 1.0, 0.0)
    ahead = jnp.dot(before.astype(jnp.bfloat16), counts.astype(jnp.bfloat16), preferred_element_type=jnp.float32)
    source = lax.broadcasted_iota(jnp.int32, (sources, LANES), 0)
    total = jnp.broadcast_to(jnp.sum(counts, axis=0, keepdims=True), (8, LANES))
    table_ref[:sources, :] = first + source * (chunks * lanes // GROUP)
    table_ref[sources : 2 * sources, :] = ahead.astype(jnp.int32)
    table_ref[2 * sources :, :] = total.astype(jnp.int32)


def model_kernel(
    plan, vectors, slots, table_ref, spots_ref, hx_ref, hz_ref, *refs
):
    sources, chunks, _ = spots_ref.shape
    kept = chunks * LANES
    height = vectors * slots
    parts, _, _, beside = fold(vectors, slots)
    value_refs, (out_ref, index, index_sem, owner, rows_src, merged, left, right, plane, along_y) = refs[:parts], refs[parts:]
    buckets = NZ // BUCKET
    rows = kept // GROUP
    y_share = out_ref.shape[2] // NX
    lead = len(plan) * vectors

    row = lax.broadcasted_iota(jnp.int32, (LANES, LANES), 0)
    eye = jnp.where(row == lax.broadcasted_iota(jnp.int32, (LANES, LANES), 1), 1.0, 0.0).astype(jnp.bfloat16)

    def turned(block):
        return lax.dot_general(eye, block, (((1,), (1,)), ((), ())), preferred_element_type=jnp.float32)

    @pl.when(pl.program_id(0) == 0)
    def scatter():
        fetch = pltpu.make_async_copy(table_ref, index, index_sem)
        fetch.start()
        tail = rows_src.shape[0] - sources * rows
        rows_src[pl.ds(sources * rows, tail), :] = jnp.full((tail, LANES), -1.0, jnp.float32)

        def unpack(src, carry):
            per_y = NY // 64
            spots = spots_ref[src]
            marks = [(spots // per_y) % NX, spots // (NX * per_y), jnp.minimum(spots % per_y, 2)]
            marks = [m.astype(jnp.float32) for m in marks]
            for half in range(rows // LANES):
                tiles = [slice((half * beside + k) * LANES, (half * beside + k + 1) * LANES) for k in range(beside)]
                block = [ref[src, :, lanes] for ref in value_refs for lanes in tiles]
                used = GROUP * height + len(marks) * GROUP
                lines = [m[half * GROUP : (half + 1) * GROUP, :] for m in marks]
                lines.append(jnp.zeros((LANES - used, LANES), jnp.float32))
                block.append(jnp.concatenate(lines, axis=0).astype(jnp.bfloat16))
                place = pl.ds(pl.multiple_of(src * rows + half * LANES, LANES), LANES)
                rows_src[place, :] = turned(jnp.concatenate(block, axis=0))
            return carry

        lax.fori_loop(0, sources, unpack, 0, unroll=4)
        fetch.wait()
        layer = lax.broadcasted_iota(jnp.int32, (BUCKET, LANES), 0).astype(jnp.float32)
        spot = lax.broadcasted_iota(jnp.int32, (NX, LANES), 0).astype(jnp.float32).astype(jnp.bfloat16)
        one, zero = jnp.bfloat16(1.0), jnp.bfloat16(0.0)

        def bucket_step(s, base):
            def merge(i, carry):
                for u in range(MOVES):
                    src = i * MOVES + u
                    to = pl.ds(base * LANES + index[sources + src, s], WINDOW)
                    merged[to, :] = rows_src[pl.ds(index[src, s], WINDOW), :]
                return carry

            lax.fori_loop(0, sources // MOVES, merge, 0)
            count = index[2 * sources, s]
            merged[pl.ds(base * LANES + count, LANES), :] = jnp.full((LANES, LANES), -1.0, jnp.float32)
            tiles = (count + LANES - 1) // LANES

            def name(t, carry):
                owner[base + t] = s
                return carry

            lax.fori_loop(0, tiles, name, 0)
            return base + tiles

        tiles = lax.fori_loop(0, buckets, bucket_step, 0)
        for extra in range(PAIR):
            owner[tiles + extra] = 0
            place = pl.ds(pl.multiple_of((tiles + extra) * LANES, LANES), LANES)
            merged[place, :] = jnp.full((LANES, LANES), -1.0, jnp.float32)
        steps = (tiles + PAIR - 1) // PAIR

        def turn(first):
            block = [merged[pl.ds(first + u * LANES, LANES), :].T for u in range(PAIR)]
            for u in range(PAIR):
                merged[pl.ds(first + u * LANES, LANES), :] = block[u]

        turn(0)
        plane[...] = jnp.zeros_like(plane)
        left[...] = jnp.zeros_like(left)
        right[...] = jnp.zeros_like(right)

        def build(u, t, first):
            here = layer + (owner[t] * BUCKET).astype(jnp.float32)
            for k in range(GROUP):
                columns = slice(k * LANES, (k + 1) * LANES)

                def line(row):
                    return merged[pl.ds(first + row, 1), :]

                x = line(GROUP * height + k)
                code = line(GROUP * height + GROUP + k) + NZ * line(GROUP * height + 2 * GROUP + k)
                marks = [jnp.where(code == here + g * NZ, 1.0, 0.0) for g in range(3)]
                marks = [jnp.concatenate([m, m], axis=0).astype(jnp.bfloat16) for m in marks]
                lines = {}
                for v in range(0, vectors, 2):
                    for slot in range(slots):
                        pair = [line(row_of(k, i, slot, vectors, slots)) for i in (v, v + 1)]
                        pair = [jnp.broadcast_to(row, (BUCKET, LANES)) for row in pair]
                        lines[v, slot] = jnp.concatenate(pair, axis=0).astype(jnp.bfloat16)
                pieces = []
                for _, _, _, slot, group in plan:
                    pieces += [lines[v, slot] * marks[group] for v in range(0, vectors, 2)]
                left[u, :, columns] = jnp.concatenate(pieces, axis=0)
                right[u, :, columns] = jnp.where(x.astype(jnp.bfloat16) == spot, one, zero)

        def tile_step(i, carry):
            first = pl.multiple_of(i * PAIR * LANES, LANES)
            turn(first + PAIR * LANES)
            products = []
            for u in range(PAIR):
                product = lax.dot_general(left[u], right[u], (((1,), (1,)), ((), ())), preferred_element_type=jnp.float32)
                products.append(product.reshape(lead, BUCKET, NX))
            for u in range(PAIR):
                build(u, i * PAIR + u, first + u * LANES)
            for u in range(PAIR):
                s = owner[jnp.maximum((i - 1) * PAIR + u, 0)]
                place = pl.ds(pl.multiple_of(s * BUCKET, BUCKET), BUCKET)
                plane[:, place, :] += products[u]
            return carry

        lax.fori_loop(0, steps + 1, tile_step, 0)

    me = lax.axis_index("tile") * lax.axis_size("col") + lax.axis_index("col")
    v = pl.program_id(0)
    fixed = REST * REST
    for begin in range(0, NZ, STRIP):
        strip = [plane[p * vectors + v, begin : begin + STRIP, :] for p in range(len(plan))]
        strip = jnp.concatenate(strip, axis=0).astype(jnp.bfloat16)
        along_x = jnp.dot(strip, hx_ref[...], preferred_element_type=jnp.float32)
        parts = [along_x[p * STRIP : (p + 1) * STRIP, :] for p in range(len(plan))]
        current = [parts[0] * (fixed * ROOT**LEVELS)]
        taken = 1
        for level in range(LEVELS):
            reach = 2 ** (LEVELS - level)
            held = max(1, y_share // reach)
            scale = fixed * ROOT ** (LEVELS - level)
            details = parts[taken : taken + held]
            taken += held
            if y_share >= reach:
                scaled = [d * scale for d in details]
                current = [e for c, d in zip(current, scaled) for e in (c + d, c - d)]
            else:
                current = [current[0] + details[0] * jnp.where(lax.rem(me * y_share, reach) < reach // 2, scale, -scale)]
        for y in range(y_share):
            along_y[y, begin : begin + STRIP, :] = current[y].astype(jnp.bfloat16)
    for y in range(y_share):
        out_ref[0, :, y * NX : (y + 1) * NX] = jnp.dot(hz_ref[...], along_y[y], preferred_element_type=jnp.float32)


def receive(plan, vectors, slots, y_share, table, values, all_spots):
    sources, chunks, _ = all_spots.shape
    rows = chunks * LANES // GROUP
    hx = jnp.asarray(haar(NX), jnp.bfloat16)
    hz = jnp.asarray(haar(NZ).T, jnp.bfloat16)
    lead = len(plan) * vectors
    most = sources * (rows + NZ // BUCKET)
    most_tiles = most // LANES + NZ // BUCKET + 3 * PAIR

    def whole(array):
        return pl.BlockSpec(array.shape, lambda v: (0,) * array.ndim)

    return pl.pallas_call(
        functools.partial(model_kernel, plan, vectors, slots),
        out_shape=jax.ShapeDtypeStruct((vectors, NZ, y_share * NX), jnp.float32),
        grid=(vectors,),
        in_specs=[pl.BlockSpec(memory_space=pl.ANY), whole(all_spots), whole(hx), whole(hz)] + [whole(v) for v in values],
        out_specs=pl.BlockSpec((1, NZ, y_share * NX), lambda v: (v, 0, 0)),
        scratch_shapes=[
            pltpu.SMEM(table.shape, jnp.int32),
            pltpu.SemaphoreType.DMA,
            pltpu.SMEM((most_tiles,), jnp.int32),
            pltpu.VMEM((sources * rows + WINDOW, LANES), jnp.float32),
            pltpu.VMEM((most_tiles * LANES, LANES), jnp.float32),
            pltpu.VMEM((PAIR, lead * BUCKET, GROUP * LANES), jnp.bfloat16),
            pltpu.VMEM((PAIR, NX, GROUP * LANES), jnp.bfloat16),
            pltpu.VMEM((lead, NZ, NX), jnp.float32),
            pltpu.VMEM((y_share, NZ, NX), jnp.bfloat16),
        ],
        compiler_params=pltpu.CompilerParams(vmem_limit_bytes=60 * 2**20),
    )(table, all_spots, hx, hz, *values)


def on_device(readings, sensitivity, kept_tile, kept_row, kept_slab, kept_block):
    devices = lax.axis_size(AXES)
    columns = lax.axis_size("col")
    kept, width, _ = sensitivity.shape
    vectors = readings.shape[1]
    per_y = NY // width
    layers = NZ // devices
    y_share = NY // devices
    plan, slots = y_plan(y_share, width)
    chunks = kept // LANES
    spread = jnp.asarray(spread_matrix(plan, slots, devices, vectors, width, y_share), jnp.bfloat16)
    used = columns * readings.shape[0] * (readings.shape[2] // width)
    parts, _, _, beside = fold(vectors, slots)
    values = jax.ShapeDtypeStruct((devices, 16, beside * (chunks // GROUP) * LANES), jnp.bfloat16)
    spots = jax.ShapeDtypeStruct((devices, chunks, LANES), jnp.int32)
    index = jax.ShapeDtypeStruct((2 * devices + 8, LANES), jnp.int32)
    hbm = pl.BlockSpec(memory_space=pl.ANY)

    def whole(array):
        return pl.BlockSpec(array.shape, lambda h, i: (0,) * len(array.shape))

    square = jax.ShapeDtypeStruct((chunks, LANES), jnp.int32)
    *values, all_spots, table = pl.pallas_call(
        functools.partial(front_kernel, layers * NX * per_y, slots),
        out_shape=(*[values] * parts, spots, index),
        grid=(parts, chunks),
        in_specs=[
            whole(readings),
            whole(square),
            whole(square),
            pl.BlockSpec((1, kept), lambda h, i: (0, 0)),
            pl.BlockSpec((1, kept), lambda h, i: (0, 0)),
            whole(spread),
            hbm,
        ],
        out_specs=(*[hbm] * parts, whole(spots), whole(index)),
        scratch_shapes=[
            pltpu.VMEM((width, width, kept), jnp.bfloat16),
            pltpu.VMEM((columns, *readings.shape), readings.dtype),
            pltpu.VMEM((2, chunks, LANES), jnp.int32),
            pltpu.VMEM((2, chunks, LANES), jnp.int32),
            pltpu.VMEM(spots.shape, jnp.int32),
            pltpu.VMEM((vectors * width, -(-used // LANES) * LANES), jnp.bfloat16),
            pltpu.VMEM((vectors // parts * width, LANES), jnp.float32),
            pltpu.VMEM((vectors // parts * width, kept), jnp.bfloat16),
            pltpu.VMEM((2, kept, kept), jnp.bfloat16),
            pltpu.VMEM((parts, *values.shape), jnp.bfloat16),
            pltpu.SemaphoreType.DMA((2,)),
            pltpu.SemaphoreType.DMA((2,)),
            pltpu.SemaphoreType.DMA((parts, 2)),
            pltpu.SemaphoreType.DMA((parts,)),
            pltpu.SemaphoreType.DMA((chunks,)),
        ],
        compiler_params=pltpu.CompilerParams(collective_id=0, has_side_effects=True, vmem_limit_bytes=60 * 2**20),
    )(
        readings, kept_slab.reshape(chunks, LANES), kept_block.reshape(chunks, LANES), kept_tile[None, :],
        kept_row[None, :], spread, sensitivity.transpose(1, 2, 0),
    )
    return receive(plan, vectors, slots, y_share, table, values, all_spots)


def solution(mesh):
    return jax.shard_map(
        on_device,
        mesh=mesh,
        in_specs=(
            P(AXES, None, None),
            P(AXES, None, None),
            P(AXES),
            P(AXES),
            P(AXES, None),
            P(AXES),
        ),
        out_specs=P(None, None, AXES),
        check_vma=False,
    )
```

```python
import functools

import jax
import jax.numpy as jnp
import numpy as np
from jax import lax
from jax.experimental import pallas as pl
from jax.experimental.pallas import tpu as pltpu
from jax.sharding import PartitionSpec as P

NX = 256
NY = 256
NZ = 256
LEVELS = 3
ROOT = 0.7071067811865476
LANES = 128
BUCKET = 8
MOVES = 32
PAIR = 3
STRIP = 32
GROUP = 4
CAP = 80
WINDOW = 24
STEPS = (239 / 256, 169 / 256, 239 / 512, 169 / 512)
REST = 256 / 239
AXES = ("tile", "col")


def segments(length):
    coarse = length // 2**LEVELS
    found = [(0, coarse, 2**LEVELS)]
    for level in range(LEVELS):
        found.append((coarse * 2**level, coarse * 2**level, 2 ** (LEVELS - level)))
    return found


def haar(length):
    matrix = np.zeros((length, length), np.float32)
    for number, (start, count, reach) in enumerate(segments(length)):
        for i in range(count):
            half = reach // 2 if number else reach
            matrix[start + i, i * reach : i * reach + half] = STEPS[reach.bit_length() - 1]
            matrix[start + i, i * reach + half : (i + 1) * reach] = -STEPS[reach.bit_length() - 1]
    return matrix


def y_plan(y_share, width):
    rows = []
    used = {}
    for start, count, reach in segments(NY):
        group = min(start // width, 2)
        for i in range(max(1, y_share // reach)):
            slot = used.get(group, 0)
            used[group] = slot + 1
            rows.append((start, reach, i, slot, group))
    return rows, max(used.values())


def fold(vectors, slots):
    parts = 2
    height = vectors // parts * slots
    stack = 16 // height
    return parts, height, stack, GROUP // stack


def row_of(k, v, slot, vectors, slots):
    parts, height, stack, beside = fold(vectors, slots)
    share = vectors // parts
    return ((v // share) * beside + k % beside) * 16 + k // beside * height + v % share * slots + slot


def spread_matrix(plan, slots, devices, vectors, width, y_share):
    per_y = NY // width
    parts, height, stack, _ = fold(vectors, slots)
    share = vectors // parts
    matrix = np.zeros((devices, stack, share, slots, stack, per_y, share, width), np.float32)
    for start, reach, i, slot, _ in plan:
        for owner in range(devices):
            y = start + owner * y_share // reach + i
            for v in range(share):
                for k in range(stack):
                    matrix[owner, k, v, slot, k, y // width, v, y % width] = 1.0
    matrix = matrix.reshape(devices, 16, stack, per_y, share * width)
    halves = np.split(matrix, 2)
    return np.stack([h[:, :, :, meets(o, per_y)].reshape(devices * 8, -1) for o, h in enumerate(halves)])


def meets(half, per_y):
    return list(range(per_y // 2)) + [per_y // 2 + half]


def front_kernel(
    lift, slots, readings_ref, slab_ref, block_ref, tiles_ref, rows_ref, spread_ref, sens_ref,
    *refs,
):
    parts, _, stack, beside = fold(readings_ref.shape[1], slots)
    value_refs, (spots_ref, index_ref, sens, group, place, mine, everyone, table, picked, made, moved, outgoing), sems = (
        refs[:parts], refs[parts : parts + 12], refs[parts + 12 :]
    )
    group_sems, spots_sems, value_sems, own_sems, sens_sems = sems
    width = sens_ref.shape[0]
    columns, _, vectors, readings = group.shape
    devices, chunks, lanes = everyone.shape
    share = vectors // parts
    per_y = NY // width
    half, step = pl.program_id(0), pl.program_id(1)
    tile, col = lax.axis_index("tile"), lax.axis_index("col")
    me = tile * columns + col
    MESH = pl.DeviceIdType.MESH

    def other(i):
        number = lax.rem(me + i, devices)
        return number, (number // columns, lax.rem(number, columns))

    def wait_all(ref, count, sems):
        part = ref.at[pl.ds(0, count)]
        copy = pltpu.make_async_remote_copy(
            src_ref=part, dst_ref=part, send_sem=sems.at[0], recv_sem=sems.at[1], device_id=(tile, col), device_id_type=MESH
        )
        copy.wait_send()
        copy.wait_recv()

    def fetch(c):
        column = pl.ds(c * lanes, lanes)
        return pltpu.make_async_copy(sens_ref.at[:, :, column], sens.at[:, :, column], sens_sems.at[c])

    @pl.when((half == 0) & (step == 0))
    def begin():
        barrier = pltpu.get_barrier_semaphore()

        def greet(i, carry):
            pl.semaphore_signal(barrier, inc=1, device_id=other(i)[1], device_id_type=MESH)
            return carry

        lax.fori_loop(1, devices, greet, 0)
        for c in range(chunks):
            fetch(c).start()
        group[col] = readings_ref[...]
        sort_blocks(lift, per_y, slab_ref, block_ref, place, mine)
        everyone[me] = mine[me // (devices // 2)]
        pl.semaphore_wait(barrier, devices - 1)

        def send_readings(i, carry):
            pltpu.make_async_remote_copy(
                src_ref=group.at[col], dst_ref=group.at[col], send_sem=group_sems.at[0], recv_sem=group_sems.at[1],
                device_id=(tile, lax.rem(col + i, columns)), device_id_type=MESH,
            ).start()
            return carry

        lax.fori_loop(1, columns, send_readings, 0)

        def send_spots(i, carry):
            number, where = other(i)
            pltpu.make_async_remote_copy(
                src_ref=mine.at[number // (devices // 2)], dst_ref=everyone.at[me],
                send_sem=spots_sems.at[0], recv_sem=spots_sems.at[1], device_id=where, device_id_type=MESH,
            ).start()
            return carry

        lax.fori_loop(1, devices, send_spots, 0)
        for o in range(2):

            def order(c, carry):
                goal = lax.broadcasted_iota(jnp.int32, (lanes, lanes), 0) + c * lanes
                hits = [jnp.where(place[o, d : d + 1, :] == goal, 1.0, 0.0) for d in range(chunks)]
                rows = pl.ds(pl.multiple_of(c * lanes, lanes), lanes)
                moved[o, rows, :] = jnp.concatenate(hits, axis=1).astype(jnp.bfloat16)
                return carry

            lax.fori_loop(0, chunks, order, 0)
        wait_all(group, columns - 1, group_sems)
        make_table(group, width, table)

    tiles = group.shape[0] * group.shape[1]
    spots = lax.broadcasted_iota(jnp.int32, (table.shape[1], lanes), 0)
    here = pl.ds(pl.multiple_of(step * lanes, lanes), lanes)
    chosen = jnp.where(rows_ref[:, here] * tiles + tiles_ref[:, here] == spots, 1.0, 0.0).astype(jnp.bfloat16)

    @pl.when(half == 0)
    def arrive():
        pltpu.make_async_copy(sens_ref.at[:, :, here], sens.at[:, :, here], sens_sems.at[step]).wait()

    readings_here = table[pl.ds(pl.multiple_of(half * (share * width), share * width), share * width), :]
    picked[...] = jnp.dot(readings_here, chosen, preferred_element_type=jnp.float32)
    sums = [jnp.zeros((width, lanes), jnp.float32) for _ in range(share)]
    for r in range(width):
        block = sens[r, :, here].astype(jnp.float32)
        for v in range(share):
            sums[v] = sums[v] + block * picked[v * width + r : v * width + r + 1, :]
    for v in range(share):
        made[v * width : (v + 1) * width, here] = sums[v].astype(jnp.bfloat16)

    @pl.when(step == chunks - 1)
    def send_half():
        middle = devices // 2
        for o in range(2):
            in_y = mine[o] % per_y
            ordered = lax.dot_general(made[...], moved[o], (((1,), (1,)), ((), ())), preferred_element_type=jnp.float32)
            masked = []
            for up in range(stack):
                picks = [part * GROUP + up * beside + k for part in range(chunks // GROUP) for k in range(beside)]
                values = jnp.concatenate([ordered[:, p * lanes : (p + 1) * lanes] for p in picks], axis=1)
                block = jnp.concatenate([in_y[p : p + 1, :] for p in picks], axis=1)
                masked += [jnp.where(block == b, values, 0.0).astype(jnp.bfloat16) for b in meets(o, per_y)]
            sent = jnp.dot(spread_ref[o], jnp.concatenate(masked, axis=0), preferred_element_type=jnp.float32)
            sent = sent.reshape(middle, *outgoing.shape[2:]).astype(jnp.bfloat16)
            outgoing[half, o * middle : (o + 1) * middle] = sent
        for h, target in enumerate(value_refs):

            @pl.when(half == h)
            def send_values():
                pltpu.make_async_copy(outgoing.at[h, me], target.at[me], own_sems.at[h]).start()

                def send(i, carry):
                    number, where = other(i)
                    pltpu.make_async_remote_copy(
                        src_ref=outgoing.at[h, number], dst_ref=target.at[me],
                        send_sem=value_sems.at[h, 0], recv_sem=value_sems.at[h, 1], device_id=where, device_id_type=MESH,
                    ).start()
                    return carry

                lax.fori_loop(1, devices, send, 0)

    @pl.when((half == parts - 1) & (step == chunks - 1))
    def end():
        wait_all(everyone, devices - 1, spots_sems)
        index_tables(everyone, index_ref)
        spots_ref[...] = everyone[...]
        for h, target in enumerate(value_refs):
            pltpu.make_async_copy(outgoing.at[h, me], target.at[me], own_sems.at[h]).wait()
            wait_all(target, devices - 1, value_sems.at[h])


def sort_blocks(lift, per_y, slab_ref, block_ref, place, mine):
    spot_all = slab_ref[...] * lift + block_ref[...]
    chunks, lanes = spot_all.shape
    kept = chunks * lanes
    number = lax.broadcasted_iota(jnp.int32, (chunks, lanes), 0) * lanes + lax.broadcasted_iota(jnp.int32, (chunks, lanes), 1)
    in_y = spot_all % per_y

    def upright(rows):
        return [jnp.broadcast_to(rows[c : c + 1, :], (lanes, lanes)).T for c in range(chunks)]

    for o in range(2):
        away = in_y == per_y // 2 + 1 - o
        spot = jnp.where(away, 3 * NZ * NX * per_y, spot_all)
        bucket = jnp.minimum(spot // (BUCKET * NX * per_y), NZ // BUCKET)
        key = (bucket * kept + number).astype(jnp.float32)
        spot = spot.astype(jnp.float32)
        key_up, spot_up = upright(key), upright(spot)
        ranks = []
        for c in range(chunks):
            line = key[c : c + 1, :]
            total = jnp.zeros((lanes, lanes), jnp.float32)
            for d in range(chunks):
                total = total + jnp.where(key_up[d] < line, 1.0, 0.0)
            ranks.append(jnp.sum(total, axis=0, keepdims=True))
        rank = jnp.concatenate(ranks, axis=0).astype(jnp.int32)
        wide = GROUP * lanes
        found = (rank // wide) * wide + (rank % GROUP) * lanes + (rank // GROUP) % lanes
        place[o] = found
        place_up = upright(found.astype(jnp.float32))
        goal = number.astype(jnp.float32)
        spots = []
        for c in range(chunks):
            line = goal[c : c + 1, :]
            total = jnp.zeros((lanes, lanes), jnp.float32)
            for d in range(chunks):
                total = total + jnp.where(place_up[d] == line, spot_up[d], 0.0)
            spots.append(jnp.sum(total, axis=0, keepdims=True))
        mine[o] = jnp.concatenate(spots, axis=0).astype(jnp.int32)


def make_table(group, width, table):
    sources, share, vectors, readings = group.shape
    lines = [group[i, j].astype(jnp.float32) for i in range(sources) for j in range(share)]
    by_vector = [jnp.concatenate([line[v : v + 1, :] for line in lines], axis=0) for v in range(vectors)]
    rows = []
    for b in range(readings // width):
        rows.append(jnp.concatenate([a[:, b * width : (b + 1) * width] for a in by_vector], axis=1))
    used = sources * share * (readings // width)
    if used < table.shape[1]:
        rows.append(jnp.zeros((table.shape[1] - used, vectors * width), jnp.float32))
    table[...] = jnp.concatenate(rows, axis=0).T.astype(jnp.bfloat16)


def index_tables(all_ref, table_ref):
    sources, chunks, lanes = all_ref.shape
    lane = lax.broadcasted_iota(jnp.int32, (sources, LANES), 1)
    buckets = NZ // BUCKET

    def below(s, low):
        less = jnp.where(all_ref[...] < s * (BUCKET * NX * (NY // 64)), 1.0, 0.0)
        return jnp.where(lane == s, jnp.sum(jnp.sum(less, axis=1), axis=1, keepdims=True), low)

    low = lax.fori_loop(1, buckets + 1, below, jnp.zeros((sources, LANES), jnp.float32)).astype(jnp.int32)
    high = pltpu.roll(low, LANES - 1, 1)
    first = low // GROUP
    counts = jnp.where(high > low, (high + GROUP - 1) // GROUP - first, 0)
    counts = jnp.where(lane < buckets, counts, 0).astype(jnp.float32)
    row = lax.broadcasted_iota(jnp.int32, (sources, sources), 0)
    before = jnp.where(row > lax.broadcasted_iota(jnp.int32, (sources, sources), 1), 1.0, 0.0)
    ahead = jnp.dot(before.astype(jnp.bfloat16), counts.astype(jnp.bfloat16), preferred_element_type=jnp.float32)
    source = lax.broadcasted_iota(jnp.int32, (sources, LANES), 0)
    total = jnp.broadcast_to(jnp.sum(counts, axis=0, keepdims=True), (8, LANES))
    table_ref[:sources, :] = first + source * (chunks * lanes // GROUP)
    table_ref[sources : 2 * sources, :] = ahead.astype(jnp.int32)
    table_ref[2 * sources :, :] = total.astype(jnp.int32)


def model_kernel(
    plan, vectors, slots, table_ref, spots_ref, hx_ref, hz_ref, *refs
):
    sources, chunks, _ = spots_ref.shape
    kept = chunks * LANES
    height = vectors * slots
    parts, _, _, beside = fold(vectors, slots)
    value_refs, (out_ref, index, index_sem, owner, rows_src, merged, left, right, plane, along_y, ready, out_sems) = refs[:parts], refs[parts:]
    buckets = NZ // BUCKET
    rows = kept // GROUP
    y_share = out_ref.shape[2] // NX
    lead = len(plan) * vectors

    row = lax.broadcasted_iota(jnp.int32, (LANES, LANES), 0)
    eye = jnp.where(row == lax.broadcasted_iota(jnp.int32, (LANES, LANES), 1), 1.0, 0.0).astype(jnp.bfloat16)

    def turned(block):
        return lax.dot_general(eye, block, (((1,), (1,)), ((), ())), preferred_element_type=jnp.float32)

    def scatter():
        fetch = pltpu.make_async_copy(table_ref, index, index_sem)
        fetch.start()
        tail = rows_src.shape[0] - sources * rows
        rows_src[pl.ds(sources * rows, tail), :] = jnp.full((tail, LANES), -1.0, jnp.float32)

        def unpack(src, carry):
            per_y = NY // 64
            spots = spots_ref[src]
            marks = [(spots // per_y) % NX, spots // (NX * per_y), jnp.minimum(spots % per_y, 2)]
            marks = [m.astype(jnp.float32) for m in marks]
            for half in range(rows // LANES):
                tiles = [slice((half * beside + k) * LANES, (half * beside + k + 1) * LANES) for k in range(beside)]
                block = [ref[src, :, lanes] for ref in value_refs for lanes in tiles]
                used = GROUP * height + len(marks) * GROUP
                lines = [m[half * GROUP : (half + 1) * GROUP, :] for m in marks]
                lines.append(jnp.zeros((LANES - used, LANES), jnp.float32))
                block.append(jnp.concatenate(lines, axis=0).astype(jnp.bfloat16))
                place = pl.ds(pl.multiple_of(src * rows + half * LANES, LANES), LANES)
                rows_src[place, :] = turned(jnp.concatenate(block, axis=0))
            return carry

        lax.fori_loop(0, sources, unpack, 0, unroll=4)
        fetch.wait()
        layer = lax.broadcasted_iota(jnp.int32, (BUCKET, LANES), 0).astype(jnp.float32)
        spot = lax.broadcasted_iota(jnp.int32, (NX, LANES), 0).astype(jnp.float32).astype(jnp.bfloat16)
        one, zero = jnp.bfloat16(1.0), jnp.bfloat16(0.0)

        def bucket_step(s, base):
            def merge(i, carry):
                for u in range(MOVES):
                    src = i * MOVES + u
                    to = pl.ds(base * LANES + index[sources + src, s], WINDOW)
                    merged[to, :] = rows_src[pl.ds(index[src, s], WINDOW), :]
                return carry

            lax.fori_loop(0, sources // MOVES, merge, 0)
            count = index[2 * sources, s]
            merged[pl.ds(base * LANES + count, LANES), :] = jnp.full((LANES, LANES), -1.0, jnp.float32)
            tiles = (count + LANES - 1) // LANES

            def name(t, carry):
                owner[base + t] = s
                return carry

            lax.fori_loop(0, tiles, name, 0)
            return base + tiles

        tiles = lax.fori_loop(0, buckets, bucket_step, 0)
        for extra in range(PAIR):
            owner[tiles + extra] = 0
            place = pl.ds(pl.multiple_of((tiles + extra) * LANES, LANES), LANES)
            merged[place, :] = jnp.full((LANES, LANES), -1.0, jnp.float32)
        steps = (tiles + PAIR - 1) // PAIR

        def turn(first):
            block = [merged[pl.ds(first + u * LANES, LANES), :].T for u in range(PAIR)]
            for u in range(PAIR):
                merged[pl.ds(first + u * LANES, LANES), :] = block[u]

        turn(0)
        plane[...] = jnp.zeros_like(plane)
        left[...] = jnp.zeros_like(left)
        right[...] = jnp.zeros_like(right)

        def build(u, t, first):
            here = layer + (owner[t] * BUCKET).astype(jnp.float32)
            for k in range(GROUP):
                columns = slice(k * LANES, (k + 1) * LANES)

                def line(row):
                    return merged[pl.ds(first + row, 1), :]

                x = line(GROUP * height + k)
                code = line(GROUP * height + GROUP + k) + NZ * line(GROUP * height + 2 * GROUP + k)
                marks = [jnp.where(code == here + g * NZ, 1.0, 0.0) for g in range(3)]
                marks = [jnp.concatenate([m, m], axis=0).astype(jnp.bfloat16) for m in marks]
                lines = {}
                for v in range(0, vectors, 2):
                    for slot in range(slots):
                        pair = [line(row_of(k, i, slot, vectors, slots)) for i in (v, v + 1)]
                        pair = [jnp.broadcast_to(row, (BUCKET, LANES)) for row in pair]
                        lines[v, slot] = jnp.concatenate(pair, axis=0).astype(jnp.bfloat16)
                pieces = []
                for _, _, _, slot, group in plan:
                    pieces += [lines[v, slot] * marks[group] for v in range(0, vectors, 2)]
                left[u, :, columns] = jnp.concatenate(pieces, axis=0)
                right[u, :, columns] = jnp.where(x.astype(jnp.bfloat16) == spot, one, zero)

        def tile_step(i, carry):
            first = pl.multiple_of(i * PAIR * LANES, LANES)
            turn(first + PAIR * LANES)
            products = []
            for u in range(PAIR):
                product = lax.dot_general(left[u], right[u], (((1,), (1,)), ((), ())), preferred_element_type=jnp.float32)
                products.append(product.reshape(lead, BUCKET, NX))
            for u in range(PAIR):
                build(u, i * PAIR + u, first + u * LANES)
            for u in range(PAIR):
                s = owner[jnp.maximum((i - 1) * PAIR + u, 0)]
                place = pl.ds(pl.multiple_of(s * BUCKET, BUCKET), BUCKET)
                plane[:, place, :] += products[u]
            return carry

        lax.fori_loop(0, steps + 1, tile_step, 0)

    me = lax.axis_index("tile") * lax.axis_size("col") + lax.axis_index("col")
    scatter()
    fixed = REST * REST
    depths = NZ // 2

    def send_out(v, j):
        deep = pl.ds(j * depths, depths)
        return pltpu.make_async_copy(ready.at[v, deep, :], out_ref.at[v, deep, :], out_sems.at[v, j])

    def finish(v, carry):
        for begin in range(0, NZ, STRIP):
            strip = [plane[p * vectors + v, begin : begin + STRIP, :] for p in range(len(plan))]
            strip = jnp.concatenate(strip, axis=0).astype(jnp.bfloat16)
            along_x = jnp.dot(strip, hx_ref[...], preferred_element_type=jnp.float32)
            parts = [along_x[p * STRIP : (p + 1) * STRIP, :] for p in range(len(plan))]
            current = [parts[0] * (fixed * ROOT**LEVELS)]
            taken = 1
            for level in range(LEVELS):
                reach = 2 ** (LEVELS - level)
                held = max(1, y_share // reach)
                scale = fixed * ROOT ** (LEVELS - level)
                details = parts[taken : taken + held]
                taken += held
                if y_share >= reach:
                    scaled = [d * scale for d in details]
                    current = [e for c, d in zip(current, scaled) for e in (c + d, c - d)]
                else:
                    current = [current[0] + details[0] * jnp.where(lax.rem(me * y_share, reach) < reach // 2, scale, -scale)]
            for y in range(y_share):
                along_y[y, begin : begin + STRIP, :] = current[y].astype(jnp.bfloat16)
        for j in range(2):
            deep = slice(j * depths, (j + 1) * depths)
            for y in range(y_share):
                ready[v, deep, y * NX : (y + 1) * NX] = jnp.dot(
                    hz_ref[deep, :], along_y[y], preferred_element_type=jnp.float32
                )
            send_out(v, j).start()
        return carry

    lax.fori_loop(0, vectors, finish, 0)
    for v in range(vectors):
        for j in range(2):
            send_out(v, j).wait()


def receive(plan, vectors, slots, y_share, table, values, all_spots):
    sources, chunks, _ = all_spots.shape
    rows = chunks * LANES // GROUP
    hx = jnp.asarray(haar(NX), jnp.bfloat16)
    hz = jnp.asarray(haar(NZ).T, jnp.bfloat16)
    lead = len(plan) * vectors
    most = sources * (rows + NZ // BUCKET)
    most_tiles = most // LANES + NZ // BUCKET + 3 * PAIR

    vmem, hbm = pl.BlockSpec(memory_space=pltpu.VMEM), pl.BlockSpec(memory_space=pl.ANY)
    return pl.pallas_call(
        functools.partial(model_kernel, plan, vectors, slots),
        out_shape=jax.ShapeDtypeStruct((vectors, NZ, y_share * NX), jnp.float32),
        in_specs=[hbm] + [vmem] * (3 + len(values)),
        out_specs=hbm,
        scratch_shapes=[
            pltpu.SMEM(table.shape, jnp.int32),
            pltpu.SemaphoreType.DMA,
            pltpu.SMEM((most_tiles,), jnp.int32),
            pltpu.VMEM((sources * rows + WINDOW, LANES), jnp.float32),
            pltpu.VMEM((most_tiles * LANES, LANES), jnp.float32),
            pltpu.VMEM((PAIR, lead * BUCKET, GROUP * LANES), jnp.bfloat16),
            pltpu.VMEM((PAIR, NX, GROUP * LANES), jnp.bfloat16),
            pltpu.VMEM((lead, NZ, NX), jnp.float32),
            pltpu.VMEM((y_share, NZ, NX), jnp.bfloat16),
            pltpu.VMEM((vectors, NZ, y_share * NX), jnp.float32),
            pltpu.SemaphoreType.DMA((vectors, 2)),
        ],
        compiler_params=pltpu.CompilerParams(vmem_limit_bytes=60 * 2**20),
    )(table, all_spots, hx, hz, *values)


def on_device(readings, sensitivity, kept_tile, kept_row, kept_slab, kept_block):
    devices = lax.axis_size(AXES)
    columns = lax.axis_size("col")
    kept, width, _ = sensitivity.shape
    vectors = readings.shape[1]
    per_y = NY // width
    layers = NZ // devices
    y_share = NY // devices
    plan, slots = y_plan(y_share, width)
    chunks = kept // LANES
    spread = jnp.asarray(spread_matrix(plan, slots, devices, vectors, width, y_share), jnp.bfloat16)
    used = columns * readings.shape[0] * (readings.shape[2] // width)
    parts, _, _, beside = fold(vectors, slots)
    values = jax.ShapeDtypeStruct((devices, 16, beside * (chunks // GROUP) * LANES), jnp.bfloat16)
    spots = jax.ShapeDtypeStruct((devices, chunks, LANES), jnp.int32)
    index = jax.ShapeDtypeStruct((2 * devices + 8, LANES), jnp.int32)
    hbm = pl.BlockSpec(memory_space=pl.ANY)

    def whole(array):
        return pl.BlockSpec(array.shape, lambda h, i: (0,) * len(array.shape))

    square = jax.ShapeDtypeStruct((chunks, LANES), jnp.int32)
    *values, all_spots, table = pl.pallas_call(
        functools.partial(front_kernel, layers * NX * per_y, slots),
        out_shape=(*[values] * parts, spots, index),
        grid=(parts, chunks),
        in_specs=[
            whole(readings),
            whole(square),
            whole(square),
            pl.BlockSpec((1, kept), lambda h, i: (0, 0)),
            pl.BlockSpec((1, kept), lambda h, i: (0, 0)),
            whole(spread),
            hbm,
        ],
        out_specs=(*[hbm] * parts, whole(spots), whole(index)),
        scratch_shapes=[
            pltpu.VMEM((width, width, kept), jnp.bfloat16),
            pltpu.VMEM((columns, *readings.shape), readings.dtype),
            pltpu.VMEM((2, chunks, LANES), jnp.int32),
            pltpu.VMEM((2, chunks, LANES), jnp.int32),
            pltpu.VMEM(spots.shape, jnp.int32),
            pltpu.VMEM((vectors * width, -(-used // LANES) * LANES), jnp.bfloat16),
            pltpu.VMEM((vectors // parts * width, LANES), jnp.float32),
            pltpu.VMEM((vectors // parts * width, kept), jnp.bfloat16),
            pltpu.VMEM((2, kept, kept), jnp.bfloat16),
            pltpu.VMEM((parts, *values.shape), jnp.bfloat16),
            pltpu.SemaphoreType.DMA((2,)),
            pltpu.SemaphoreType.DMA((2,)),
            pltpu.SemaphoreType.DMA((parts, 2)),
            pltpu.SemaphoreType.DMA((parts,)),
            pltpu.SemaphoreType.DMA((chunks,)),
        ],
        compiler_params=pltpu.CompilerParams(collective_id=0, has_side_effects=True, vmem_limit_bytes=60 * 2**20),
    )(
        readings, kept_slab.reshape(chunks, LANES), kept_block.reshape(chunks, LANES), kept_tile[None, :],
        kept_row[None, :], spread, sensitivity.transpose(1, 2, 0),
    )
    return receive(plan, vectors, slots, y_share, table, values, all_spots)


def solution(mesh):
    return jax.shard_map(
        on_device,
        mesh=mesh,
        in_specs=(
            P(AXES, None, None),
            P(AXES, None, None),
            P(AXES),
            P(AXES),
            P(AXES, None),
            P(AXES),
        ),
        out_specs=P(None, None, AXES),
        check_vma=False,
    )
```

```python
import functools

import jax
import jax.numpy as jnp
import numpy as np
from jax import lax
from jax.experimental import pallas as pl
from jax.experimental.pallas import tpu as pltpu
from jax.sharding import PartitionSpec as P

NX = 256
NY = 256
NZ = 256
LEVELS = 3
ROOT = 0.7071067811865476
LANES = 128
BUCKET = 8
MOVES = 32
PAIR = 3
STRIP = 32
GROUP = 4
CAP = 80
WINDOW = 24
STEPS = (239 / 256, 169 / 256, 239 / 512, 169 / 512)
REST = 256 / 239
AXES = ("tile", "col")


def segments(length):
    coarse = length // 2**LEVELS
    found = [(0, coarse, 2**LEVELS)]
    for level in range(LEVELS):
        found.append((coarse * 2**level, coarse * 2**level, 2 ** (LEVELS - level)))
    return found


def haar(length):
    matrix = np.zeros((length, length), np.float32)
    for number, (start, count, reach) in enumerate(segments(length)):
        for i in range(count):
            half = reach // 2 if number else reach
            matrix[start + i, i * reach : i * reach + half] = STEPS[reach.bit_length() - 1]
            matrix[start + i, i * reach + half : (i + 1) * reach] = -STEPS[reach.bit_length() - 1]
    return matrix


def y_plan(y_share, width):
    rows = []
    used = {}
    for start, count, reach in segments(NY):
        group = min(start // width, 2)
        for i in range(max(1, y_share // reach)):
            slot = used.get(group, 0)
            used[group] = slot + 1
            rows.append((start, reach, i, slot, group))
    return rows, max(used.values())


def fold(vectors, slots):
    parts = 2
    height = vectors // parts * slots
    stack = 16 // height
    return parts, height, stack, GROUP // stack


def row_of(k, v, slot, vectors, slots):
    parts, height, stack, beside = fold(vectors, slots)
    share = vectors // parts
    return ((v // share) * beside + k % beside) * 16 + k // beside * height + v % share * slots + slot


def spread_matrix(plan, slots, devices, vectors, width, y_share):
    per_y = NY // width
    parts, height, stack, _ = fold(vectors, slots)
    share = vectors // parts
    matrix = np.zeros((devices, stack, share, slots, stack, per_y, share, width), np.float32)
    for start, reach, i, slot, _ in plan:
        for owner in range(devices):
            y = start + owner * y_share // reach + i
            for v in range(share):
                for k in range(stack):
                    matrix[owner, k, v, slot, k, y // width, v, y % width] = 1.0
    matrix = matrix.reshape(devices, 16, stack, per_y, share * width)
    halves = np.split(matrix, 2)
    return np.stack([h[:, :, :, meets(o, per_y)].reshape(devices * 8, -1) for o, h in enumerate(halves)])


def meets(half, per_y):
    return list(range(per_y // 2)) + [per_y // 2 + half]


def front_kernel(
    lift, slots, readings_ref, slab_ref, block_ref, tiles_ref, rows_ref, spread_ref, sens_ref,
    *refs,
):
    parts, _, stack, beside = fold(readings_ref.shape[1], slots)
    value_refs, (spots_ref, index_ref, sens, group, place, mine, everyone, table, picked, made, moved, outgoing), sems = (
        refs[:parts], refs[parts : parts + 12], refs[parts + 12 :]
    )
    group_sems, spots_sems, value_sems, own_sems, sens_sems = sems
    width = sens_ref.shape[0]
    columns, _, vectors, readings = group.shape
    devices, chunks, lanes = everyone.shape
    share = vectors // parts
    per_y = NY // width
    tile, col = lax.axis_index("tile"), lax.axis_index("col")
    me = tile * columns + col
    MESH = pl.DeviceIdType.MESH

    def other(i):
        number = lax.rem(me + i, devices)
        return number, (number // columns, lax.rem(number, columns))

    def wait_all(ref, count, sems):
        part = ref.at[pl.ds(0, count)]
        copy = pltpu.make_async_remote_copy(
            src_ref=part, dst_ref=part, send_sem=sems.at[0], recv_sem=sems.at[1], device_id=(tile, col), device_id_type=MESH
        )
        copy.wait_send()
        copy.wait_recv()

    def fetch(c):
        column = pl.ds(c * lanes, lanes)
        return pltpu.make_async_copy(sens_ref.at[:, :, column], sens.at[:, :, column], sens_sems.at[c])

    def begin():
        barrier = pltpu.get_barrier_semaphore()

        def greet(i, carry):
            pl.semaphore_signal(barrier, inc=1, device_id=other(i)[1], device_id_type=MESH)
            return carry

        lax.fori_loop(1, devices, greet, 0)
        for c in range(chunks):
            fetch(c).start()
        group[col] = readings_ref[...]
        sort_blocks(lift, per_y, slab_ref, block_ref, place, mine)
        everyone[me] = mine[me // (devices // 2)]
        pl.semaphore_wait(barrier, devices - 1)

        def send_readings(i, carry):
            pltpu.make_async_remote_copy(
                src_ref=group.at[col], dst_ref=group.at[col], send_sem=group_sems.at[0], recv_sem=group_sems.at[1],
                device_id=(tile, lax.rem(col + i, columns)), device_id_type=MESH,
            ).start()
            return carry

        lax.fori_loop(1, columns, send_readings, 0)

        def send_spots(i, carry):
            number, where = other(i)
            pltpu.make_async_remote_copy(
                src_ref=mine.at[number // (devices // 2)], dst_ref=everyone.at[me],
                send_sem=spots_sems.at[0], recv_sem=spots_sems.at[1], device_id=where, device_id_type=MESH,
            ).start()
            return carry

        lax.fori_loop(1, devices, send_spots, 0)
        for o in range(2):

            def order(c, carry):
                goal = lax.broadcasted_iota(jnp.int32, (lanes, lanes), 0) + c * lanes
                hits = [jnp.where(place[o, d : d + 1, :] == goal, 1.0, 0.0) for d in range(chunks)]
                rows = pl.ds(pl.multiple_of(c * lanes, lanes), lanes)
                moved[o, rows, :] = jnp.concatenate(hits, axis=1).astype(jnp.bfloat16)
                return carry

            lax.fori_loop(0, chunks, order, 0)
        wait_all(group, columns - 1, group_sems)
        make_table(group, width, table)

    def make(half, step):
        tiles = group.shape[0] * group.shape[1]
        spots = lax.broadcasted_iota(jnp.int32, (table.shape[1], lanes), 0)
        here = pl.ds(pl.multiple_of(step * lanes, lanes), lanes)
        chosen = jnp.where(rows_ref[:, here] * tiles + tiles_ref[:, here] == spots, 1.0, 0.0).astype(jnp.bfloat16)

        if half == 0:
            pltpu.make_async_copy(sens_ref.at[:, :, here], sens.at[:, :, here], sens_sems.at[step]).wait()
        readings_here = table[pl.ds(pl.multiple_of(half * (share * width), share * width), share * width), :]
        picked[...] = jnp.dot(readings_here, chosen, preferred_element_type=jnp.float32)
        sums = [jnp.zeros((width, lanes), jnp.float32) for _ in range(share)]
        for r in range(width):
            block = sens[r, :, here].astype(jnp.float32)
            for v in range(share):
                sums[v] = sums[v] + block * picked[v * width + r : v * width + r + 1, :]
        for v in range(share):
            made[v * width : (v + 1) * width, here] = sums[v].astype(jnp.bfloat16)

    def send_half(half):
        middle = devices // 2
        for o in range(2):
            in_y = mine[o] % per_y
            ordered = lax.dot_general(made[...], moved[o], (((1,), (1,)), ((), ())), preferred_element_type=jnp.float32)
            masked = []
            for up in range(stack):
                picks = [part * GROUP + up * beside + k for part in range(chunks // GROUP) for k in range(beside)]
                values = jnp.concatenate([ordered[:, p * lanes : (p + 1) * lanes] for p in picks], axis=1)
                block = jnp.concatenate([in_y[p : p + 1, :] for p in picks], axis=1)
                masked += [jnp.where(block == b, values, 0.0).astype(jnp.bfloat16) for b in meets(o, per_y)]
            sent = jnp.dot(spread_ref[o], jnp.concatenate(masked, axis=0), preferred_element_type=jnp.float32)
            sent = sent.reshape(middle, *outgoing.shape[2:]).astype(jnp.bfloat16)
            outgoing[half, o * middle : (o + 1) * middle] = sent
        target = value_refs[half]
        pltpu.make_async_copy(outgoing.at[half, me], target.at[me], own_sems.at[half]).start()

        def send(i, carry):
            number, where = other(i)
            pltpu.make_async_remote_copy(
                src_ref=outgoing.at[half, number], dst_ref=target.at[me],
                send_sem=value_sems.at[half, 0], recv_sem=value_sems.at[half, 1], device_id=where, device_id_type=MESH,
            ).start()
            return carry

        lax.fori_loop(1, devices, send, 0)

    def end():
        wait_all(everyone, devices - 1, spots_sems)
        index_tables(everyone, index_ref)
        spots_ref[...] = everyone[...]
        for h, target in enumerate(value_refs):
            pltpu.make_async_copy(outgoing.at[h, me], target.at[me], own_sems.at[h]).wait()
            wait_all(target, devices - 1, value_sems.at[h])

    begin()
    for half in range(parts):

        def product_step(step, carry, half=half):
            make(half, step)
            return carry

        lax.fori_loop(0, chunks, product_step, 0)
        send_half(half)
    end()


def sort_blocks(lift, per_y, slab_ref, block_ref, place, mine):
    spot_all = slab_ref[...] * lift + block_ref[...]
    chunks, lanes = spot_all.shape
    kept = chunks * lanes
    number = lax.broadcasted_iota(jnp.int32, (chunks, lanes), 0) * lanes + lax.broadcasted_iota(jnp.int32, (chunks, lanes), 1)
    in_y = spot_all % per_y

    def upright(rows):
        return [jnp.broadcast_to(rows[c : c + 1, :], (lanes, lanes)).T for c in range(chunks)]

    for o in range(2):
        away = in_y == per_y // 2 + 1 - o
        spot = jnp.where(away, 3 * NZ * NX * per_y, spot_all)
        bucket = jnp.minimum(spot // (BUCKET * NX * per_y), NZ // BUCKET)
        key = (bucket * kept + number).astype(jnp.float32)
        spot = spot.astype(jnp.float32)
        key_up, spot_up = upright(key), upright(spot)
        ranks = []
        for c in range(chunks):
            line = key[c : c + 1, :]
            total = jnp.zeros((lanes, lanes), jnp.float32)
            for d in range(chunks):
                total = total + jnp.where(key_up[d] < line, 1.0, 0.0)
            ranks.append(jnp.sum(total, axis=0, keepdims=True))
        rank = jnp.concatenate(ranks, axis=0).astype(jnp.int32)
        wide = GROUP * lanes
        found = (rank // wide) * wide + (rank % GROUP) * lanes + (rank // GROUP) % lanes
        place[o] = found
        place_up = upright(found.astype(jnp.float32))
        goal = number.astype(jnp.float32)
        spots = []
        for c in range(chunks):
            line = goal[c : c + 1, :]
            total = jnp.zeros((lanes, lanes), jnp.float32)
            for d in range(chunks):
                total = total + jnp.where(place_up[d] == line, spot_up[d], 0.0)
            spots.append(jnp.sum(total, axis=0, keepdims=True))
        mine[o] = jnp.concatenate(spots, axis=0).astype(jnp.int32)


def make_table(group, width, table):
    sources, share, vectors, readings = group.shape
    lines = [group[i, j].astype(jnp.float32) for i in range(sources) for j in range(share)]
    by_vector = [jnp.concatenate([line[v : v + 1, :] for line in lines], axis=0) for v in range(vectors)]
    rows = []
    for b in range(readings // width):
        rows.append(jnp.concatenate([a[:, b * width : (b + 1) * width] for a in by_vector], axis=1))
    used = sources * share * (readings // width)
    if used < table.shape[1]:
        rows.append(jnp.zeros((table.shape[1] - used, vectors * width), jnp.float32))
    table[...] = jnp.concatenate(rows, axis=0).T.astype(jnp.bfloat16)


def index_tables(all_ref, table_ref):
    sources, chunks, lanes = all_ref.shape
    lane = lax.broadcasted_iota(jnp.int32, (sources, LANES), 1)
    buckets = NZ // BUCKET

    def below(s, low):
        less = jnp.where(all_ref[...] < s * (BUCKET * NX * (NY // 64)), 1.0, 0.0)
        return jnp.where(lane == s, jnp.sum(jnp.sum(less, axis=1), axis=1, keepdims=True), low)

    low = lax.fori_loop(1, buckets + 1, below, jnp.zeros((sources, LANES), jnp.float32)).astype(jnp.int32)
    high = pltpu.roll(low, LANES - 1, 1)
    first = low // GROUP
    counts = jnp.where(high > low, (high + GROUP - 1) // GROUP - first, 0)
    counts = jnp.where(lane < buckets, counts, 0).astype(jnp.float32)
    row = lax.broadcasted_iota(jnp.int32, (sources, sources), 0)
    before = jnp.where(row > lax.broadcasted_iota(jnp.int32, (sources, sources), 1), 1.0, 0.0)
    ahead = jnp.dot(before.astype(jnp.bfloat16), counts.astype(jnp.bfloat16), preferred_element_type=jnp.float32)
    source = lax.broadcasted_iota(jnp.int32, (sources, LANES), 0)
    total = jnp.broadcast_to(jnp.sum(counts, axis=0, keepdims=True), (8, LANES))
    table_ref[:sources, :] = first + source * (chunks * lanes // GROUP)
    table_ref[sources : 2 * sources, :] = ahead.astype(jnp.int32)
    table_ref[2 * sources :, :] = total.astype(jnp.int32)


def model_kernel(
    plan, vectors, slots, table_ref, spots_ref, hx_ref, hz_ref, *refs
):
    sources, chunks, _ = spots_ref.shape
    kept = chunks * LANES
    height = vectors * slots
    parts, _, _, beside = fold(vectors, slots)
    value_refs, (out_ref, index, index_sem, owner, rows_src, merged, left, right, plane, along_y, ready, out_sems) = refs[:parts], refs[parts:]
    buckets = NZ // BUCKET
    rows = kept // GROUP
    y_share = out_ref.shape[2] // NX
    lead = len(plan) * vectors

    row = lax.broadcasted_iota(jnp.int32, (LANES, LANES), 0)
    eye = jnp.where(row == lax.broadcasted_iota(jnp.int32, (LANES, LANES), 1), 1.0, 0.0).astype(jnp.bfloat16)

    def turned(block):
        return lax.dot_general(eye, block, (((1,), (1,)), ((), ())), preferred_element_type=jnp.float32)

    def scatter():
        fetch = pltpu.make_async_copy(table_ref, index, index_sem)
        fetch.start()
        tail = rows_src.shape[0] - sources * rows
        rows_src[pl.ds(sources * rows, tail), :] = jnp.full((tail, LANES), -1.0, jnp.float32)

        def unpack(src, carry):
            per_y = NY // 64
            spots = spots_ref[src]
            marks = [(spots // per_y) % NX, spots // (NX * per_y), jnp.minimum(spots % per_y, 2)]
            marks = [m.astype(jnp.float32) for m in marks]
            for half in range(rows // LANES):
                tiles = [slice((half * beside + k) * LANES, (half * beside + k + 1) * LANES) for k in range(beside)]
                block = [ref[src, :, lanes] for ref in value_refs for lanes in tiles]
                used = GROUP * height + len(marks) * GROUP
                lines = [m[half * GROUP : (half + 1) * GROUP, :] for m in marks]
                lines.append(jnp.zeros((LANES - used, LANES), jnp.float32))
                block.append(jnp.concatenate(lines, axis=0).astype(jnp.bfloat16))
                place = pl.ds(pl.multiple_of(src * rows + half * LANES, LANES), LANES)
                rows_src[place, :] = turned(jnp.concatenate(block, axis=0))
            return carry

        lax.fori_loop(0, sources, unpack, 0, unroll=4)
        fetch.wait()
        layer = lax.broadcasted_iota(jnp.int32, (BUCKET, LANES), 0).astype(jnp.float32)
        spot = lax.broadcasted_iota(jnp.int32, (NX, LANES), 0).astype(jnp.float32).astype(jnp.bfloat16)
        one, zero = jnp.bfloat16(1.0), jnp.bfloat16(0.0)

        def bucket_step(s, base):
            def merge(i, carry):
                for u in range(MOVES):
                    src = i * MOVES + u
                    to = pl.ds(base * LANES + index[sources + src, s], WINDOW)
                    merged[to, :] = rows_src[pl.ds(index[src, s], WINDOW), :]
                return carry

            lax.fori_loop(0, sources // MOVES, merge, 0)
            count = index[2 * sources, s]
            merged[pl.ds(base * LANES + count, LANES), :] = jnp.full((LANES, LANES), -1.0, jnp.float32)
            tiles = (count + LANES - 1) // LANES

            def name(t, carry):
                owner[base + t] = s
                return carry

            lax.fori_loop(0, tiles, name, 0)
            return base + tiles

        tiles = lax.fori_loop(0, buckets, bucket_step, 0)
        for extra in range(PAIR):
            owner[tiles + extra] = 0
            place = pl.ds(pl.multiple_of((tiles + extra) * LANES, LANES), LANES)
            merged[place, :] = jnp.full((LANES, LANES), -1.0, jnp.float32)
        steps = (tiles + PAIR - 1) // PAIR

        def turn(first):
            block = [merged[pl.ds(first + u * LANES, LANES), :].T for u in range(PAIR)]
            for u in range(PAIR):
                merged[pl.ds(first + u * LANES, LANES), :] = block[u]

        turn(0)
        plane[...] = jnp.zeros_like(plane)
        left[...] = jnp.zeros_like(left)
        right[...] = jnp.zeros_like(right)

        def build(u, t, first):
            here = layer + (owner[t] * BUCKET).astype(jnp.float32)
            for k in range(GROUP):
                columns = slice(k * LANES, (k + 1) * LANES)

                def line(row):
                    return merged[pl.ds(first + row, 1), :]

                x = line(GROUP * height + k)
                code = line(GROUP * height + GROUP + k) + NZ * line(GROUP * height + 2 * GROUP + k)
                marks = [jnp.where(code == here + g * NZ, 1.0, 0.0) for g in range(3)]
                marks = [jnp.concatenate([m, m], axis=0).astype(jnp.bfloat16) for m in marks]
                lines = {}
                for v in range(0, vectors, 2):
                    for slot in range(slots):
                        pair = [line(row_of(k, i, slot, vectors, slots)) for i in (v, v + 1)]
                        pair = [jnp.broadcast_to(row, (BUCKET, LANES)) for row in pair]
                        lines[v, slot] = jnp.concatenate(pair, axis=0).astype(jnp.bfloat16)
                pieces = []
                for _, _, _, slot, group in plan:
                    pieces += [lines[v, slot] * marks[group] for v in range(0, vectors, 2)]
                left[u, :, columns] = jnp.concatenate(pieces, axis=0)
                right[u, :, columns] = jnp.where(x.astype(jnp.bfloat16) == spot, one, zero)

        def tile_step(i, carry):
            first = pl.multiple_of(i * PAIR * LANES, LANES)
            turn(first + PAIR * LANES)
            products = []
            for u in range(PAIR):
                product = lax.dot_general(left[u], right[u], (((1,), (1,)), ((), ())), preferred_element_type=jnp.float32)
                products.append(product.reshape(lead, BUCKET, NX))
            for u in range(PAIR):
                build(u, i * PAIR + u, first + u * LANES)
            for u in range(PAIR):
                s = owner[jnp.maximum((i - 1) * PAIR + u, 0)]
                place = pl.ds(pl.multiple_of(s * BUCKET, BUCKET), BUCKET)
                plane[:, place, :] += products[u]
            return carry

        lax.fori_loop(0, steps + 1, tile_step, 0)

    me = lax.axis_index("tile") * lax.axis_size("col") + lax.axis_index("col")
    scatter()
    fixed = REST * REST
    depths = NZ // 2

    def send_out(v, j):
        deep = pl.ds(j * depths, depths)
        return pltpu.make_async_copy(ready.at[v, deep, :], out_ref.at[v, deep, :], out_sems.at[v, j])

    def finish(v, carry):
        for begin in range(0, NZ, STRIP):
            strip = [plane[p * vectors + v, begin : begin + STRIP, :] for p in range(len(plan))]
            strip = jnp.concatenate(strip, axis=0).astype(jnp.bfloat16)
            along_x = jnp.dot(strip, hx_ref[...], preferred_element_type=jnp.float32)
            parts = [along_x[p * STRIP : (p + 1) * STRIP, :] for p in range(len(plan))]
            current = [parts[0] * (fixed * ROOT**LEVELS)]
            taken = 1
            for level in range(LEVELS):
                reach = 2 ** (LEVELS - level)
                held = max(1, y_share // reach)
                scale = fixed * ROOT ** (LEVELS - level)
                details = parts[taken : taken + held]
                taken += held
                if y_share >= reach:
                    scaled = [d * scale for d in details]
                    current = [e for c, d in zip(current, scaled) for e in (c + d, c - d)]
                else:
                    current = [current[0] + details[0] * jnp.where(lax.rem(me * y_share, reach) < reach // 2, scale, -scale)]
            for y in range(y_share):
                along_y[y, begin : begin + STRIP, :] = current[y].astype(jnp.bfloat16)
        for j in range(2):
            deep = slice(j * depths, (j + 1) * depths)
            for y in range(y_share):
                ready[v, deep, y * NX : (y + 1) * NX] = jnp.dot(
                    hz_ref[deep, :], along_y[y], preferred_element_type=jnp.float32
                )
            send_out(v, j).start()
        return carry

    lax.fori_loop(0, vectors, finish, 0)
    for v in range(vectors):
        for j in range(2):
            send_out(v, j).wait()


def receive(plan, vectors, slots, y_share, table, values, all_spots):
    sources, chunks, _ = all_spots.shape
    rows = chunks * LANES // GROUP
    hx = jnp.asarray(haar(NX), jnp.bfloat16)
    hz = jnp.asarray(haar(NZ).T, jnp.bfloat16)
    lead = len(plan) * vectors
    most = sources * (rows + NZ // BUCKET)
    most_tiles = most // LANES + NZ // BUCKET + 3 * PAIR

    vmem, hbm = pl.BlockSpec(memory_space=pltpu.VMEM), pl.BlockSpec(memory_space=pl.ANY)
    return pl.pallas_call(
        functools.partial(model_kernel, plan, vectors, slots),
        out_shape=jax.ShapeDtypeStruct((vectors, NZ, y_share * NX), jnp.float32),
        in_specs=[hbm] + [vmem] * (3 + len(values)),
        out_specs=hbm,
        scratch_shapes=[
            pltpu.SMEM(table.shape, jnp.int32),
            pltpu.SemaphoreType.DMA,
            pltpu.SMEM((most_tiles,), jnp.int32),
            pltpu.VMEM((sources * rows + WINDOW, LANES), jnp.float32),
            pltpu.VMEM((most_tiles * LANES, LANES), jnp.float32),
            pltpu.VMEM((PAIR, lead * BUCKET, GROUP * LANES), jnp.bfloat16),
            pltpu.VMEM((PAIR, NX, GROUP * LANES), jnp.bfloat16),
            pltpu.VMEM((lead, NZ, NX), jnp.float32),
            pltpu.VMEM((y_share, NZ, NX), jnp.bfloat16),
            pltpu.VMEM((vectors, NZ, y_share * NX), jnp.float32),
            pltpu.SemaphoreType.DMA((vectors, 2)),
        ],
        compiler_params=pltpu.CompilerParams(vmem_limit_bytes=60 * 2**20),
    )(table, all_spots, hx, hz, *values)


def on_device(readings, sensitivity, kept_tile, kept_row, kept_slab, kept_block):
    devices = lax.axis_size(AXES)
    columns = lax.axis_size("col")
    kept, width, _ = sensitivity.shape
    vectors = readings.shape[1]
    per_y = NY // width
    layers = NZ // devices
    y_share = NY // devices
    plan, slots = y_plan(y_share, width)
    chunks = kept // LANES
    spread = jnp.asarray(spread_matrix(plan, slots, devices, vectors, width, y_share), jnp.bfloat16)
    used = columns * readings.shape[0] * (readings.shape[2] // width)
    parts, _, _, beside = fold(vectors, slots)
    values = jax.ShapeDtypeStruct((devices, 16, beside * (chunks // GROUP) * LANES), jnp.bfloat16)
    spots = jax.ShapeDtypeStruct((devices, chunks, LANES), jnp.int32)
    index = jax.ShapeDtypeStruct((2 * devices + 8, LANES), jnp.int32)
    hbm = pl.BlockSpec(memory_space=pl.ANY)

    vmem = pl.BlockSpec(memory_space=pltpu.VMEM)
    *values, all_spots, table = pl.pallas_call(
        functools.partial(front_kernel, layers * NX * per_y, slots),
        out_shape=(*[values] * parts, spots, index),
        in_specs=[vmem] * 6 + [hbm],
        out_specs=(*[hbm] * parts, vmem, vmem),
        scratch_shapes=[
            pltpu.VMEM((width, width, kept), jnp.bfloat16),
            pltpu.VMEM((columns, *readings.shape), readings.dtype),
            pltpu.VMEM((2, chunks, LANES), jnp.int32),
            pltpu.VMEM((2, chunks, LANES), jnp.int32),
            pltpu.VMEM(spots.shape, jnp.int32),
            pltpu.VMEM((vectors * width, -(-used // LANES) * LANES), jnp.bfloat16),
            pltpu.VMEM((vectors // parts * width, LANES), jnp.float32),
            pltpu.VMEM((vectors // parts * width, kept), jnp.bfloat16),
            pltpu.VMEM((2, kept, kept), jnp.bfloat16),
            pltpu.VMEM((parts, *values.shape), jnp.bfloat16),
            pltpu.SemaphoreType.DMA((2,)),
            pltpu.SemaphoreType.DMA((2,)),
            pltpu.SemaphoreType.DMA((parts, 2)),
            pltpu.SemaphoreType.DMA((parts,)),
            pltpu.SemaphoreType.DMA((chunks,)),
        ],
        compiler_params=pltpu.CompilerParams(collective_id=0, has_side_effects=True, vmem_limit_bytes=60 * 2**20),
    )(
        readings, kept_slab.reshape(chunks, LANES), kept_block.reshape(chunks, LANES), kept_tile[None, :],
        kept_row[None, :], spread, sensitivity.transpose(1, 2, 0),
    )
    return receive(plan, vectors, slots, y_share, table, values, all_spots)


def solution(mesh):
    return jax.shard_map(
        on_device,
        mesh=mesh,
        in_specs=(
            P(AXES, None, None),
            P(AXES, None, None),
            P(AXES),
            P(AXES),
            P(AXES, None),
            P(AXES),
        ),
        out_specs=P(None, None, AXES),
        check_vma=False,
    )
```

```python
import functools

import jax
import jax.numpy as jnp
import numpy as np
from jax import lax
from jax.experimental import pallas as pl
from jax.experimental.pallas import tpu as pltpu
from jax.sharding import PartitionSpec as P

NX = 256
NY = 256
NZ = 256
LEVELS = 3
ROOT = 0.7071067811865476
LANES = 128
BUCKET = 8
MOVES = 32
PAIR = 3
STRIP = 32
GROUP = 4
CAP = 80
WINDOW = 24
STEPS = (239 / 256, 169 / 256, 239 / 512, 169 / 512)
REST = 256 / 239
AXES = ("tile", "col")


def segments(length):
    coarse = length // 2**LEVELS
    found = [(0, coarse, 2**LEVELS)]
    for level in range(LEVELS):
        found.append((coarse * 2**level, coarse * 2**level, 2 ** (LEVELS - level)))
    return found


def haar(length):
    matrix = np.zeros((length, length), np.float32)
    for number, (start, count, reach) in enumerate(segments(length)):
        for i in range(count):
            half = reach // 2 if number else reach
            matrix[start + i, i * reach : i * reach + half] = STEPS[reach.bit_length() - 1]
            matrix[start + i, i * reach + half : (i + 1) * reach] = -STEPS[reach.bit_length() - 1]
    return matrix


def y_plan(y_share, width):
    rows = []
    used = {}
    for start, count, reach in segments(NY):
        group = min(start // width, 2)
        for i in range(max(1, y_share // reach)):
            slot = used.get(group, 0)
            used[group] = slot + 1
            rows.append((start, reach, i, slot, group))
    return rows, max(used.values())


def fold(vectors, slots):
    parts = 2
    height = vectors // parts * slots
    stack = 16 // height
    return parts, height, stack, GROUP // stack


def row_of(k, v, slot, vectors, slots):
    parts, height, stack, beside = fold(vectors, slots)
    share = vectors // parts
    return ((v // share) * beside + k % beside) * 16 + k // beside * height + v % share * slots + slot


def spread_matrix(plan, slots, devices, vectors, width, y_share):
    per_y = NY // width
    parts, height, stack, _ = fold(vectors, slots)
    share = vectors // parts
    matrix = np.zeros((devices, stack, share, slots, stack, per_y, share, width), np.float32)
    for start, reach, i, slot, _ in plan:
        for owner in range(devices):
            y = start + owner * y_share // reach + i
            for v in range(share):
                for k in range(stack):
                    matrix[owner, k, v, slot, k, y // width, v, y % width] = 1.0
    matrix = matrix.reshape(devices, 16, stack, per_y, share * width)
    halves = np.split(matrix, 2)
    return np.stack([h[:, :, :, meets(o, per_y)].reshape(devices * 8, -1) for o, h in enumerate(halves)])


def meets(half, per_y):
    return list(range(per_y // 2)) + [per_y // 2 + half]


def front_kernel(
    lift, slots, readings_ref, slab_ref, block_ref, tiles_ref, rows_ref, spread_ref, sens_ref,
    *refs,
):
    parts, _, stack, beside = fold(readings_ref.shape[1], slots)
    value_refs, (spots_ref, index_ref, sens, group, place, mine, everyone, table, picked, made, moved, outgoing), sems = (
        refs[:parts], refs[parts : parts + 12], refs[parts + 12 :]
    )
    group_sems, spots_sems, value_sems, own_sems, sens_sems = sems
    width = sens_ref.shape[0]
    columns, _, vectors, readings = group.shape
    devices, chunks, lanes = everyone.shape
    share = vectors // parts
    per_y = NY // width
    half, step = pl.program_id(0), pl.program_id(1)
    tile, col = lax.axis_index("tile"), lax.axis_index("col")
    me = tile * columns + col
    MESH = pl.DeviceIdType.MESH

    def other(i):
        number = lax.rem(me + i, devices)
        return number, (number // columns, lax.rem(number, columns))

    def wait_all(ref, count, sems):
        part = ref.at[pl.ds(0, count)]
        copy = pltpu.make_async_remote_copy(
            src_ref=part, dst_ref=part, send_sem=sems.at[0], recv_sem=sems.at[1], device_id=(tile, col), device_id_type=MESH
        )
        copy.wait_send()
        copy.wait_recv()

    def fetch(c):
        column = pl.ds(c * lanes, lanes)
        return pltpu.make_async_copy(sens_ref.at[:, :, column], sens.at[:, :, column], sens_sems.at[c])

    @pl.when((half == 0) & (step == 0))
    def begin():
        barrier = pltpu.get_barrier_semaphore()

        def greet(i, carry):
            pl.semaphore_signal(barrier, inc=1, device_id=other(i)[1], device_id_type=MESH)
            return carry

        lax.fori_loop(1, devices, greet, 0)
        for c in range(chunks):
            fetch(c).start()
        group[col] = readings_ref[...]
        sort_blocks(lift, per_y, slab_ref, block_ref, place, mine)
        everyone[me] = mine[me // (devices // 2)]
        pl.semaphore_wait(barrier, devices - 1)

        def send_readings(i, carry):
            pltpu.make_async_remote_copy(
                src_ref=group.at[col], dst_ref=group.at[col], send_sem=group_sems.at[0], recv_sem=group_sems.at[1],
                device_id=(tile, lax.rem(col + i, columns)), device_id_type=MESH,
            ).start()
            return carry

        lax.fori_loop(1, columns, send_readings, 0)

        def send_spots(i, carry):
            number, where = other(i)
            pltpu.make_async_remote_copy(
                src_ref=mine.at[number // (devices // 2)], dst_ref=everyone.at[me],
                send_sem=spots_sems.at[0], recv_sem=spots_sems.at[1], device_id=where, device_id_type=MESH,
            ).start()
            return carry

        lax.fori_loop(1, devices, send_spots, 0)
        for o in range(2):

            def order(c, carry):
                goal = lax.broadcasted_iota(jnp.int32, (lanes, lanes), 0) + c * lanes
                hits = [jnp.where(place[o, d : d + 1, :] == goal, 1.0, 0.0) for d in range(chunks)]
                rows = pl.ds(pl.multiple_of(c * lanes, lanes), lanes)
                moved[o, rows, :] = jnp.concatenate(hits, axis=1).astype(jnp.bfloat16)
                return carry

            lax.fori_loop(0, chunks, order, 0)
        wait_all(group, columns - 1, group_sems)
        make_table(group, width, table)

    tiles = group.shape[0] * group.shape[1]
    spots = lax.broadcasted_iota(jnp.int32, (table.shape[1], lanes), 0)
    here = pl.ds(pl.multiple_of(step * lanes, lanes), lanes)
    chosen = jnp.where(rows_ref[:, here] * tiles + tiles_ref[:, here] == spots, 1.0, 0.0).astype(jnp.bfloat16)

    @pl.when(half == 0)
    def arrive():
        pltpu.make_async_copy(sens_ref.at[:, :, here], sens.at[:, :, here], sens_sems.at[step]).wait()

    readings_here = table[pl.ds(pl.multiple_of(half * (share * width), share * width), share * width), :]
    picked[...] = jnp.dot(readings_here, chosen, preferred_element_type=jnp.float32)
    sums = [jnp.zeros((width, lanes), jnp.float32) for _ in range(share)]
    for r in range(width):
        block = sens[r, :, here].astype(jnp.float32)
        for v in range(share):
            sums[v] = sums[v] + block * picked[v * width + r : v * width + r + 1, :]
    for v in range(share):
        made[v * width : (v + 1) * width, here] = sums[v].astype(jnp.bfloat16)

    @pl.when(step == chunks - 1)
    def send_half():
        middle = devices // 2
        for o in range(2):
            in_y = mine[o] % per_y
            ordered = lax.dot_general(made[...], moved[o], (((1,), (1,)), ((), ())), preferred_element_type=jnp.float32)
            masked = []
            for up in range(stack):
                picks = [part * GROUP + up * beside + k for part in range(chunks // GROUP) for k in range(beside)]
                values = jnp.concatenate([ordered[:, p * lanes : (p + 1) * lanes] for p in picks], axis=1)
                block = jnp.concatenate([in_y[p : p + 1, :] for p in picks], axis=1)
                masked += [jnp.where(block == b, values, 0.0).astype(jnp.bfloat16) for b in meets(o, per_y)]
            sent = jnp.dot(spread_ref[o], jnp.concatenate(masked, axis=0), preferred_element_type=jnp.float32)
            sent = sent.reshape(middle, *outgoing.shape[2:]).astype(jnp.bfloat16)
            outgoing[half, o * middle : (o + 1) * middle] = sent
        for h, target in enumerate(value_refs):

            @pl.when(half == h)
            def send_values():
                pltpu.make_async_copy(outgoing.at[h, me], target.at[me], own_sems.at[h]).start()

                def send(i, carry):
                    number, where = other(i)
                    pltpu.make_async_remote_copy(
                        src_ref=outgoing.at[h, number], dst_ref=target.at[me],
                        send_sem=value_sems.at[h, 0], recv_sem=value_sems.at[h, 1], device_id=where, device_id_type=MESH,
                    ).start()
                    return carry

                lax.fori_loop(1, devices, send, 0)

    @pl.when((half == parts - 1) & (step == chunks - 1))
    def end():
        wait_all(everyone, devices - 1, spots_sems)
        index_tables(everyone, index_ref)
        spots_ref[...] = everyone[...]
        for h, target in enumerate(value_refs):
            pltpu.make_async_copy(outgoing.at[h, me], target.at[me], own_sems.at[h]).wait()
            wait_all(target, devices - 1, value_sems.at[h])


def sort_blocks(lift, per_y, slab_ref, block_ref, place, mine):
    spot_all = slab_ref[...] * lift + block_ref[...]
    chunks, lanes = spot_all.shape
    kept = chunks * lanes
    number = lax.broadcasted_iota(jnp.int32, (chunks, lanes), 0) * lanes + lax.broadcasted_iota(jnp.int32, (chunks, lanes), 1)
    in_y = spot_all % per_y

    def upright(rows):
        return [jnp.broadcast_to(rows[c : c + 1, :], (lanes, lanes)).T for c in range(chunks)]

    for o in range(2):
        away = in_y == per_y // 2 + 1 - o
        spot = jnp.where(away, 3 * NZ * NX * per_y, spot_all)
        bucket = jnp.minimum(spot // (BUCKET * NX * per_y), NZ // BUCKET)
        key = (bucket * kept + number).astype(jnp.float32)
        spot = spot.astype(jnp.float32)
        key_up, spot_up = upright(key), upright(spot)
        ranks = []
        for c in range(chunks):
            line = key[c : c + 1, :]
            total = jnp.zeros((lanes, lanes), jnp.float32)
            for d in range(chunks):
                total = total + jnp.where(key_up[d] < line, 1.0, 0.0)
            ranks.append(jnp.sum(total, axis=0, keepdims=True))
        rank = jnp.concatenate(ranks, axis=0).astype(jnp.int32)
        wide = GROUP * lanes
        found = (rank // wide) * wide + (rank % GROUP) * lanes + (rank // GROUP) % lanes
        place[o] = found
        place_up = upright(found.astype(jnp.float32))
        goal = number.astype(jnp.float32)
        spots = []
        for c in range(chunks):
            line = goal[c : c + 1, :]
            total = jnp.zeros((lanes, lanes), jnp.float32)
            for d in range(chunks):
                total = total + jnp.where(place_up[d] == line, spot_up[d], 0.0)
            spots.append(jnp.sum(total, axis=0, keepdims=True))
        mine[o] = jnp.concatenate(spots, axis=0).astype(jnp.int32)


def make_table(group, width, table):
    sources, share, vectors, readings = group.shape
    lines = [group[i, j].astype(jnp.float32) for i in range(sources) for j in range(share)]
    by_vector = [jnp.concatenate([line[v : v + 1, :] for line in lines], axis=0) for v in range(vectors)]
    rows = []
    for b in range(readings // width):
        rows.append(jnp.concatenate([a[:, b * width : (b + 1) * width] for a in by_vector], axis=1))
    used = sources * share * (readings // width)
    if used < table.shape[1]:
        rows.append(jnp.zeros((table.shape[1] - used, vectors * width), jnp.float32))
    table[...] = jnp.concatenate(rows, axis=0).T.astype(jnp.bfloat16)


def index_tables(all_ref, table_ref):
    sources, chunks, lanes = all_ref.shape
    lane = lax.broadcasted_iota(jnp.int32, (sources, LANES), 1)
    buckets = NZ // BUCKET

    def below(s, low):
        less = jnp.where(all_ref[...] < s * (BUCKET * NX * (NY // 64)), 1.0, 0.0)
        return jnp.where(lane == s, jnp.sum(jnp.sum(less, axis=1), axis=1, keepdims=True), low)

    low = lax.fori_loop(1, buckets + 1, below, jnp.zeros((sources, LANES), jnp.float32)).astype(jnp.int32)
    high = pltpu.roll(low, LANES - 1, 1)
    first = low // GROUP
    counts = jnp.where(high > low, (high + GROUP - 1) // GROUP - first, 0)
    counts = jnp.where(lane < buckets, counts, 0).astype(jnp.float32)
    row = lax.broadcasted_iota(jnp.int32, (sources, sources), 0)
    before = jnp.where(row > lax.broadcasted_iota(jnp.int32, (sources, sources), 1), 1.0, 0.0)
    ahead = jnp.dot(before.astype(jnp.bfloat16), counts.astype(jnp.bfloat16), preferred_element_type=jnp.float32)
    source = lax.broadcasted_iota(jnp.int32, (sources, LANES), 0)
    total = jnp.broadcast_to(jnp.sum(counts, axis=0, keepdims=True), (8, LANES))
    table_ref[:sources, :] = first + source * (chunks * lanes // GROUP)
    table_ref[sources : 2 * sources, :] = ahead.astype(jnp.int32)
    table_ref[2 * sources :, :] = total.astype(jnp.int32)


def model_kernel(
    plan, vectors, slots, table_ref, spots_ref, hx_ref, hz_ref, *refs
):
    sources, chunks, _ = spots_ref.shape
    kept = chunks * LANES
    height = vectors * slots
    parts, _, _, beside = fold(vectors, slots)
    value_refs, (out_ref, index, index_sem, owner, rows_src, merged, left, right, plane, along_y, ready, out_sems) = refs[:parts], refs[parts:]
    buckets = NZ // BUCKET
    rows = kept // GROUP
    y_share = out_ref.shape[2] // NX
    lead = len(plan) * vectors

    row = lax.broadcasted_iota(jnp.int32, (LANES, LANES), 0)
    eye = jnp.where(row == lax.broadcasted_iota(jnp.int32, (LANES, LANES), 1), 1.0, 0.0).astype(jnp.bfloat16)

    def turned(block):
        return lax.dot_general(eye, block, (((1,), (1,)), ((), ())), preferred_element_type=jnp.float32)

    def scatter():
        fetch = pltpu.make_async_copy(table_ref, index, index_sem)
        fetch.start()
        tail = rows_src.shape[0] - sources * rows
        rows_src[pl.ds(sources * rows, tail), :] = jnp.full((tail, LANES), -1.0, jnp.float32)

        share = NZ // sources

        def unpack(src, carry):
            per_y = NY // 64
            if share % BUCKET == 0:
                cleared = pl.ds(pl.multiple_of(src * share, BUCKET), share)
                plane[:, cleared, :] = jnp.zeros((lead, share, NX), jnp.float32)
            spots = spots_ref[src]
            marks = [(spots // per_y) % NX, spots // (NX * per_y), jnp.minimum(spots % per_y, 2)]
            marks = [m.astype(jnp.float32) for m in marks]
            for half in range(rows // LANES):
                tiles = [slice((half * beside + k) * LANES, (half * beside + k + 1) * LANES) for k in range(beside)]
                block = [ref[src, :, lanes] for ref in value_refs for lanes in tiles]
                used = GROUP * height + len(marks) * GROUP
                lines = [m[half * GROUP : (half + 1) * GROUP, :] for m in marks]
                lines.append(jnp.zeros((LANES - used, LANES), jnp.float32))
                block.append(jnp.concatenate(lines, axis=0).astype(jnp.bfloat16))
                place = pl.ds(pl.multiple_of(src * rows + half * LANES, LANES), LANES)
                rows_src[place, :] = turned(jnp.concatenate(block, axis=0))
            return carry

        lax.fori_loop(0, sources, unpack, 0, unroll=4)
        fetch.wait()
        layer = lax.broadcasted_iota(jnp.int32, (BUCKET, LANES), 0).astype(jnp.float32)
        spot = lax.broadcasted_iota(jnp.int32, (NX, LANES), 0).astype(jnp.float32).astype(jnp.bfloat16)
        one, zero = jnp.bfloat16(1.0), jnp.bfloat16(0.0)

        def bucket_step(s, base):
            def merge(i, carry):
                for u in range(MOVES):
                    src = i * MOVES + u
                    to = pl.ds(base * LANES + index[sources + src, s], WINDOW)
                    merged[to, :] = rows_src[pl.ds(index[src, s], WINDOW), :]
                return carry

            lax.fori_loop(0, sources // MOVES, merge, 0)
            count = index[2 * sources, s]
            merged[pl.ds(base * LANES + count, LANES), :] = jnp.full((LANES, LANES), -1.0, jnp.float32)
            tiles = (count + LANES - 1) // LANES

            def name(t, carry):
                owner[base + t] = s
                return carry

            lax.fori_loop(0, tiles, name, 0)
            return base + tiles

        tiles = lax.fori_loop(0, buckets, bucket_step, 0)
        for extra in range(PAIR):
            owner[tiles + extra] = 0
            place = pl.ds(pl.multiple_of((tiles + extra) * LANES, LANES), LANES)
            merged[place, :] = jnp.full((LANES, LANES), -1.0, jnp.float32)
        steps = (tiles + PAIR - 1) // PAIR

        def turn(first):
            block = [merged[pl.ds(first + u * LANES, LANES), :].T for u in range(PAIR)]
            for u in range(PAIR):
                merged[pl.ds(first + u * LANES, LANES), :] = block[u]

        turn(0)
        if share % BUCKET:
            plane[...] = jnp.zeros_like(plane)
        left[...] = jnp.zeros_like(left)
        right[...] = jnp.zeros_like(right)

        def build(u, t, first):
            here = layer + (owner[t] * BUCKET).astype(jnp.float32)
            for k in range(GROUP):
                columns = slice(k * LANES, (k + 1) * LANES)

                def line(row):
                    return merged[pl.ds(first + row, 1), :]

                x = line(GROUP * height + k)
                code = line(GROUP * height + GROUP + k) + NZ * line(GROUP * height + 2 * GROUP + k)
                marks = [jnp.where(code == here + g * NZ, 1.0, 0.0) for g in range(3)]
                marks = [jnp.concatenate([m, m], axis=0).astype(jnp.bfloat16) for m in marks]
                lines = {}
                for v in range(0, vectors, 2):
                    for slot in range(slots):
                        pair = [line(row_of(k, i, slot, vectors, slots)) for i in (v, v + 1)]
                        pair = [jnp.broadcast_to(row, (BUCKET, LANES)) for row in pair]
                        lines[v, slot] = jnp.concatenate(pair, axis=0).astype(jnp.bfloat16)
                pieces = []
                for _, _, _, slot, group in plan:
                    pieces += [lines[v, slot] * marks[group] for v in range(0, vectors, 2)]
                left[u, :, columns] = jnp.concatenate(pieces, axis=0)
                right[u, :, columns] = jnp.where(x.astype(jnp.bfloat16) == spot, one, zero)

        def tile_step(i, carry):
            first = pl.multiple_of(i * PAIR * LANES, LANES)
            turn(first + PAIR * LANES)
            products = []
            for u in range(PAIR):
                product = lax.dot_general(left[u], right[u], (((1,), (1,)), ((), ())), preferred_element_type=jnp.float32)
                products.append(product.reshape(lead, BUCKET, NX))
            for u in range(PAIR):
                build(u, i * PAIR + u, first + u * LANES)
            for u in range(PAIR):
                s = owner[jnp.maximum((i - 1) * PAIR + u, 0)]
                place = pl.ds(pl.multiple_of(s * BUCKET, BUCKET), BUCKET)
                plane[:, place, :] += products[u]
            return carry

        lax.fori_loop(0, steps + 1, tile_step, 0)

    me = lax.axis_index("tile") * lax.axis_size("col") + lax.axis_index("col")
    scatter()
    fixed = REST * REST
    depths = NZ // 2

    def send_out(v, j):
        deep = pl.ds(j * depths, depths)
        return pltpu.make_async_copy(ready.at[v, deep, :], out_ref.at[v, deep, :], out_sems.at[v, j])

    def finish(v, carry):
        for begin in range(0, NZ, STRIP):
            strip = [plane[p * vectors + v, begin : begin + STRIP, :] for p in range(len(plan))]
            strip = jnp.concatenate(strip, axis=0).astype(jnp.bfloat16)
            along_x = jnp.dot(strip, hx_ref[...], preferred_element_type=jnp.float32)
            parts = [along_x[p * STRIP : (p + 1) * STRIP, :] for p in range(len(plan))]
            current = [parts[0] * (fixed * ROOT**LEVELS)]
            taken = 1
            for level in range(LEVELS):
                reach = 2 ** (LEVELS - level)
                held = max(1, y_share // reach)
                scale = fixed * ROOT ** (LEVELS - level)
                details = parts[taken : taken + held]
                taken += held
                if y_share >= reach:
                    scaled = [d * scale for d in details]
                    current = [e for c, d in zip(current, scaled) for e in (c + d, c - d)]
                else:
                    current = [current[0] + details[0] * jnp.where(lax.rem(me * y_share, reach) < reach // 2, scale, -scale)]
            for y in range(y_share):
                along_y[y, begin : begin + STRIP, :] = current[y].astype(jnp.bfloat16)
        for j in range(2):
            deep = slice(j * depths, (j + 1) * depths)
            for y in range(y_share):
                ready[v, deep, y * NX : (y + 1) * NX] = jnp.dot(
                    hz_ref[deep, :], along_y[y], preferred_element_type=jnp.float32
                )
            send_out(v, j).start()
        return carry

    lax.fori_loop(0, vectors, finish, 0)
    for v in range(vectors):
        for j in range(2):
            send_out(v, j).wait()


def receive(plan, vectors, slots, y_share, table, values, all_spots):
    sources, chunks, _ = all_spots.shape
    rows = chunks * LANES // GROUP
    hx = jnp.asarray(haar(NX), jnp.bfloat16)
    hz = jnp.asarray(haar(NZ).T, jnp.bfloat16)
    lead = len(plan) * vectors
    most = sources * (rows + NZ // BUCKET)
    most_tiles = most // LANES + NZ // BUCKET + 3 * PAIR

    vmem, hbm = pl.BlockSpec(memory_space=pltpu.VMEM), pl.BlockSpec(memory_space=pl.ANY)
    return pl.pallas_call(
        functools.partial(model_kernel, plan, vectors, slots),
        out_shape=jax.ShapeDtypeStruct((vectors, NZ, y_share * NX), jnp.float32),
        in_specs=[hbm] + [vmem] * (3 + len(values)),
        out_specs=hbm,
        scratch_shapes=[
            pltpu.SMEM(table.shape, jnp.int32),
            pltpu.SemaphoreType.DMA,
            pltpu.SMEM((most_tiles,), jnp.int32),
            pltpu.VMEM((sources * rows + WINDOW, LANES), jnp.float32),
            pltpu.VMEM((most_tiles * LANES, LANES), jnp.float32),
            pltpu.VMEM((PAIR, lead * BUCKET, GROUP * LANES), jnp.bfloat16),
            pltpu.VMEM((PAIR, NX, GROUP * LANES), jnp.bfloat16),
            pltpu.VMEM((lead, NZ, NX), jnp.float32),
            pltpu.VMEM((y_share, NZ, NX), jnp.bfloat16),
            pltpu.VMEM((vectors, NZ, y_share * NX), jnp.float32),
            pltpu.SemaphoreType.DMA((vectors, 2)),
        ],
        compiler_params=pltpu.CompilerParams(vmem_limit_bytes=60 * 2**20),
    )(table, all_spots, hx, hz, *values)


def on_device(readings, sensitivity, kept_tile, kept_row, kept_slab, kept_block):
    devices = lax.axis_size(AXES)
    columns = lax.axis_size("col")
    kept, width, _ = sensitivity.shape
    vectors = readings.shape[1]
    per_y = NY // width
    layers = NZ // devices
    y_share = NY // devices
    plan, slots = y_plan(y_share, width)
    chunks = kept // LANES
    spread = jnp.asarray(spread_matrix(plan, slots, devices, vectors, width, y_share), jnp.bfloat16)
    used = columns * readings.shape[0] * (readings.shape[2] // width)
    parts, _, _, beside = fold(vectors, slots)
    values = jax.ShapeDtypeStruct((devices, 16, beside * (chunks // GROUP) * LANES), jnp.bfloat16)
    spots = jax.ShapeDtypeStruct((devices, chunks, LANES), jnp.int32)
    index = jax.ShapeDtypeStruct((2 * devices + 8, LANES), jnp.int32)
    hbm = pl.BlockSpec(memory_space=pl.ANY)

    def whole(array):
        return pl.BlockSpec(array.shape, lambda h, i: (0,) * len(array.shape))

    square = jax.ShapeDtypeStruct((chunks, LANES), jnp.int32)
    *values, all_spots, table = pl.pallas_call(
        functools.partial(front_kernel, layers * NX * per_y, slots),
        out_shape=(*[values] * parts, spots, index),
        grid=(parts, chunks),
        in_specs=[
            whole(readings),
            whole(square),
            whole(square),
            pl.BlockSpec((1, kept), lambda h, i: (0, 0)),
            pl.BlockSpec((1, kept), lambda h, i: (0, 0)),
            whole(spread),
            hbm,
        ],
        out_specs=(*[hbm] * parts, whole(spots), whole(index)),
        scratch_shapes=[
            pltpu.VMEM((width, width, kept), jnp.bfloat16),
            pltpu.VMEM((columns, *readings.shape), readings.dtype),
            pltpu.VMEM((2, chunks, LANES), jnp.int32),
            pltpu.VMEM((2, chunks, LANES), jnp.int32),
            pltpu.VMEM(spots.shape, jnp.int32),
            pltpu.VMEM((vectors * width, -(-used // LANES) * LANES), jnp.bfloat16),
            pltpu.VMEM((vectors // parts * width, LANES), jnp.float32),
            pltpu.VMEM((vectors // parts * width, kept), jnp.bfloat16),
            pltpu.VMEM((2, kept, kept), jnp.bfloat16),
            pltpu.VMEM((parts, *values.shape), jnp.bfloat16),
            pltpu.SemaphoreType.DMA((2,)),
            pltpu.SemaphoreType.DMA((2,)),
            pltpu.SemaphoreType.DMA((parts, 2)),
            pltpu.SemaphoreType.DMA((parts,)),
            pltpu.SemaphoreType.DMA((chunks,)),
        ],
        compiler_params=pltpu.CompilerParams(collective_id=0, has_side_effects=True, vmem_limit_bytes=60 * 2**20),
    )(
        readings, kept_slab.reshape(chunks, LANES), kept_block.reshape(chunks, LANES), kept_tile[None, :],
        kept_row[None, :], spread, sensitivity.transpose(1, 2, 0),
    )
    return receive(plan, vectors, slots, y_share, table, values, all_spots)


def solution(mesh):
    return jax.shard_map(
        on_device,
        mesh=mesh,
        in_specs=(
            P(AXES, None, None),
            P(AXES, None, None),
            P(AXES),
            P(AXES),
            P(AXES, None),
            P(AXES),
        ),
        out_specs=P(None, None, AXES),
        check_vma=False,
    )
```
